32 devices in a mesh: parts: 2 (over y), patch: 4 (over z), level: 2 (over x), sub: 2 (over core).
Axes of the slice: x: 2, y: 2, z: 4, core: 2. Of those that a mesh axis runs over, the one named last changes fastest.
Arguments:
- adjoint_height: float32 [4, 1024, 1024], P(('parts', 'level'), ('patch', 'sub')), parts along dimension 0, may hold values from -6 to 6
- adjoint_momenta: float32 [2, 4, 1024, 1024], P(None, ('parts', 'level'), ('patch', 'sub')), parts along dimension 1, may hold values from -6 to 6
- depth: float32 [2, 1024, 1024], P('level', ('patch', 'sub')), may hold values from 0.2 to 1
- wet_mask: int32 [2, 1024, 1024], P('level', ('patch', 'sub')), may hold values 0 or 1
- adjacency: int32 [2, 4, 4], P('level'), may hold values from -1 to 3, as said below
- nest_gain: float32 [2, 8192], P(None, ('patch', 'sub')), may hold values from 0.75 to 1
- nest_index: int32 [2, 8192], P(None, ('patch', 'sub')), may hold values from 0 to 1023, as said below
Outputs:
- height_out: float32 [4, 1024, 1024], P(('parts', 'level'), ('patch', 'sub')), parts along dimension 0
- momenta_out: float32 [2, 4, 1024, 1024], P(None, ('parts', 'level'), ('patch', 'sub')), parts along dimension 1
The draws below stay inside these ranges and needn't reach their ends.
There are 2 independent parts, one for each index of `parts`. The reference program is written for one: setup_inputs(seed, part) draws one part's arguments, and reference() takes and returns one part's arrays. A program takes and returns all parts, laid end to end along the dimension named above; an argument that names none is the same for every part. Nothing has to cross between parts.
Inputs may be any that keep to these rules, and one draw needn't show every extreme that they name: `adjacency`: the patches of a level sit on a grid of cells in an order drawn from the seed; each row of a patch lists its grid neighbours, -1 at the grid's edge, and neighbour links are symmetric. `nest_index`: entries index a cell of the same half patch's strip, 1024 cells long.
All inputs are finite; a program needn't handle non-finite values. No bound on the sum of `wet_mask` on one device may be relied on, other than what follows from the above.
Results may differ from the reference program's by a relative error of at most 0.00002.
Values sent between devices are 32-bit elements; how exact they have to be, the bound alone decides.
A program may use at most 64 MiB of HBM per device.

```python
import math
import jax
import jax.numpy as jnp

BR = 128
COLS = 1024
STEPS = 2
LEVELS = 2
PATCHES = 4
ROWS = 256
TOTAL_ROWS = 1024
SEGS = 8


def level_links(key):
    gcols = 1 << (PATCHES.bit_length() - 1) // 2
    grows = PATCHES // gcols
    order = jax.random.permutation(key, PATCHES).astype(jnp.int32)
    places = jnp.arange(PATCHES, dtype=jnp.int32)
    row_of = places // gcols
    col_of = places % gcols
    none = jnp.full((PATCHES,), -1, jnp.int32)
    north_place = jnp.where(row_of > 0, places - gcols, none)
    south_place = jnp.where(row_of < grows - 1, places + gcols, none)
    west_place = jnp.where(col_of > 0, places - 1, none)
    east_place = jnp.where(col_of < gcols - 1, places + 1, none)
    stacked = jnp.stack([north_place, south_place, west_place, east_place], axis=1)
    named = jnp.where(stacked >= 0, order[jnp.clip(stacked, 0, PATCHES - 1)], -1)
    return jnp.zeros((PATCHES, 4), jnp.int32).at[order].set(named)


def draw_adjacency(key, part):
    keys = jax.random.split(jax.random.fold_in(key, 11), LEVELS)
    return jax.vmap(level_links)(keys)


def draw_nest_index(key, part):
    first, second = jax.random.split(jax.random.fold_in(key, 23))
    offsets = jax.random.randint(first, (LEVELS, SEGS, 1), 0, COLS)
    jitter = jax.random.randint(second, (LEVELS, SEGS, COLS), 0, 3)
    cells = jnp.arange(COLS, dtype=jnp.int32)[None, None, :]
    table = (3 * cells + offsets + jitter) % COLS
    return table.reshape(LEVELS, SEGS * COLS).astype(jnp.int32)


def set_ends(result, rng, low, largest):
    place = [jax.random.randint(jax.random.fold_in(rng, axis), (), 0, length) for axis, length in enumerate(result.shape)]
    longest = result.shape.index(max(result.shape))
    beside = place[:longest] + [(place[longest] + 1) % result.shape[longest]] + place[longest + 1:]
    return result.at[tuple(place)].set(low).at[tuple(beside)].set(largest)


def block_levels(rng, shape, shards, least, high):
    loudness = 1.0
    for dim, shards_of in shards:
        heights = jax.random.uniform(jax.random.fold_in(jax.random.fold_in(rng, 6), dim), (shards_of,), jnp.float32, least / len(shards), high / len(shards))
        loudness = loudness * jnp.repeat(jnp.exp(heights), shape[dim] // shards_of).reshape((-1,) + (1,) * (len(shape) - 1 - dim))
    return loudness


def centred(rng, extent, spread, most, cuts=(), kind=jnp.bfloat16):
    factor_of = block_levels(rng, extent, cuts, -0.22, 0.18) if cuts else 1.0
    entries = jax.random.normal(rng, extent, jnp.float32) * spread * factor_of
    return jnp.minimum(jnp.maximum(entries, -most), most).astype(kind)


def setup_inputs(seed: int = 0, part: int = 0) -> dict:
    arg_keys = jax.random.split(jax.random.key(seed), 8)
    part_splits = jax.random.split(jax.random.fold_in(arg_keys[7], part), 8)
    return {
        "adjoint_height": centred(part_splits[0], (LEVELS, TOTAL_ROWS, COLS), 1.0, 6.0, ((0, 2), (1, 8)), jnp.float32),
        "adjoint_momenta": centred(part_splits[1], (2, LEVELS, TOTAL_ROWS, COLS), 1.0, 6.0, ((1, 2), (2, 8)), jnp.float32),
        "depth": jnp.clip(0.2 + 0.8 * jax.random.uniform(arg_keys[2], (LEVELS, TOTAL_ROWS, COLS), jnp.float32) ** block_levels(arg_keys[2], (LEVELS, TOTAL_ROWS, COLS), ((0, 2), (1, 8)), -0.2, 0.2), 0.2, 1.0),
        "wet_mask": set_ends((jax.random.randint(arg_keys[3], (LEVELS, TOTAL_ROWS, COLS), 0, 4) < 3).astype(jnp.int32), jax.random.fold_in(arg_keys[3], 1), 0, 1),
        "adjacency": draw_adjacency(jax.random.fold_in(arg_keys[7], 71), part),
        "nest_gain": jnp.clip(jnp.exp(math.log(1.0) - 0.2876821 * jax.random.uniform(arg_keys[5], (LEVELS, SEGS * COLS), jnp.float32) ** block_levels(arg_keys[5], (LEVELS, SEGS * COLS), ((1, 8),), -0.2, 0.2)), 0.75, 1.0),
        "nest_index": draw_nest_index(jax.random.fold_in(arg_keys[7], 71), part),
    }


courant = 0.45


def neighbour(field, links, level_ids):
    picked = field[level_ids, jnp.clip(links, 0, PATCHES - 1)]
    return picked * (links >= 0).astype(jnp.float32)[:, :, None, None]


def reference(adjoint_height, adjoint_momenta, depth, wet_mask, adjacency, nest_gain, nest_index):
    shape4 = (LEVELS, PATCHES, ROWS, COLS)
    eta = adjoint_height.reshape(shape4)
    mom_row = adjoint_momenta[0].reshape(shape4)
    mom_col = adjoint_momenta[1].reshape(shape4)
    height = depth.reshape(shape4)
    wet = wet_mask.astype(jnp.float32).reshape(shape4)
    north = adjacency[:, :, 0]
    south = adjacency[:, :, 1]
    west = adjacency[:, :, 2]
    east = adjacency[:, :, 3]
    level_ids = jnp.arange(LEVELS)[:, None]
    gains = nest_gain.reshape(LEVELS, SEGS, COLS)
    tables = nest_index.reshape(LEVELS, SEGS, COLS)
    for step in range(STEPS):
        halves = eta.reshape(LEVELS, SEGS, BR, COLS)
        strips = halves[:, :, 0, :]
        flux = jnp.zeros((SEGS, COLS), jnp.float32)
        inflows = []
        for lev in range(LEVELS - 1, -1, -1):
            inflow = gains[lev] * jnp.take_along_axis(flux, tables[lev], axis=1)
            flux = inflow + strips[lev]
            inflows.insert(0, inflow)
        halves = halves.at[:, :, 0, :].add(jnp.stack(inflows))
        eta = halves.reshape(shape4)
        east_eta = jnp.concatenate([eta[..., 1:], neighbour(eta, east, level_ids)[..., :1]], axis=3)
        south_eta = jnp.concatenate([eta[:, :, 1:, :], neighbour(eta, south, level_ids)[:, :, :1, :]], axis=2)
        mom_row = wet * (mom_row - courant * (east_eta - eta))
        mom_col = wet * (mom_col - courant * (south_eta - eta))
        west_row = jnp.concatenate([neighbour(mom_row, west, level_ids)[..., -1:], mom_row[..., :-1]], axis=3)
        north_col = jnp.concatenate([neighbour(mom_col, north, level_ids)[:, :, -1:, :], mom_col[:, :, :-1, :]], axis=2)
        eta = wet * (eta - courant * height * ((mom_row - west_row) + (mom_col - north_col)))
    flat = (LEVELS, TOTAL_ROWS, COLS)
    return eta.reshape(flat), jnp.stack([mom_row.reshape(flat), mom_col.reshape(flat)])
```

```python
import functools

import jax
import jax.numpy as jnp
from jax import lax
from jax.experimental import pallas as pl
from jax.experimental.pallas import tpu as pltpu
from jax.sharding import PartitionSpec as P

STEPS = 2
COURANT = 0.45
LANES = 128
BLOCK = 8


def advance(r, E, Pm, Q, H, W, halo, E_to, P_to, Q_to):
    cols = Pm.shape[1]
    lane_ids = lax.broadcasted_iota(jnp.int32, (BLOCK, cols), 1)
    span = slice(r, r + BLOCK)
    e = E[span, :]
    wet = W[span, :].astype(jnp.float32)
    e_south = E[r + 1:r + 1 + BLOCK, :]
    e_east = pltpu.roll(e, cols - 1, 1)
    if halo is not None:
        e_east = jnp.where(lane_ids == cols - 1, halo[span, 0:1], e_east)
    p = wet * (Pm[span, :] - COURANT * (e_east - e))
    q = wet * (Q[8 + r:16 + r, :] - COURANT * (e_south - e))
    p_west = pltpu.roll(p, 1, 1)
    if halo is not None:
        p_edge = halo[span, 1:2] - COURANT * halo[span, 2:3] * e[:, 0:1]
        p_west = jnp.where(lane_ids == 0, p_edge, p_west)
    P_to[span, :] = p
    Q_to[8 + r:16 + r, :] = q
    q_north = Q_to[7 + r:15 + r, :]
    E_to[span, :] = wet * (e - COURANT * H[span, :] * ((p - p_west) + (q - q_north)))


def finish(rows, E, Pm, Q, H, W, halo, E2, P2, Q2, eta_out, mom_out, Ef, Pf, Qf, sems):
    cols = Pm.shape[1]
    end = rows - BLOCK
    mid = slice(BLOCK, end)
    head, tail = slice(0, LANES), slice(cols - LANES, cols)
    before, inner = slice(0, cols - LANES), slice(LANES, cols - LANES)
    stores = []

    def store(src, dst):
        copy = pltpu.make_async_copy(src, dst, sems.at[len(stores)])
        copy.start()
        stores.append(copy)

    eta_to, row_to, col_to = eta_out.at[0], mom_out.at[0, 0], mom_out.at[1, 0]
    store(Q2.at[BLOCK + 8:end + 8], col_to.at[mid])
    store(P2.at[mid, before], row_to.at[mid, before])
    store(E2.at[mid, inner], eta_to.at[mid, inner])
    edges = halo[...]
    lane_ids = lax.broadcasted_iota(jnp.int32, (end - BLOCK, LANES), 1)

    across = Q2[BLOCK + 8:end + 8, head] - Q2[BLOCK + 7:end + 7, head]
    e = E[mid, head]
    wet = W[mid, head].astype(jnp.float32)
    p_edge = edges[mid, 1:2] - COURANT * edges[mid, 2:3] * e[:, 0:1]
    fixed = wet * (e - COURANT * H[mid, head] * ((P2[mid, head] - p_edge) + across))
    Ef[mid, head] = jnp.where(lane_ids == 0, fixed, E2[mid, head])
    store(Ef.at[mid, head], eta_to.at[mid, head])

    across = Q2[BLOCK + 8:end + 8, tail] - Q2[BLOCK + 7:end + 7, tail]
    e = E[mid, tail]
    wet = W[mid, tail].astype(jnp.float32)
    p = wet * (Pm[mid, tail] - COURANT * (edges[mid, 0:1] - e))
    p = jnp.where(lane_ids == LANES - 1, p, P2[mid, tail])
    Pf[mid, tail] = p
    store(Pf.at[mid, tail], row_to.at[mid, tail])
    fixed = wet * (e - COURANT * H[mid, tail] * ((p - pltpu.roll(p, 1, 1)) + across))
    Ef[mid, tail] = jnp.where(lane_ids == LANES - 1, fixed, E2[mid, tail])
    store(Ef.at[mid, tail], eta_to.at[mid, tail])

    for r in (0, end):
        Qf[7 + r:8 + r, :] = (Q if r == 0 else Q2)[7 + r:8 + r, :]
        advance(r, E, Pm, Q, H, W, edges, Ef, Pf, Qf)
        at = slice(r, r + BLOCK)
        store(Pf.at[at], row_to.at[at])
        store(Qf.at[8 + r:16 + r], col_to.at[at])
        store(Ef.at[at], eta_to.at[at])
    for copy in stores:
        copy.wait()


def exchange(patches, levels, rows, cols,
             adj_hbm, eta_hbm, mom_hbm, depth_hbm, wet_hbm, gain_hbm, table_hbm,
             E1, P1, Q1, H, W, halo_out, E2, P2, Q2,
             adj, E0, P0, Q0, gain_v, table_v, f8, idx8, gain8, tmp,
             sfirst, slast, scol, sinf, sew,
             rown, in_sems, send_sems, recv_sems, own_sems, *landing):
    rfirst, rlast, rcol, rnbr, rew = (landing[n * STEPS:(n + 1) * STEPS] for n in range(5))
    fields = ((E0, P0, Q0), (E1, P1, Q1))
    patch = lax.axis_index("patch")
    level = lax.axis_index("level")
    half = lax.axis_index("sub")
    chunks = cols // LANES
    other = 1 - half

    loads = [
        pltpu.make_async_copy(eta_hbm.at[0], E0.at[0:rows], in_sems.at[0]),
        pltpu.make_async_copy(mom_hbm.at[0, 0], P0, in_sems.at[1]),
        pltpu.make_async_copy(mom_hbm.at[1, 0], Q0.at[8:8 + rows], in_sems.at[2]),
        pltpu.make_async_copy(wet_hbm.at[0], W, in_sems.at[3]),
        pltpu.make_async_copy(table_hbm, table_v, in_sems.at[4]),
        pltpu.make_async_copy(gain_hbm, gain_v, in_sems.at[5]),
        pltpu.make_async_copy(adj_hbm, adj, in_sems.at[6]),
        pltpu.make_async_copy(depth_hbm.at[0], H, in_sems.at[7]),
    ]
    barrier = pltpu.get_barrier_semaphore()

    peers = [patch] + [lax.rem(patch + d, patches) for d in range(1, patches)]

    def greet(d, h, lev):
        pl.semaphore_signal(barrier, inc=1, device_id={
            "patch": peers[d], "sub": h, "level": lev},
            device_id_type=pl.DeviceIdType.MESH)

    for d in range(patches - 1, -1, -1):
        greet(d, other, level)
        if d:
            greet(d, half, level)

    @pl.when(level > 0)
    def _():
        for d in range(patches):
            greet(d, half, level - 1)
            greet(d, other, level - 1)

    @pl.when(level < levels - 1)
    def _():
        for d in range(patches):
            greet(d, half, level + 1)
            greet(d, other, level + 1)

    for load in loads:
        load.start()

    for load in loads[:7]:
        load.wait()

    lower = jnp.maximum(level - 1, 0)
    for c in range(chunks):
        lane = slice(c * LANES, (c + 1) * LANES)
        index, gain = table_v[0:1, lane], gain_v[0:1, lane]
        for lev in range(1, levels - 1):
            index = jnp.where(lower == lev, table_v[lev:lev + 1, lane], index)
            gain = jnp.where(lower == lev, gain_v[lev:lev + 1, lane], gain)
        idx8[c:c + 1, :] = index
        gain8[c:c + 1, :] = gain

    def remote(t, kind, src, buf, slot, d, h, lev):
        return pltpu.make_async_remote_copy(
            src_ref=src, dst_ref=buf, send_sem=send_sems.at[t, kind, d],
            recv_sem=recv_sems.at[t, kind, slot],
            device_id={"patch": peers[d], "sub": h, "level": lev},
            device_id_type=pl.DeviceIdType.MESH)

    def last_part(t):
        return slice(0, 2) if t == 0 else slice(t + 1, t + 2)

    def column_copy(t, slot, d):
        return remote(t, 0, scol.at[t, 0:3], rcol[t].at[slot, 0:3], slot, d, half, level)

    def first_copy(t, slot, d):
        return remote(t, 1, sfirst.at[t], rfirst[t].at[slot], slot, d, other, level)

    def last_copy(t, slot, d):
        part = last_part(t)
        return remote(t, 2, slast.at[part], rlast[t].at[slot], slot, d, other, level)

    def beside_copy(t, slot, d):
        return remote(t, 3, sinf.at[t], rnbr[t].at[slot], slot, d, other, lower)

    def ends_copy(t, slot, d):
        return remote(t, 4, sew.at[t], rew[t].at[slot], slot, d, half, lower)

    def per_half(across, inside, act):
        @pl.when(half == across)
        def _():
            for d in range(1, patches):
                act(d)

        @pl.when(half == inside)
        def _():
            act(0)

    def own_copy(t):
        return pltpu.make_async_remote_copy(
            src_ref=sinf.at[t], dst_ref=rown.at[t], send_sem=own_sems.at[t, 0],
            recv_sem=own_sems.at[t, 1], device_id={"level": lower},
            device_id_type=pl.DeviceIdType.MESH)

    def make_inflow(t):
        E = fields[t][0]
        for c in range(chunks):
            f8[c:c + 1, :] = E[0:1, c * LANES:(c + 1) * LANES]
        index = idx8[...]
        inside = jnp.bitwise_and(index, LANES - 1)
        which = lax.shift_right_logical(index, 7)
        picked = jnp.zeros((chunks, LANES), jnp.float32)
        for c in range(chunks):
            source = jnp.broadcast_to(f8[c:c + 1, :], (chunks, LANES))
            got = jnp.take_along_axis(source, inside, axis=1, mode="promise_in_bounds")
            picked = jnp.where(which == c, got, picked)
        inflow = gain8[...] * picked
        sinf[t] = inflow
        sew[t, 0:1, :] = inflow[0:1, :]
        sew[t, 1:2, :] = pltpu.roll(inflow[chunks - 1:chunks, :], 1, 1)

    def send_inflow(t):
        own_copy(t).start()
        per_half(0, 1, lambda d: beside_copy(t, patch, d).start())
        for d in range(1, patches):
            ends_copy(t, patch, d).start()

    def inflow_waits(t):
        per_half(1, 0, lambda d: beside_copy(t, peers[d], d).wait_recv())
        for d in range(1, patches):
            ends_copy(t, peers[d], d).wait_recv()

    def inflow_send_waits(t):
        own_copy(t).wait_send()
        per_half(0, 1, lambda d: beside_copy(t, patch, d).wait_send())
        for d in range(1, patches):
            ends_copy(t, patch, d).wait_send()

    def send_halos(t, act):
        send_rows(t, act)
        send_columns(t, act)

    def send_columns(t, act):
        for d in range(1, patches):
            act(column_copy(t, patch, d))

    def send_rows(t, act):
        @pl.when(half == 0)
        def _():
            for d in range(1, patches):
                act(first_copy(t, patch, d))
            act(last_copy(t, patch, 0))

        @pl.when(half == 1)
        def _():
            for d in range(1, patches):
                act(last_copy(t, patch, d))
            act(first_copy(t, patch, 0))

    def receive_halos(t):
        @pl.when(half == 0)
        def _():
            first_copy(t, peers[0], 0).wait_recv()
            for d in range(1, patches):
                last_copy(t, peers[d], d).wait_recv()

        @pl.when(half == 1)
        def _():
            last_copy(t, peers[0], 0).wait_recv()
            for d in range(1, patches):
                first_copy(t, peers[d], d).wait_recv()

        for d in range(1, patches):
            column_copy(t, peers[d], d).wait_recv()

    north = adj[0, patch, 0]
    south = adj[0, patch, 1]
    west = adj[0, patch, 2]
    east = adj[0, patch, 3]
    south_ok = jnp.logical_or(half == 0, south >= 0)
    north_ok = jnp.logical_or(half == 1, north >= 0)
    south_at = jnp.where(half == 0, patch, jnp.maximum(south, 0))
    north_at = jnp.where(half == 1, patch, jnp.maximum(north, 0))
    west_at = jnp.maximum(west, 0)
    east_at = jnp.maximum(east, 0)
    finer = level < levels - 1
    lane_ids = lax.broadcasted_iota(jnp.int32, (rows, LANES), 1)
    first_lane = lax.broadcasted_iota(jnp.int32, (1, LANES), 1) == 0
    tail = slice(cols - LANES, cols)
    end = rows - 1

    def make_messages(t):
        @pl.when(level == levels - 1)
        def _():
            make_inflow(t)

        make_rows(t)
        make_columns(t)

    def make_rows(t):
        E, Pm, Q = fields[t]
        sfirst[t] = E[0:1, :]
        wet_row = W[end:rows, :].astype(jnp.float32)
        slast[t + 1] = wet_row * (Q[8 + end:8 + rows, :] + COURANT * E[end:rows, :])
        if t == 0:
            slast[0] = wet_row

    def make_columns(t):
        E, Pm, Q = fields[t]
        wet_tail = W[:, tail].astype(jnp.float32)
        share = wet_tail * (Pm[:, tail] + COURANT * E[0:rows, tail])
        mixed = jnp.where(lane_ids == 0, E[0:rows, 0:LANES],
                          jnp.where(lane_ids == 1, pltpu.roll(share, 2, 1),
                                    pltpu.roll(wet_tail, 3, 1)))
        scol[t] = jnp.transpose(mixed[:, 0:8])

    def send_messages(t):
        @pl.when(level == levels - 1)
        def _():
            send_inflow(t)

        send_halos(t, lambda copy: copy.start())

    def receive(t):
        E, Pm, Q = fields[t]

        @pl.when(finer)
        def _():
            own_copy(t).wait_recv()
            for c in range(chunks):
                lane = slice(c * LANES, (c + 1) * LANES)
                E[0:1, lane] += rown[t, c:c + 1, :]

        if levels > 2:
            @pl.when(jnp.logical_and(level > 0, level < levels - 1))
            def _():
                make_inflow(t)
                send_inflow(t)

        receive_halos(t)

        @pl.when(finer)
        def _():
            inflow_waits(t)

        east_row = rcol[t][east_at][0:1, :]
        east_row += jnp.where(jnp.logical_and(first_lane, finer), rew[t][east_at][0:1, :], 0.0)
        west_cols = rcol[t][west_at]
        share = west_cols[1:2, :]
        wet_w = west_cols[2:3, :]
        share += jnp.where(jnp.logical_and(first_lane, finer),
                           COURANT * wet_w * rew[t][west_at][1:2, :], 0.0)
        tmp[0:1, :] = jnp.where(east >= 0, east_row, 0.0)
        tmp[1:2, :] = jnp.where(west >= 0, share, 0.0)
        tmp[2:3, :] = jnp.where(west >= 0, wet_w, 0.0)
        beside = rnbr[t][south_at]
        below = rfirst[t][south_at]
        for c in range(chunks):
            lane = slice(c * LANES, (c + 1) * LANES)
            value = below[:, lane] + jnp.where(finer, beside[c:c + 1, :], 0.0)
            E[rows:rows + 1, lane] = jnp.where(south_ok, value, 0.0)
        share_n = rlast[t][north_at, 1 if t == 0 else 0]
        wet_n = rlast[0][north_at, 0]
        Q_to = Q1
        Q_to[7:8, :] = jnp.where(north_ok, share_n - COURANT * wet_n * E[0:1, :], 0.0)
        return jnp.transpose(tmp[...])

    make_messages(0)
    sides = (level > 0).astype(jnp.int32) + (level < levels - 1).astype(jnp.int32)
    pl.semaphore_wait(barrier, 2 * patches - 1 + 2 * patches * sides)
    send_messages(0)
    loads[7].wait()
    for r in range(0, rows - BLOCK, BLOCK):
        advance(r, E0, P0, Q0, H, W, None, E1, P1, Q1)
    halo = receive(0)
    for r in (0, rows - BLOCK):
        advance(r, E0, P0, Q0, H, W, None, E1, P1, Q1)
    head = slice(0, LANES)
    e = E0[0:rows, head]
    wet = W[:, head].astype(jnp.float32)
    p_edge = halo[:, 1:2] - COURANT * halo[:, 2:3] * e[:, 0:1]
    across = Q1[8:8 + rows, head] - Q1[7:7 + rows, head]
    fixed = wet * (e - COURANT * H[:, head] * ((P1[:, head] - p_edge) + across))
    E1[0:rows, head] = jnp.where(lane_ids == 0, fixed, E1[0:rows, head])
    e = E0[0:rows, tail]
    wet = W[:, tail].astype(jnp.float32)
    p = wet * (P0[:, tail] - COURANT * (halo[:, 0:1] - e))
    p = jnp.where(lane_ids == LANES - 1, p, P1[:, tail])
    P1[:, tail] = p
    across = Q1[8:8 + rows, tail] - Q1[7:7 + rows, tail]
    fixed = wet * (e - COURANT * H[:, tail] * ((p - pltpu.roll(p, 1, 1)) + across))
    E1[0:rows, tail] = jnp.where(lane_ids == LANES - 1, fixed, E1[0:rows, tail])

    @pl.when(level == levels - 1)
    def _():
        make_inflow(1)
        send_inflow(1)

    make_rows(1)
    send_rows(1, lambda copy: copy.start())
    make_columns(1)
    send_columns(1, lambda copy: copy.start())
    for r in range(0, rows - BLOCK, BLOCK):
        advance(r, E1, P1, Q1, H, W, None, E2, P2, Q2)
    halo_out[...] = receive(1)
    for t in range(STEPS):
        send_halos(t, lambda copy: copy.wait_send())

        @pl.when(level > 0)
        def _():
            inflow_send_waits(t)


def body(mesh, adjoint_height, adjoint_momenta, depth, wet_mask, adjacency, nest_gain, nest_index):
    patches, levels = mesh.shape["patch"], mesh.shape["level"]
    rows, cols = adjoint_height.shape[1:]
    chunks = cols // LANES
    f32 = jnp.float32
    anywhere = pl.BlockSpec(memory_space=pl.ANY)
    v = pltpu.VMEM
    dma = pltpu.SemaphoreType.DMA
    whole = (v((rows + 8, cols), f32), v((rows, cols), f32), v((rows + 8, cols), f32))
    scratch = [
        pltpu.SMEM(adjacency.shape, jnp.int32),
        *whole,
        v(nest_gain.shape, f32), v(nest_index.shape, jnp.int32),
        v((chunks, LANES), f32), v((chunks, LANES), jnp.int32), v((chunks, LANES), f32),
        v((8, LANES), f32),
        v((STEPS, 1, cols), f32), v((STEPS + 1, 1, cols), f32), v((STEPS, 8, LANES), f32),
        v((STEPS, chunks, LANES), f32), v((STEPS, 2, LANES), f32),
        v((STEPS, chunks, LANES), f32),
        dma((8,)), dma((STEPS, 5, patches)), dma((STEPS, 5, patches)), dma((STEPS, 2)),
    ]
    scratch += [v((patches, 1, cols), f32)] * STEPS
    scratch += [v((patches, 2 if t == 0 else 1, 1, cols), f32) for t in range(STEPS)]
    scratch += [v((patches, 8, LANES), f32)] * STEPS
    scratch += [v((patches, chunks, LANES), f32)] * STEPS
    scratch += [v((patches, 2, LANES), f32)] * STEPS
    here = pl.BlockSpec(memory_space=pltpu.VMEM)
    state = pl.pallas_call(
        functools.partial(exchange, patches, levels, rows, cols),
        out_shape=(*whole, v((rows, cols), f32), v((rows, cols), jnp.int32), v((rows, 8), f32), *whole),
        in_specs=[anywhere] * 7,
        out_specs=(here,) * 9,
        scratch_shapes=scratch,
        compiler_params=pltpu.CompilerParams(collective_id=0, has_side_effects=True,
                                             vmem_limit_bytes=12 << 20),
    )(*[pltpu.with_memory_space_constraint(x, pltpu.HBM) for x in (
        adjacency, adjoint_height, adjoint_momenta, depth, wet_mask, nest_gain, nest_index)])
    state = [pltpu.with_memory_space_constraint(x, pltpu.VMEM) for x in state]
    return pl.pallas_call(
        functools.partial(finish, rows),
        out_shape=(jax.ShapeDtypeStruct(adjoint_height.shape, f32),
                   jax.ShapeDtypeStruct(adjoint_momenta.shape, f32)),
        in_specs=[here] * 9,
        out_specs=(anywhere, anywhere),
        scratch_shapes=[*whole, dma((12,))],
        compiler_params=pltpu.CompilerParams(vmem_limit_bytes=12 << 20),
    )(*state)


FULL, TAIL, ENDS = (8, 72), (8, 26), (24, 26)


def step_rows(r, E, Pm, Q, H, W, edge, E_to, P_to, Q_to):
    cols = Pm.shape[1]
    lane_ids = lax.broadcasted_iota(jnp.int32, (BLOCK, cols), 1)
    span = slice(r, r + BLOCK)
    e = E[span, :]
    wet = W[span, :].astype(jnp.float32)
    e_south = E[r + 1:r + 1 + BLOCK, :]
    e_east = pltpu.roll(e, cols - 1, 1)
    if edge is not None:
        e_east = jnp.where(lane_ids == cols - 1, edge[span, 0:1], e_east)
    p = wet * (Pm[span, :] - COURANT * (e_east - e))
    q = wet * (Q[8 + r:16 + r, :] - COURANT * (e_south - e))
    p_west = pltpu.roll(p, 1, 1)
    if edge is not None:
        p_west = jnp.where(lane_ids == 0, edge[span, 1:2] - edge[span, 2:3] * e[:, 0:1], p_west)
    P_to[span, :] = p
    Q_to[8 + r:16 + r, :] = q
    q_north = Q_to[7 + r:15 + r, :]
    E_to[span, :] = wet * (e - COURANT * H[span, :] * ((p - p_west) + (q - q_north)))


def settle(rows, E, Pm, Q, H, W, halo, E2, P2, Q2, eta_out, mom_out, Ef, Pf, Qf, sems):
    cols = Pm.shape[1]
    end = rows - BLOCK
    mid = slice(BLOCK, end)
    head, tail = slice(0, LANES), slice(cols - LANES, cols)
    inner = slice(LANES, cols - LANES)
    stores = []

    def store(src, dst):
        copy = pltpu.make_async_copy(src, dst, sems.at[len(stores)])
        copy.start()
        stores.append(copy)

    eta_to, row_to, col_to = eta_out.at[0], mom_out.at[0, 0], mom_out.at[1, 0]
    store(Q2.at[BLOCK + 8:end + 8, inner], col_to.at[mid, inner])
    store(P2.at[mid, inner], row_to.at[mid, inner])
    store(E2.at[mid, inner], eta_to.at[mid, inner])
    edge = halo[...]

    def ends(r):
        step_rows(r, E, Pm, Q, H, W, edge, Ef, Pf, Qf)
        at = slice(r, r + BLOCK)
        store(Pf.at[at], row_to.at[at])
        store(Qf.at[8 + r:16 + r], col_to.at[at])
        store(Ef.at[at], eta_to.at[at])

    Qf[7:8, :] = Q2[7:8, :]
    ends(0)
    lane_ids = lax.broadcasted_iota(jnp.int32, (end - BLOCK, LANES), 1)
    for lane in (head, tail):
        e = E[mid, lane]
        wet = W[mid, lane].astype(jnp.float32)
        q = wet * (Q[BLOCK + 8:end + 8, lane] - COURANT * (E[BLOCK + 1:end + 1, lane] - e))
        Qf[BLOCK + 8:end + 8, lane] = q
        across = q - Qf[BLOCK + 7:end + 7, lane]
        e_east = pltpu.roll(e, LANES - 1, 1)
        if lane == tail:
            e_east = jnp.where(lane_ids == LANES - 1, edge[mid, 0:1], e_east)
        p = wet * (Pm[mid, lane] - COURANT * (e_east - e))
        p_west = pltpu.roll(p, 1, 1)
        if lane == head:
            p = jnp.where(lane_ids == LANES - 1, P2[mid, lane], p)
            p_west = jnp.where(lane_ids == 0, edge[mid, 1:2] - edge[mid, 2:3] * e[:, 0:1], p_west)
        eta = wet * (e - COURANT * H[mid, lane] * ((p - p_west) + across))
        if lane == head:
            eta = jnp.where(lane_ids == LANES - 1, E2[mid, lane], eta)
        else:
            eta = jnp.where(lane_ids == 0, E2[mid, lane], eta)
        Pf[mid, lane] = p
        Ef[mid, lane] = eta
        store(Qf.at[BLOCK + 8:end + 8, lane], col_to.at[mid, lane])
        store(Pf.at[mid, lane], row_to.at[mid, lane])
        store(Ef.at[mid, lane], eta_to.at[mid, lane])
    Qf[7 + end:8 + end, inner] = Q2[7 + end:8 + end, inner]
    ends(end)
    for copy in stores:
        copy.wait()


def swap(patches, rows, cols,
         adj_hbm, eta_hbm, mom_hbm, depth_hbm, wet_hbm, gain_hbm, table_hbm,
         E1, P1, Q1, H, W, halo_out, E2, P2, Q2,
         adj, E0, P0, Q0, gain_v, table_v, line, stack, qb, sfirst, slast, scol,
         nsel, flow, corner, tmp, in_sems, send_sems, recv_sems, down_sems,
         rfirst, rlast, rcol, rdown):
    f32 = jnp.float32
    patch = lax.axis_index("patch")
    level = lax.axis_index("level")
    half = lax.axis_index("sub")
    other = 1 - half
    chunks = cols // LANES
    last = cols - 1
    end = rows - BLOCK
    head, tail = slice(0, LANES), slice(cols - LANES, cols)
    inner = slice(LANES, cols - LANES)
    mid = slice(BLOCK, end)
    loads = []

    def load(src, dst):
        copy = pltpu.make_async_copy(src, dst, in_sems.at[len(loads)])
        copy.start()
        loads.append(copy)

    fields = ((eta_hbm.at[0], E0, 0), (mom_hbm.at[0, 0], P0, 0), (mom_hbm.at[1, 0], Q0, 8),
              (wet_hbm.at[0], W, 0), (depth_hbm.at[0], H, 0))

    def load_part(at, lane):
        for src, dst, shift in fields:
            load(src.at[at, lane], dst.at[at.start + shift:at.stop + shift, lane])

    for at in (slice(0, BLOCK), slice(end, rows)):
        load_part(at, slice(0, cols))
    load(adj_hbm, adj)
    load(table_hbm, table_v)
    load(gain_hbm, gain_v)
    n_rows = len(loads)

    barrier = pltpu.get_barrier_semaphore()
    peers = [patch] + [lax.rem(patch + d, patches) for d in range(1, patches)]

    def greet(d, h, lev):
        pl.semaphore_signal(barrier, inc=1, device_id={
            "patch": peers[d], "sub": h, "level": lev},
            device_id_type=pl.DeviceIdType.MESH)

    for d in range(1, patches):
        greet(d, other, level)
        greet(d, half, level)
    greet(0, other, level)

    @pl.when(level == 0)
    def _():
        for d in list(range(1, patches)) + [0]:
            greet(d, half, 1)
            greet(d, other, 1)

    for lane in (head, tail):
        load_part(mid, lane)
    n_tiles = len(loads)
    load_part(mid, inner)

    E0[rows:rows + 8, :] = jnp.zeros((8, cols), f32)
    qb[0:8, :] = jnp.zeros((8, LANES), f32)
    lane_ids = lax.broadcasted_iota(jnp.int32, (chunks, LANES), 1)
    cell_ids = lax.broadcasted_iota(jnp.int32, (chunks, LANES), 0) * LANES + lane_ids
    row_lane = lax.broadcasted_iota(jnp.int32, (1, LANES), 1)

    def east_of(x, beyond):
        y = pltpu.roll(x, LANES - 1, 1)
        y = jnp.where(lane_ids == LANES - 1, pltpu.roll(y, chunks - 1, 0), y)
        return jnp.where(cell_ids == last, beyond, y)

    def west_of(x, beyond):
        y = pltpu.roll(x, 1, 1)
        y = jnp.where(lane_ids == 0, pltpu.roll(y, 1, 0), y)
        return jnp.where(cell_ids == 0, beyond, y)

    def gather(x, index):
        inside = jnp.bitwise_and(index, LANES - 1)
        which = lax.shift_right_logical(index, 7)
        picked = jnp.zeros((chunks, LANES), f32)
        for c in range(chunks):
            source = jnp.broadcast_to(x[c:c + 1, :], (chunks, LANES))
            got = jnp.take_along_axis(source, inside, axis=1, mode="promise_in_bounds")
            picked = jnp.where(which == c, got, picked)
        return picked

    for copy in loads[:n_rows]:
        copy.wait()

    def lines(n, ref, r):
        for c in range(chunks):
            line[n, c:c + 1, :] = ref[r:r + 1, c * LANES:(c + 1) * LANES].astype(f32)

    for n, (ref, r) in enumerate((
            (E0, 0), (E0, 1), (P0, 0), (Q0, 8), (W, 0), (H, 0),
            (E0, rows - 1), (P0, rows - 1), (Q0, rows + 7), (W, rows - 1), (H, rows - 1),
            (E0, rows - 2), (Q0, rows + 6), (W, rows - 2))):
        lines(n, ref, r)

    e, p, q, m = line[0], line[2], line[3], line[4]
    e_first = e
    km = COURANT * m
    khm = km * line[5]
    mp = m * p
    sfirst[0:8, :] = e
    sfirst[8:16, :] = mp - west_of(mp, 0.0) + (m * q - km * line[1])
    sfirst[16:24, :] = khm
    stack[4:5, :] = jnp.where(row_lane < 64, e[0:1, :], e[chunks - 1:chunks, :])
    stack[5:6, :] = jnp.where(row_lane < 64, mp[0:1, :], mp[chunks - 1:chunks, :])
    stack[6:7, :] = jnp.where(row_lane < 64, km[0:1, :], km[chunks - 1:chunks, :])
    el, ml = line[6], line[9]
    kml = COURANT * ml
    khml = kml * line[10]
    pl_new = ml * line[7] - kml * (east_of(el, 0.0) - el)
    q_above = line[13] * (line[12] - COURANT * (el - line[11]))
    aq = ml * line[8] + kml * el
    ap = ml * line[7] + kml * el
    slast[0:8, :] = ml * el - khml * (pl_new - west_of(pl_new, 0.0) - q_above)
    slast[8:16, :] = aq
    slast[16:24, :] = khml
    for n, x in enumerate((el, aq, kml, ap)):
        stack[n:n + 1, :] = jnp.where(row_lane < 64, x[0:1, :], x[chunks - 1:chunks, :])
    for n in range(3):
        side = adj[0, patch, (0, 2, 3)[n]]
        stack[13 + n:14 + n, :] = jnp.full((1, LANES), side, jnp.int32).astype(f32)

    @pl.when(level == 0)
    def _():
        stack[7:13, :] = jnp.zeros((6, LANES), f32)

    @pl.when(level == 1)
    def _():
        for c in range(chunks):
            lane = slice(c * LANES, (c + 1) * LANES)
            line[14, c:c + 1, :] = gain_v[0:1, lane]
            line[15, c:c + 1, :] = table_v[0:1, lane].astype(f32)
        gain = line[14]
        index = line[15].astype(jnp.int32)
        p_new = mp - km * (east_of(e, 0.0) - e)
        q_new = m * q - km * (line[1] - e)
        there = m * e - khm * (p_new - west_of(p_new, 0.0) + q_new)
        inflow = gain * gather(e, index)
        hm_at = gather(khm, index)
        parts = (inflow, gain * gather(there, index), gain * hm_at,
                 COURANT * hm_at * inflow, line[15])
        for n, x in enumerate(parts):
            slast[32 + 8 * n:40 + 8 * n, :] = x
        rows_of = (inflow, None) + parts[1:]
        for n, x in enumerate(rows_of):
            if x is None:
                low = pltpu.roll(inflow, LANES - 1, 1)[0:1, :]
                high = pltpu.roll(inflow, 1, 1)[chunks - 1:chunks, :]
            else:
                low, high = x[0:1, :], x[chunks - 1:chunks, :]
            stack[7 + n:8 + n, :] = jnp.where(row_lane < 64, low, high)

    turned = jnp.transpose(stack[...])
    for ref in (sfirst, slast):
        ref[24:25, 0:16] = turned[0:1, :]
        ref[25:26, 0:16] = turned[LANES - 1:LANES, :]

    def remote(kind, src, dst, recv_sem, d, h, lev):
        return pltpu.make_async_remote_copy(
            src_ref=src, dst_ref=dst, send_sem=send_sems.at[kind, d], recv_sem=recv_sem,
            device_id={"patch": peers[d], "sub": h, "level": lev},
            device_id_type=pl.DeviceIdType.MESH)

    def column_copy(slot, d):
        return remote(0, scol, rcol.at[slot], recv_sems.at[0, slot], d, half, level)

    def first_copy(slot, d):
        return remote(1, sfirst.at[0:26], rfirst.at[slot, 0:26], recv_sems.at[1, slot], d, other, level)

    def last_copy(slot, d):
        return remote(2, slast.at[0:26], rlast.at[slot, 0:26], recv_sems.at[2, slot], d, other, level)

    def down_copy(part, from_half, slot, d, h):
        at = slice(*part)
        return remote(3 + h, slast.at[at], rdown.at[from_half, slot, at],
                      down_sems.at[from_half, slot], d, h, 1 - level)

    far = list(range(1, patches)) + [0]

    def send_rows(act):
        @pl.when(half == 0)
        def _():
            for d in range(1, patches):
                act(first_copy(patch, d))
            act(last_copy(patch, 0))

        @pl.when(half == 1)
        def _():
            for d in range(1, patches):
                act(last_copy(patch, d))
            act(first_copy(patch, 0))

    def send_down(act):
        @pl.when(jnp.logical_and(level == 1, half == 0))
        def _():
            for d in far:
                act(down_copy(FULL, 0, patch, d, 1))
                act(down_copy(ENDS if d else FULL, 0, patch, d, 0))

        @pl.when(jnp.logical_and(level == 1, half == 1))
        def _():
            for d in far:
                act(down_copy(TAIL if d else FULL, 1, patch, d, 0))
                act(down_copy(TAIL if d else FULL, 1, patch, d, 1))

    def send_columns(act):
        for d in range(1, patches):
            act(column_copy(patch, d))

    def receive():
        @pl.when(half == 0)
        def _():
            first_copy(patch, 0).wait_recv()
            for d in range(1, patches):
                last_copy(peers[d], d).wait_recv()

        @pl.when(half == 1)
        def _():
            last_copy(patch, 0).wait_recv()
            for d in range(1, patches):
                first_copy(peers[d], d).wait_recv()

        for d in range(1, patches):
            column_copy(peers[d], d).wait_recv()

        @pl.when(jnp.logical_and(level == 0, half == 0))
        def _():
            for d in far:
                down_copy(TAIL if d else FULL, 1, peers[d], d, 0).wait_recv()
                down_copy(ENDS if d else FULL, 0, peers[d], d, 0).wait_recv()

        @pl.when(jnp.logical_and(level == 0, half == 1))
        def _():
            for d in far:
                down_copy(TAIL if d else FULL, 1, peers[d], d, 1).wait_recv()
                down_copy(FULL, 0, peers[d], d, 1).wait_recv()

    pl.semaphore_wait(barrier, 2 * patches - 1 + 2 * patches * level)
    send_down(lambda copy: copy.start())
    send_rows(lambda copy: copy.start())

    for copy in loads[n_rows:n_tiles]:
        copy.wait()
    tile_lanes = lax.broadcasted_iota(jnp.int32, (rows, LANES), 1)
    mixed = None
    for lane in (head, tail):
        e = E0[0:rows, lane]
        m = W[:, lane].astype(f32)
        km = COURANT * m
        khm = km * H[:, lane]
        p_new = m * P0[:, lane] - km * (pltpu.roll(e, LANES - 1, 1) - e)
        q_new = m * Q0[8:8 + rows, lane] - km * (E0[1:rows + 1, lane] - e)
        qb[8:8 + rows, :] = q_new
        across = q_new - qb[7:7 + rows, :]
        if lane == head:
            parts = ((e, 0), (m * e - khm * (p_new + across), 0), (khm, 0))
        else:
            parts = ((m * P0[:, lane] + km * e, LANES - 1),
                     (m * e - khm * (across - pltpu.roll(p_new, 1, 1)), LANES - 1),
                     (khm, LANES - 1), (e, LANES - 1), (km, LANES - 2))
        for n, (x, at) in enumerate(parts):
            to = n + (0 if lane == head else 3)
            moved = pltpu.roll(x, (to - at) % LANES, 1) if (to - at) % LANES else x
            mixed = moved if mixed is None else jnp.where(tile_lanes == to, moved, mixed)
    scol[...] = jnp.transpose(mixed[:, 0:8])
    send_columns(lambda copy: copy.start())

    for copy in loads[n_tiles:]:
        copy.wait()
    for r in range(0, rows, BLOCK):
        step_rows(r, E0, P0, Q0, H, W, None, E1, P1, Q1)
    for r in range(0, end, BLOCK):
        step_rows(r, E1, P1, Q1, H, W, None, E2, P2, Q2)

    north, south = adj[0, patch, 0], adj[0, patch, 1]
    west, east = adj[0, patch, 2], adj[0, patch, 3]
    south_ok = jnp.logical_or(half == 0, south >= 0)
    north_ok = jnp.logical_or(half == 1, north >= 0)
    south_at = jnp.where(half == 0, patch, jnp.maximum(south, 0))
    north_at = jnp.where(half == 1, patch, jnp.maximum(north, 0))
    west_ok, east_ok = west >= 0, east >= 0
    west_at, east_at = jnp.maximum(west, 0), jnp.maximum(east, 0)

    def beyond(at, ok, side):
        to = adj[0, at, side]
        return jnp.maximum(to, 0), jnp.logical_and(ok, to >= 0)

    nw_at, nw_ok = beyond(north_at, north_ok, 2)
    ne_at, ne_ok = beyond(north_at, north_ok, 3)
    sw_at, sw_ok = beyond(south_at, south_ok, 2)
    se_at, se_ok = beyond(south_at, south_ok, 3)

    receive()

    @pl.when(level == 1)
    def _():
        flow[...] = jnp.zeros(flow.shape, f32)
        corner[...] = jnp.zeros(corner.shape, f32)

    @pl.when(level == 0)
    def _():
        ends = slice(*ENDS)

        def pick(h, link, at):
            got = None
            for j in range(patches):
                x = jnp.where(link == float(j), rdown[h, j, at, :], 0.0)
                got = x if got is None else got + x
            return got

        own_ends = rdown[half, patch, ends, :]
        south_ends = rdown[other, south_at, ends, :]
        west_ends = rdown[half, west_at, ends, :]
        east_ends = rdown[half, east_at, ends, :]
        near = slice(8, 24)

        def above(x):
            return x[0:1, 13:14]

        @pl.when(half == 0)
        def _():
            nsel[0] = pick(1, above(own_ends), near)
            nsel[1] = rdown[0, patch, near, :]
            nsel[2] = pick(1, above(west_ends), near)
            nsel[3] = pick(1, above(east_ends), near)

        @pl.when(half == 1)
        def _():
            nsel[0] = rdown[0, patch, near, :]
            nsel[1] = pick(1, above(south_ends), near)
            nsel[2] = rdown[0, west_at, near, :]
            nsel[3] = rdown[0, east_at, near, :]

        def terms(h, x):
            w = pick(h, x[0:1, 14:15], ends)
            e = pick(h, x[0:1, 15:16], ends)
            p_edge = w[1:2, 5:6] + w[1:2, 6:7] * (w[1:2, 4:5] - x[0:1, 4:5])
            return p_edge, COURANT * e[0:1, 4:5]

        def wetness(x):
            return (x > 0.0).astype(f32)

        for n, (h, at, x) in enumerate(((half, patch, own_ends), (other, south_at, south_ends))):
            first_term, last_term = terms(h, x)
            index = rdown[h, at, 64:72, :].astype(jnp.int32)
            above_row = gather(nsel[n, 0:8, :], index)
            above_row += jnp.where(index == 0, first_term, 0.0)
            above_row += jnp.where(index == last, last_term, 0.0)
            wet_row = gather(wetness(nsel[n, 8:16, :]), index)
            flow[2 * n] = rdown[h, at, 32:40, :]
            flow[2 * n + 1] = (rdown[h, at, 40:48, :] + rdown[h, at, 48:56, :] * above_row
                               - rdown[h, at, 56:64, :] * wet_row)

        def total(x):
            return jnp.sum(jnp.sum(x, axis=0, keepdims=True), axis=1, keepdims=True)

        for n, x, r in ((2, west_ends, 1), (3, east_ends, 0)):
            first_term, last_term = terms(half, x)
            at = slice(r, r + 1)
            index = x[at, 12:13]
            here = cell_ids.astype(f32) == index
            value = total(jnp.where(here, nsel[n, 0:8, :], 0.0))
            value += jnp.where(index == 0.0, first_term, 0.0)
            value += jnp.where(index == float(last), last_term, 0.0)
            wet_at = total(jnp.where(here, wetness(nsel[n, 8:16, :]), 0.0))
            second = x[at, 9:10] + x[at, 10:11] * value - x[at, 11:12] * wet_at
            for k, v in enumerate((x[at, 7:8], x[at, 8:9], second)):
                corner[3 * (n - 2) + k:3 * (n - 2) + k + 1, :] = jnp.broadcast_to(v, (1, LANES))
        corner[6:7, :] = jnp.broadcast_to(rdown[other, sw_at, 25:26, 7:8], (1, LANES))
        corner[7:8, :] = jnp.broadcast_to(rdown[other, se_at, 24:25, 7:8], (1, LANES))

    def kept(ok, x):
        return jnp.where(ok, x, 0.0)

    @pl.when(half == 0)
    def _():
        tmp[0:1, :] = rlast[north_at, 24:25, :]
        tmp[1:2, :] = rlast[nw_at, 25:26, :]
        tmp[2:3, :] = rlast[ne_at, 24:25, :]
        tmp[3:4, :] = rlast[sw_at, 25:26, :]
        tmp[4:5, :] = rlast[se_at, 24:25, :]

    @pl.when(half == 1)
    def _():
        tmp[0:1, :] = rlast[north_at, 24:25, :]
        tmp[1:2, :] = rfirst[nw_at, 25:26, :]
        tmp[2:3, :] = rfirst[ne_at, 24:25, :]
        tmp[3:4, :] = rfirst[sw_at, 25:26, :]
        tmp[4:5, :] = rfirst[se_at, 24:25, :]

    n_ends = kept(north_ok, tmp[0:1, :])
    nw_ends, ne_ends = kept(nw_ok, tmp[1:2, :]), kept(ne_ok, tmp[2:3, :])
    sw_ends, se_ends = kept(sw_ok, tmp[3:4, :]), kept(se_ok, tmp[4:5, :])
    sw_eta = sw_ends[:, 4:5] + kept(sw_ok, corner[6:7, 0:1])
    se_eta = se_ends[:, 4:5] + kept(se_ok, corner[7:8, 0:1])

    e_below = kept(south_ok, rfirst[south_at, 0:8, :] + flow[2])
    khm = kept(south_ok, rfirst[south_at, 16:24, :])
    m = (khm > 0.0).astype(f32)
    km = COURANT * m
    push = km * (e_below - east_of(e_below, se_eta))
    p_out = sw_ends[:, 5:6] + sw_ends[:, 6:7] * (sw_eta - e_below[0:1, 0:1])
    flat = rfirst[south_at, 8:16, :] + push - west_of(push, p_out) + km * e_below
    below = kept(south_ok, m * e_below - khm * kept(south_ok, flat) + flow[3])
    e_here = e_first + flow[0]
    khm_n = kept(north_ok, rlast[north_at, 16:24, :])
    km_n = COURANT * (khm_n > 0.0).astype(f32)
    q_n = kept(north_ok, rlast[north_at, 8:16, :]) - km_n * e_here
    p_out = nw_ends[:, 3:4] - nw_ends[:, 2:3] * n_ends[:, 0:1]
    side = jnp.where(cell_ids == 0, p_out, 0.0)
    side += jnp.where(cell_ids == last, COURANT * ne_ends[:, 0:1], 0.0)
    e_n = kept(north_ok, rlast[north_at, 0:8, :]) - khm_n * (q_n - side)
    for n, x in enumerate((q_n + km_n * e_n, km_n, below, khm, flow[1])):
        line[n] = x
    line[5] = e_below
    line[6] = q_n
    for c in range(chunks):
        lane = slice(c * LANES, (c + 1) * LANES)
        E0[0:1, lane] += flow[0, c:c + 1, :]
        E0[rows:rows + 1, lane] = line[5, c:c + 1, :]
        Q1[7:8, lane] = line[6, c:c + 1, :]

    first_row, second_row, last_row = row_lane == 0, row_lane == 1, row_lane == rows - 1
    w = kept(west_ok, rcol[west_at])
    khm_w = w[5:6, :]
    m_w = (khm_w > 0.0).astype(f32)
    km_w = COURANT * m_w
    in1 = kept(west_ok, corner[0:1, :])
    in2 = kept(west_ok, corner[1:2, :])
    q_nw = nw_ends[:, 1:2] - nw_ends[:, 2:3] * (w[6:7, :] + in1)
    tip = m_w * in1 - khm_w * (w[7:8, :] * (in1 - in2) + km_w * in1 - q_nw)
    w_share = w[3:4, :] + jnp.where(first_row, km_w * in1, 0.0)
    w_eta = w[4:5, :] + jnp.where(first_row, tip + kept(west_ok, corner[2:3, :]), 0.0)
    w_eta += jnp.where(last_row, khm_w * km_w * sw_eta, 0.0)
    w_eta += jnp.where(second_row, khm_w * km_w[:, 0:1] * in1, 0.0)
    x = kept(east_ok, rcol[east_at])
    khm_e = x[2:3, :]
    m_e = (khm_e > 0.0).astype(f32)
    km_e = COURANT * m_e
    in1 = kept(east_ok, corner[3:4, :])
    in2 = kept(east_ok, corner[4:5, :])
    q_ne = ne_ends[:, 1:2] - ne_ends[:, 2:3] * (x[0:1, :] + in1)
    tip = m_e * in1 + khm_e * (km_e * (in2 - in1) - km_e * in1 + q_ne)
    x_eta = x[0:1, :] + jnp.where(first_row, in1, 0.0)
    x_next = x[1:2, :] + jnp.where(first_row, tip + kept(east_ok, corner[5:6, :]), 0.0)
    x_next += jnp.where(last_row, khm_e * km_e * se_eta, 0.0)
    x_next += jnp.where(second_row, khm_e * km_e[:, 0:1] * in1, 0.0)
    for n, v in enumerate((x_eta, w_share, km_w, w_eta, khm_w, x_next, khm_e)):
        tmp[n:n + 1, :] = v
    tmp[7:8, :] = jnp.zeros((1, LANES), f32)
    halo = jnp.transpose(tmp[...])

    for r in (0, end):
        step_rows(r, E0, P0, Q0, H, W, None, E1, P1, Q1)
    e = E0[0:rows, head]
    wet = W[:, head].astype(f32)
    p_edge = halo[:, 1:2] - halo[:, 2:3] * e[:, 0:1]
    across = Q1[8:8 + rows, head] - Q1[7:7 + rows, head]
    fixed = wet * (e - COURANT * H[:, head] * ((P1[:, head] - p_edge) + across))
    E1[0:rows, head] = jnp.where(tile_lanes == 0, fixed, E1[0:rows, head])
    e = E0[0:rows, tail]
    wet = W[:, tail].astype(f32)
    p = wet * (P0[:, tail] - COURANT * (halo[:, 0:1] - e))
    p = jnp.where(tile_lanes == LANES - 1, p, P1[:, tail])
    P1[:, tail] = p
    across = Q1[8:8 + rows, tail] - Q1[7:7 + rows, tail]
    fixed = wet * (e - COURANT * H[:, tail] * ((p - pltpu.roll(p, 1, 1)) + across))
    E1[0:rows, tail] = jnp.where(tile_lanes == LANES - 1, fixed, E1[0:rows, tail])
    halo_out[:, 0:1] = halo[:, 5:6] + halo[:, 6:7] * p[:, LANES - 1:LANES]
    halo_out[:, 1:2] = p_edge + halo[:, 2:3] * (halo[:, 3:4] - halo[:, 4:5] * p_edge)
    halo_out[:, 2:3] = halo[:, 2:3]
    for c in range(chunks):
        lane = slice(c * LANES, (c + 1) * LANES)
        e1 = E1[0:1, lane] + line[4, c:c + 1, :]
        E1[0:1, lane] = e1
        E1[rows:rows + 1, lane] = line[2, c:c + 1, :] + line[3, c:c + 1, :] * Q1[rows + 7:rows + 8, lane]
        Q2[7:8, lane] = line[0, c:c + 1, :] - line[1, c:c + 1, :] * e1
    send_columns(lambda copy: copy.wait_send())
    send_rows(lambda copy: copy.wait_send())
    send_down(lambda copy: copy.wait_send())


def two_level(mesh, adjoint_height, adjoint_momenta, depth, wet_mask, adjacency, nest_gain, nest_index):
    patches = mesh.shape["patch"]
    rows, cols = adjoint_height.shape[1:]
    chunks = cols // LANES
    f32 = jnp.float32
    anywhere = pl.BlockSpec(memory_space=pl.ANY)
    v = pltpu.VMEM
    dma = pltpu.SemaphoreType.DMA
    whole = (v((rows + 8, cols), f32), v((rows, cols), f32), v((rows + 8, cols), f32))
    scratch = [
        pltpu.SMEM(adjacency.shape, jnp.int32),
        *whole,
        v(nest_gain.shape, f32), v(nest_index.shape, jnp.int32),
        v((16, chunks, LANES), f32), v((16, LANES), f32), v((rows + 8, LANES), f32),
        v((32, LANES), f32), v((72, LANES), f32), v((8, LANES), f32),
        v((4, 16, LANES), f32), v((4, chunks, LANES), f32), v((8, LANES), f32), v((8, LANES), f32),
        dma((28,)), dma((5, patches)), dma((3, patches)), dma((2, patches)),
        v((patches, 32, LANES), f32), v((patches, 32, LANES), f32), v((patches, 8, LANES), f32),
        v((2, patches, 72, LANES), f32),
    ]
    here = pl.BlockSpec(memory_space=pltpu.VMEM)
    state = pl.pallas_call(
        functools.partial(swap, patches, rows, cols),
        out_shape=(*whole, v((rows, cols), f32), v((rows, cols), jnp.int32), v((rows, 8), f32), *whole),
        in_specs=[anywhere] * 7,
        out_specs=(here,) * 9,
        scratch_shapes=scratch,
        compiler_params=pltpu.CompilerParams(collective_id=0, has_side_effects=True,
                                             vmem_limit_bytes=14 << 20),
    )(*[pltpu.with_memory_space_constraint(x, pltpu.HBM) for x in (
        adjacency, adjoint_height, adjoint_momenta, depth, wet_mask, nest_gain, nest_index)])
    state = [pltpu.with_memory_space_constraint(x, pltpu.VMEM) for x in state]
    return pl.pallas_call(
        functools.partial(settle, rows),
        out_shape=(jax.ShapeDtypeStruct(adjoint_height.shape, f32),
                   jax.ShapeDtypeStruct(adjoint_momenta.shape, f32)),
        in_specs=[here] * 9,
        out_specs=(anywhere, anywhere),
        scratch_shapes=[*whole, dma((15,))],
        compiler_params=pltpu.CompilerParams(vmem_limit_bytes=12 << 20),
    )(*state)


def solution(mesh):
    in_specs = (
        P(("parts", "level"), ("patch", "sub"), None),
        P(None, ("parts", "level"), ("patch", "sub"), None),
        P("level", ("patch", "sub"), None),
        P("level", ("patch", "sub"), None),
        P("level", None, None),
        P(None, ("patch", "sub")),
        P(None, ("patch", "sub")),
    )
    out_specs = (
        P(("parts", "level"), ("patch", "sub"), None),
        P(None, ("parts", "level"), ("patch", "sub"), None),
    )
    run = two_level if mesh.shape["level"] == 2 else body
    return jax.shard_map(functools.partial(run, mesh), mesh=mesh, in_specs=in_specs,
                         out_specs=out_specs, check_vma=False)
```

```python
import functools

import jax
import jax.numpy as jnp
from jax import lax
from jax.experimental import pallas as pl
from jax.experimental.pallas import tpu as pltpu
from jax.sharding import PartitionSpec as P

STEPS = 2
COURANT = 0.45
LANES = 128
BLOCK = 8


def advance(r, E, Pm, Q, H, W, halo, E_to, P_to, Q_to):
    cols = Pm.shape[1]
    lane_ids = lax.broadcasted_iota(jnp.int32, (BLOCK, cols), 1)
    span = slice(r, r + BLOCK)
    e = E[span, :]
    wet = W[span, :].astype(jnp.float32)
    e_south = E[r + 1:r + 1 + BLOCK, :]
    e_east = pltpu.roll(e, cols - 1, 1)
    if halo is not None:
        e_east = jnp.where(lane_ids == cols - 1, halo[span, 0:1], e_east)
    p = wet * (Pm[span, :] - COURANT * (e_east - e))
    q = wet * (Q[8 + r:16 + r, :] - COURANT * (e_south - e))
    p_west = pltpu.roll(p, 1, 1)
    if halo is not None:
        p_edge = halo[span, 1:2] - COURANT * halo[span, 2:3] * e[:, 0:1]
        p_west = jnp.where(lane_ids == 0, p_edge, p_west)
    P_to[span, :] = p
    Q_to[8 + r:16 + r, :] = q
    q_north = Q_to[7 + r:15 + r, :]
    E_to[span, :] = wet * (e - COURANT * H[span, :] * ((p - p_west) + (q - q_north)))


def finish(rows, E, Pm, Q, H, W, halo, E2, P2, Q2, eta_out, mom_out, Ef, Pf, Qf, sems):
    cols = Pm.shape[1]
    end = rows - BLOCK
    mid = slice(BLOCK, end)
    head, tail = slice(0, LANES), slice(cols - LANES, cols)
    before, inner = slice(0, cols - LANES), slice(LANES, cols - LANES)
    stores = []

    def store(src, dst):
        copy = pltpu.make_async_copy(src, dst, sems.at[len(stores)])
        copy.start()
        stores.append(copy)

    eta_to, row_to, col_to = eta_out.at[0], mom_out.at[0, 0], mom_out.at[1, 0]
    store(Q2.at[BLOCK + 8:end + 8], col_to.at[mid])
    store(P2.at[mid, before], row_to.at[mid, before])
    store(E2.at[mid, inner], eta_to.at[mid, inner])
    edges = halo[...]
    lane_ids = lax.broadcasted_iota(jnp.int32, (end - BLOCK, LANES), 1)

    across = Q2[BLOCK + 8:end + 8, head] - Q2[BLOCK + 7:end + 7, head]
    e = E[mid, head]
    wet = W[mid, head].astype(jnp.float32)
    p_edge = edges[mid, 1:2] - COURANT * edges[mid, 2:3] * e[:, 0:1]
    fixed = wet * (e - COURANT * H[mid, head] * ((P2[mid, head] - p_edge) + across))
    Ef[mid, head] = jnp.where(lane_ids == 0, fixed, E2[mid, head])
    store(Ef.at[mid, head], eta_to.at[mid, head])

    across = Q2[BLOCK + 8:end + 8, tail] - Q2[BLOCK + 7:end + 7, tail]
    e = E[mid, tail]
    wet = W[mid, tail].astype(jnp.float32)
    p = wet * (Pm[mid, tail] - COURANT * (edges[mid, 0:1] - e))
    p = jnp.where(lane_ids == LANES - 1, p, P2[mid, tail])
    Pf[mid, tail] = p
    store(Pf.at[mid, tail], row_to.at[mid, tail])
    fixed = wet * (e - COURANT * H[mid, tail] * ((p - pltpu.roll(p, 1, 1)) + across))
    Ef[mid, tail] = jnp.where(lane_ids == LANES - 1, fixed, E2[mid, tail])
    store(Ef.at[mid, tail], eta_to.at[mid, tail])

    for r in (0, end):
        Qf[7 + r:8 + r, :] = (Q if r == 0 else Q2)[7 + r:8 + r, :]
        advance(r, E, Pm, Q, H, W, edges, Ef, Pf, Qf)
        at = slice(r, r + BLOCK)
        store(Pf.at[at], row_to.at[at])
        store(Qf.at[8 + r:16 + r], col_to.at[at])
        store(Ef.at[at], eta_to.at[at])
    for copy in stores:
        copy.wait()


def exchange(patches, levels, rows, cols,
             adj_hbm, eta_hbm, mom_hbm, depth_hbm, wet_hbm, gain_hbm, table_hbm,
             E1, P1, Q1, H, W, halo_out, E2, P2, Q2,
             adj, E0, P0, Q0, gain_v, table_v, f8, idx8, gain8, tmp,
             sfirst, slast, scol, sinf, sew,
             rown, in_sems, send_sems, recv_sems, own_sems, *landing):
    rfirst, rlast, rcol, rnbr, rew = (landing[n * STEPS:(n + 1) * STEPS] for n in range(5))
    fields = ((E0, P0, Q0), (E1, P1, Q1))
    patch = lax.axis_index("patch")
    level = lax.axis_index("level")
    half = lax.axis_index("sub")
    chunks = cols // LANES
    other = 1 - half

    loads = [
        pltpu.make_async_copy(eta_hbm.at[0], E0.at[0:rows], in_sems.at[0]),
        pltpu.make_async_copy(mom_hbm.at[0, 0], P0, in_sems.at[1]),
        pltpu.make_async_copy(mom_hbm.at[1, 0], Q0.at[8:8 + rows], in_sems.at[2]),
        pltpu.make_async_copy(wet_hbm.at[0], W, in_sems.at[3]),
        pltpu.make_async_copy(table_hbm, table_v, in_sems.at[4]),
        pltpu.make_async_copy(gain_hbm, gain_v, in_sems.at[5]),
        pltpu.make_async_copy(adj_hbm, adj, in_sems.at[6]),
        pltpu.make_async_copy(depth_hbm.at[0], H, in_sems.at[7]),
    ]
    barrier = pltpu.get_barrier_semaphore()

    peers = [patch] + [lax.rem(patch + d, patches) for d in range(1, patches)]

    def greet(d, h, lev):
        pl.semaphore_signal(barrier, inc=1, device_id={
            "patch": peers[d], "sub": h, "level": lev},
            device_id_type=pl.DeviceIdType.MESH)

    for d in range(patches - 1, -1, -1):
        greet(d, other, level)
        if d:
            greet(d, half, level)

    @pl.when(level > 0)
    def _():
        for d in range(patches):
            greet(d, half, level - 1)
            greet(d, other, level - 1)

    @pl.when(level < levels - 1)
    def _():
        for d in range(patches):
            greet(d, half, level + 1)
            greet(d, other, level + 1)

    for load in loads:
        load.start()

    for load in loads[:7]:
        load.wait()

    lower = jnp.maximum(level - 1, 0)
    for c in range(chunks):
        lane = slice(c * LANES, (c + 1) * LANES)
        index, gain = table_v[0:1, lane], gain_v[0:1, lane]
        for lev in range(1, levels - 1):
            index = jnp.where(lower == lev, table_v[lev:lev + 1, lane], index)
            gain = jnp.where(lower == lev, gain_v[lev:lev + 1, lane], gain)
        idx8[c:c + 1, :] = index
        gain8[c:c + 1, :] = gain

    def remote(t, kind, src, buf, slot, d, h, lev):
        return pltpu.make_async_remote_copy(
            src_ref=src, dst_ref=buf, send_sem=send_sems.at[t, kind, d],
            recv_sem=recv_sems.at[t, kind, slot],
            device_id={"patch": peers[d], "sub": h, "level": lev},
            device_id_type=pl.DeviceIdType.MESH)

    def last_part(t):
        return slice(0, 2) if t == 0 else slice(t + 1, t + 2)

    def column_copy(t, slot, d):
        return remote(t, 0, scol.at[t, 0:3], rcol[t].at[slot, 0:3], slot, d, half, level)

    def first_copy(t, slot, d):
        return remote(t, 1, sfirst.at[t], rfirst[t].at[slot], slot, d, other, level)

    def last_copy(t, slot, d):
        part = last_part(t)
        return remote(t, 2, slast.at[part], rlast[t].at[slot], slot, d, other, level)

    def beside_copy(t, slot, d):
        return remote(t, 3, sinf.at[t], rnbr[t].at[slot], slot, d, other, lower)

    def ends_copy(t, slot, d):
        return remote(t, 4, sew.at[t], rew[t].at[slot], slot, d, half, lower)

    def per_half(across, inside, act):
        @pl.when(half == across)
        def _():
            for d in range(1, patches):
                act(d)

        @pl.when(half == inside)
        def _():
            act(0)

    def own_copy(t):
        return pltpu.make_async_remote_copy(
            src_ref=sinf.at[t], dst_ref=rown.at[t], send_sem=own_sems.at[t, 0],
            recv_sem=own_sems.at[t, 1], device_id={"level": lower},
            device_id_type=pl.DeviceIdType.MESH)

    def make_inflow(t):
        E = fields[t][0]
        for c in range(chunks):
            f8[c:c + 1, :] = E[0:1, c * LANES:(c + 1) * LANES]
        index = idx8[...]
        inside = jnp.bitwise_and(index, LANES - 1)
        which = lax.shift_right_logical(index, 7)
        picked = jnp.zeros((chunks, LANES), jnp.float32)
        for c in range(chunks):
            source = jnp.broadcast_to(f8[c:c + 1, :], (chunks, LANES))
            got = jnp.take_along_axis(source, inside, axis=1, mode="promise_in_bounds")
            picked = jnp.where(which == c, got, picked)
        inflow = gain8[...] * picked
        sinf[t] = inflow
        sew[t, 0:1, :] = inflow[0:1, :]
        sew[t, 1:2, :] = pltpu.roll(inflow[chunks - 1:chunks, :], 1, 1)

    def send_inflow(t):
        own_copy(t).start()
        per_half(0, 1, lambda d: beside_copy(t, patch, d).start())
        for d in range(1, patches):
            ends_copy(t, patch, d).start()

    def inflow_waits(t):
        per_half(1, 0, lambda d: beside_copy(t, peers[d], d).wait_recv())
        for d in range(1, patches):
            ends_copy(t, peers[d], d).wait_recv()

    def inflow_send_waits(t):
        own_copy(t).wait_send()
        per_half(0, 1, lambda d: beside_copy(t, patch, d).wait_send())
        for d in range(1, patches):
            ends_copy(t, patch, d).wait_send()

    def send_halos(t, act):
        send_rows(t, act)
        send_columns(t, act)

    def send_columns(t, act):
        for d in range(1, patches):
            act(column_copy(t, patch, d))

    def send_rows(t, act):
        @pl.when(half == 0)
        def _():
            for d in range(1, patches):
                act(first_copy(t, patch, d))
            act(last_copy(t, patch, 0))

        @pl.when(half == 1)
        def _():
            for d in range(1, patches):
                act(last_copy(t, patch, d))
            act(first_copy(t, patch, 0))

    def receive_halos(t):
        @pl.when(half == 0)
        def _():
            first_copy(t, peers[0], 0).wait_recv()
            for d in range(1, patches):
                last_copy(t, peers[d], d).wait_recv()

        @pl.when(half == 1)
        def _():
            last_copy(t, peers[0], 0).wait_recv()
            for d in range(1, patches):
                first_copy(t, peers[d], d).wait_recv()

        for d in range(1, patches):
            column_copy(t, peers[d], d).wait_recv()

    north = adj[0, patch, 0]
    south = adj[0, patch, 1]
    west = adj[0, patch, 2]
    east = adj[0, patch, 3]
    south_ok = jnp.logical_or(half == 0, south >= 0)
    north_ok = jnp.logical_or(half == 1, north >= 0)
    south_at = jnp.where(half == 0, patch, jnp.maximum(south, 0))
    north_at = jnp.where(half == 1, patch, jnp.maximum(north, 0))
    west_at = jnp.maximum(west, 0)
    east_at = jnp.maximum(east, 0)
    finer = level < levels - 1
    lane_ids = lax.broadcasted_iota(jnp.int32, (rows, LANES), 1)
    first_lane = lax.broadcasted_iota(jnp.int32, (1, LANES), 1) == 0
    tail = slice(cols - LANES, cols)
    end = rows - 1

    def make_messages(t):
        @pl.when(level == levels - 1)
        def _():
            make_inflow(t)

        make_rows(t)
        make_columns(t)

    def make_rows(t):
        E, Pm, Q = fields[t]
        sfirst[t] = E[0:1, :]
        wet_row = W[end:rows, :].astype(jnp.float32)
        slast[t + 1] = wet_row * (Q[8 + end:8 + rows, :] + COURANT * E[end:rows, :])
        if t == 0:
            slast[0] = wet_row

    def make_columns(t):
        E, Pm, Q = fields[t]
        wet_tail = W[:, tail].astype(jnp.float32)
        share = wet_tail * (Pm[:, tail] + COURANT * E[0:rows, tail])
        mixed = jnp.where(lane_ids == 0, E[0:rows, 0:LANES],
                          jnp.where(lane_ids == 1, pltpu.roll(share, 2, 1),
                                    pltpu.roll(wet_tail, 3, 1)))
        scol[t] = jnp.transpose(mixed[:, 0:8])

    def send_messages(t):
        @pl.when(level == levels - 1)
        def _():
            send_inflow(t)

        send_halos(t, lambda copy: copy.start())

    def receive(t):
        E, Pm, Q = fields[t]

        @pl.when(finer)
        def _():
            own_copy(t).wait_recv()
            for c in range(chunks):
                lane = slice(c * LANES, (c + 1) * LANES)
                E[0:1, lane] += rown[t, c:c + 1, :]

        if levels > 2:
            @pl.when(jnp.logical_and(level > 0, level < levels - 1))
            def _():
                make_inflow(t)
                send_inflow(t)

        receive_halos(t)

        @pl.when(finer)
        def _():
            inflow_waits(t)

        east_row = rcol[t][east_at][0:1, :]
        east_row += jnp.where(jnp.logical_and(first_lane, finer), rew[t][east_at][0:1, :], 0.0)
        west_cols = rcol[t][west_at]
        share = west_cols[1:2, :]
        wet_w = west_cols[2:3, :]
        share += jnp.where(jnp.logical_and(first_lane, finer),
                           COURANT * wet_w * rew[t][west_at][1:2, :], 0.0)
        tmp[0:1, :] = jnp.where(east >= 0, east_row, 0.0)
        tmp[1:2, :] = jnp.where(west >= 0, share, 0.0)
        tmp[2:3, :] = jnp.where(west >= 0, wet_w, 0.0)
        beside = rnbr[t][south_at]
        below = rfirst[t][south_at]
        for c in range(chunks):
            lane = slice(c * LANES, (c + 1) * LANES)
            value = below[:, lane] + jnp.where(finer, beside[c:c + 1, :], 0.0)
            E[rows:rows + 1, lane] = jnp.where(south_ok, value, 0.0)
        share_n = rlast[t][north_at, 1 if t == 0 else 0]
        wet_n = rlast[0][north_at, 0]
        Q_to = Q1
        Q_to[7:8, :] = jnp.where(north_ok, share_n - COURANT * wet_n * E[0:1, :], 0.0)
        return jnp.transpose(tmp[...])

    make_messages(0)
    sides = (level > 0).astype(jnp.int32) + (level < levels - 1).astype(jnp.int32)
    pl.semaphore_wait(barrier, 2 * patches - 1 + 2 * patches * sides)
    send_messages(0)
    loads[7].wait()
    for r in range(0, rows - BLOCK, BLOCK):
        advance(r, E0, P0, Q0, H, W, None, E1, P1, Q1)
    halo = receive(0)
    for r in (0, rows - BLOCK):
        advance(r, E0, P0, Q0, H, W, None, E1, P1, Q1)
    head = slice(0, LANES)
    e = E0[0:rows, head]
    wet = W[:, head].astype(jnp.float32)
    p_edge = halo[:, 1:2] - COURANT * halo[:, 2:3] * e[:, 0:1]
    across = Q1[8:8 + rows, head] - Q1[7:7 + rows, head]
    fixed = wet * (e - COURANT * H[:, head] * ((P1[:, head] - p_edge) + across))
    E1[0:rows, head] = jnp.where(lane_ids == 0, fixed, E1[0:rows, head])
    e = E0[0:rows, tail]
    wet = W[:, tail].astype(jnp.float32)
    p = wet * (P0[:, tail] - COURANT * (halo[:, 0:1] - e))
    p = jnp.where(lane_ids == LANES - 1, p, P1[:, tail])
    P1[:, tail] = p
    across = Q1[8:8 + rows, tail] - Q1[7:7 + rows, tail]
    fixed = wet * (e - COURANT * H[:, tail] * ((p - pltpu.roll(p, 1, 1)) + across))
    E1[0:rows, tail] = jnp.where(lane_ids == LANES - 1, fixed, E1[0:rows, tail])

    @pl.when(level == levels - 1)
    def _():
        make_inflow(1)
        send_inflow(1)

    make_rows(1)
    send_rows(1, lambda copy: copy.start())
    make_columns(1)
    send_columns(1, lambda copy: copy.start())
    for r in range(0, rows - BLOCK, BLOCK):
        advance(r, E1, P1, Q1, H, W, None, E2, P2, Q2)
    halo_out[...] = receive(1)
    for t in range(STEPS):
        send_halos(t, lambda copy: copy.wait_send())

        @pl.when(level > 0)
        def _():
            inflow_send_waits(t)


def body(mesh, adjoint_height, adjoint_momenta, depth, wet_mask, adjacency, nest_gain, nest_index):
    patches, levels = mesh.shape["patch"], mesh.shape["level"]
    rows, cols = adjoint_height.shape[1:]
    chunks = cols // LANES
    f32 = jnp.float32
    anywhere = pl.BlockSpec(memory_space=pl.ANY)
    v = pltpu.VMEM
    dma = pltpu.SemaphoreType.DMA
    whole = (v((rows + 8, cols), f32), v((rows, cols), f32), v((rows + 8, cols), f32))
    scratch = [
        pltpu.SMEM(adjacency.shape, jnp.int32),
        *whole,
        v(nest_gain.shape, f32), v(nest_index.shape, jnp.int32),
        v((chunks, LANES), f32), v((chunks, LANES), jnp.int32), v((chunks, LANES), f32),
        v((8, LANES), f32),
        v((STEPS, 1, cols), f32), v((STEPS + 1, 1, cols), f32), v((STEPS, 8, LANES), f32),
        v((STEPS, chunks, LANES), f32), v((STEPS, 2, LANES), f32),
        v((STEPS, chunks, LANES), f32),
        dma((8,)), dma((STEPS, 5, patches)), dma((STEPS, 5, patches)), dma((STEPS, 2)),
    ]
    scratch += [v((patches, 1, cols), f32)] * STEPS
    scratch += [v((patches, 2 if t == 0 else 1, 1, cols), f32) for t in range(STEPS)]
    scratch += [v((patches, 8, LANES), f32)] * STEPS
    scratch += [v((patches, chunks, LANES), f32)] * STEPS
    scratch += [v((patches, 2, LANES), f32)] * STEPS
    here = pl.BlockSpec(memory_space=pltpu.VMEM)
    state = pl.pallas_call(
        functools.partial(exchange, patches, levels, rows, cols),
        out_shape=(*whole, v((rows, cols), f32), v((rows, cols), jnp.int32), v((rows, 8), f32), *whole),
        in_specs=[anywhere] * 7,
        out_specs=(here,) * 9,
        scratch_shapes=scratch,
        compiler_params=pltpu.CompilerParams(collective_id=0, has_side_effects=True,
                                             vmem_limit_bytes=12 << 20),
    )(*[pltpu.with_memory_space_constraint(x, pltpu.HBM) for x in (
        adjacency, adjoint_height, adjoint_momenta, depth, wet_mask, nest_gain, nest_index)])
    state = [pltpu.with_memory_space_constraint(x, pltpu.VMEM) for x in state]
    return pl.pallas_call(
        functools.partial(finish, rows),
        out_shape=(jax.ShapeDtypeStruct(adjoint_height.shape, f32),
                   jax.ShapeDtypeStruct(adjoint_momenta.shape, f32)),
        in_specs=[here] * 9,
        out_specs=(anywhere, anywhere),
        scratch_shapes=[*whole, dma((12,))],
        compiler_params=pltpu.CompilerParams(vmem_limit_bytes=12 << 20),
    )(*state)


FULL, TAIL, ENDS = (0, 58), (40, 58), (56, 58)
DRY = 1e30


def step_rows(r, E, Pm, Q, H, W, edge, E_to, P_to, Q_to):
    cols = Pm.shape[1]
    lane_ids = lax.broadcasted_iota(jnp.int32, (BLOCK, cols), 1)
    span = slice(r, r + BLOCK)
    e = E[span, :]
    wet = W[span, :].astype(jnp.float32)
    e_south = E[r + 1:r + 1 + BLOCK, :]
    e_east = pltpu.roll(e, cols - 1, 1)
    if edge is not None:
        e_east = jnp.where(lane_ids == cols - 1, edge[span, 0:1], e_east)
    p = wet * (Pm[span, :] - COURANT * (e_east - e))
    q = wet * (Q[8 + r:16 + r, :] - COURANT * (e_south - e))
    p_west = pltpu.roll(p, 1, 1)
    if edge is not None:
        p_west = jnp.where(lane_ids == 0, edge[span, 1:2] - edge[span, 2:3] * e[:, 0:1], p_west)
    P_to[span, :] = p
    Q_to[8 + r:16 + r, :] = q
    q_north = Q_to[7 + r:15 + r, :]
    E_to[span, :] = wet * (e - COURANT * H[span, :] * ((p - p_west) + (q - q_north)))


def settle(rows, E, Pm, Q, H, W, halo, E2, P2, Q2, eta_out, mom_out, Ef, Pf, Qf, sems):
    end = rows - BLOCK
    mid = slice(BLOCK, end)
    stores = []

    def store(src, dst):
        copy = pltpu.make_async_copy(src, dst, sems.at[len(stores)])
        copy.start()
        stores.append(copy)

    eta_to, row_to, col_to = eta_out.at[0], mom_out.at[0, 0], mom_out.at[1, 0]
    store(Q2.at[BLOCK + 8:end + 8], col_to.at[mid])
    store(P2.at[mid], row_to.at[mid])
    store(E2.at[mid], eta_to.at[mid])
    edge = halo[...]

    def ends(r):
        step_rows(r, E, Pm, Q, H, W, edge, Ef, Pf, Qf)
        at = slice(r, r + BLOCK)
        store(Pf.at[at], row_to.at[at])
        store(Qf.at[8 + r:16 + r], col_to.at[at])
        store(Ef.at[at], eta_to.at[at])

    for r in (0, end):
        Qf[7 + r:8 + r, :] = Q2[7 + r:8 + r, :]
        ends(r)
    for copy in stores:
        copy.wait()


def swap(patches, rows, cols,
         adj_hbm, eta_hbm, mom_hbm, depth_hbm, wet_hbm, gain_hbm, table_hbm,
         E1, P1, Q1, H, W, halo_out, E2, P2, Q2,
         adj, fine, E0, P0, Q0, gain_v, table_v, line, stack, qb, sfirst, slast, sdown, scol,
         flow, corner, tmp, in_sems, send_sems, recv_sems, down_sems, fine_sems,
         rfirst, rlast, rcol, rdown):
    f32 = jnp.float32
    patch = lax.axis_index("patch")
    level = lax.axis_index("level")
    half = lax.axis_index("sub")
    other = 1 - half
    chunks = cols // LANES
    last = cols - 1
    end = rows - BLOCK
    head, tail = slice(0, LANES), slice(cols - LANES, cols)
    inner = slice(LANES, cols - LANES)
    mid = slice(BLOCK, end)
    loads = []

    def load(src, dst):
        copy = pltpu.make_async_copy(src, dst, in_sems.at[len(loads)])
        copy.start()
        loads.append(copy)

    fields = ((eta_hbm.at[0], E0, 0), (mom_hbm.at[0, 0], P0, 0), (mom_hbm.at[1, 0], Q0, 8),
              (wet_hbm.at[0], W, 0), (depth_hbm.at[0], H, 0))

    def load_part(at, lane):
        for src, dst, shift in fields:
            load(src.at[at, lane], dst.at[at.start + shift:at.stop + shift, lane])

    for at in (slice(0, BLOCK), slice(end, rows)):
        load_part(at, slice(0, cols))
    load(adj_hbm, adj)
    load(table_hbm, table_v)
    load(gain_hbm, gain_v)
    n_rows = len(loads)

    barrier = pltpu.get_barrier_semaphore()
    peers = [patch] + [lax.rem(patch + d, patches) for d in range(1, patches)]

    def greet(d, h, lev):
        pl.semaphore_signal(barrier, inc=1, device_id={
            "patch": peers[d], "sub": h, "level": lev},
            device_id_type=pl.DeviceIdType.MESH)

    for d in range(1, patches):
        greet(d, other, level)
        greet(d, half, level)
    greet(0, other, level)

    @pl.when(level == 0)
    def _():
        for d in list(range(1, patches)) + [0]:
            greet(d, half, 1)
            greet(d, other, 1)

    for lane in (head, tail):
        load_part(mid, lane)
    n_tiles = len(loads)
    load_part(mid, inner)

    E0[rows:rows + 8, :] = jnp.zeros((8, cols), f32)
    qb[0:8, :] = jnp.zeros((8, LANES), f32)
    lane_ids = lax.broadcasted_iota(jnp.int32, (chunks, LANES), 1)
    cell_ids = lax.broadcasted_iota(jnp.int32, (chunks, LANES), 0) * LANES + lane_ids
    row_lane = lax.broadcasted_iota(jnp.int32, (1, LANES), 1)

    def east_of(x, beyond):
        y = pltpu.roll(x, LANES - 1, 1)
        y = jnp.where(lane_ids == LANES - 1, pltpu.roll(y, chunks - 1, 0), y)
        return jnp.where(cell_ids == last, beyond, y)

    def west_of(x, beyond):
        y = pltpu.roll(x, 1, 1)
        y = jnp.where(lane_ids == 0, pltpu.roll(y, 1, 0), y)
        return jnp.where(cell_ids == 0, beyond, y)

    def gather(x, index):
        inside = jnp.bitwise_and(index, LANES - 1)
        which = lax.shift_right_logical(index, 7)
        picked = jnp.zeros((chunks, LANES), f32)
        for c in range(chunks):
            source = jnp.broadcast_to(x[c:c + 1, :], (chunks, LANES))
            got = jnp.take_along_axis(source, inside, axis=1, mode="promise_in_bounds")
            picked = jnp.where(which == c, got, picked)
        return picked

    for copy in loads[:n_rows]:
        copy.wait()

    def lines(n, ref, r):
        for c in range(chunks):
            line[n, c:c + 1, :] = ref[r:r + 1, c * LANES:(c + 1) * LANES].astype(f32)

    for n, (ref, r) in enumerate((
            (E0, 0), (E0, 1), (P0, 0), (Q0, 8), (W, 0), (H, 0),
            (E0, rows - 1), (P0, rows - 1), (Q0, rows + 7), (W, rows - 1), (H, rows - 1),
            (E0, rows - 2), (Q0, rows + 6), (W, rows - 2))):
        lines(n, ref, r)

    e, p, q, m = line[0], line[2], line[3], line[4]
    e_first = e
    km = COURANT * m
    khm = km * line[5]
    mp = m * p
    sfirst[0:8, :] = e
    sfirst[8:16, :] = mp - west_of(mp, 0.0) + (m * q - km * line[1])
    sfirst[16:24, :] = khm
    stack[4:5, :] = jnp.where(row_lane < 64, e[0:1, :], e[chunks - 1:chunks, :])
    stack[5:6, :] = jnp.where(row_lane < 64, mp[0:1, :], mp[chunks - 1:chunks, :])
    stack[6:7, :] = jnp.where(row_lane < 64, km[0:1, :], km[chunks - 1:chunks, :])
    el, ml = line[6], line[9]
    kml = COURANT * ml
    khml = kml * line[10]
    pl_new = ml * line[7] - kml * (east_of(el, 0.0) - el)
    q_above = line[13] * (line[12] - COURANT * (el - line[11]))
    aq = ml * line[8] + kml * el
    ap = ml * line[7] + kml * el
    slast[0:8, :] = ml * el - khml * (pl_new - west_of(pl_new, 0.0) - q_above)
    slast[8:16, :] = aq
    slast[16:24, :] = khml
    sdown[40:48, :] = aq
    sdown[48:56, :] = khml
    for n, x in enumerate((el, aq, kml, ap)):
        stack[n:n + 1, :] = jnp.where(row_lane < 64, x[0:1, :], x[chunks - 1:chunks, :])
    stack[13:16, :] = jnp.zeros((3, LANES), f32)

    @pl.when(level == 0)
    def _():
        stack[7:13, :] = jnp.zeros((6, LANES), f32)

    @pl.when(level == 1)
    def _():
        for c in range(chunks):
            lane = slice(c * LANES, (c + 1) * LANES)
            line[14, c:c + 1, :] = gain_v[0:1, lane]
            line[15, c:c + 1, :] = table_v[0:1, lane].astype(f32)
        gain = line[14]
        index = line[15].astype(jnp.int32)
        p_new = mp - km * (east_of(e, 0.0) - e)
        q_new = m * q - km * (line[1] - e)
        there = m * e - khm * (p_new - west_of(p_new, 0.0) + q_new)
        inflow = gain * gather(e, index)
        hm_at = gather(khm, index)
        parts = (inflow, gain * gather(there, index), gain * hm_at,
                 COURANT * hm_at * inflow, line[15])
        for n, x in enumerate(parts):
            sdown[8 * n:8 * n + 8, :] = x
        rows_of = (inflow, None) + parts[1:]
        for n, x in enumerate(rows_of):
            if x is None:
                low = pltpu.roll(inflow, LANES - 1, 1)[0:1, :]
                high = pltpu.roll(inflow, 1, 1)[chunks - 1:chunks, :]
            else:
                low, high = x[0:1, :], x[chunks - 1:chunks, :]
            stack[7 + n:8 + n, :] = jnp.where(row_lane < 64, low, high)

    turned = jnp.transpose(stack[...])
    for ref, at in ((sfirst, 24), (slast, 24), (sdown, 56)):
        ref[at:at + 1, 0:16] = turned[0:1, :]
        ref[at + 1:at + 2, 0:16] = turned[LANES - 1:LANES, :]

    def remote(kind, src, dst, recv_sem, d, h, lev):
        return pltpu.make_async_remote_copy(
            src_ref=src, dst_ref=dst, send_sem=send_sems.at[kind, d], recv_sem=recv_sem,
            device_id={"patch": peers[d], "sub": h, "level": lev},
            device_id_type=pl.DeviceIdType.MESH)

    def column_copy(slot, d):
        return remote(0, scol, rcol.at[slot], recv_sems.at[0, slot], d, half, level)

    def first_copy(slot, d):
        return remote(1, sfirst.at[0:26], rfirst.at[slot, 0:26], recv_sems.at[1, slot], d, other, level)

    def last_copy(slot, d):
        return remote(2, slast.at[0:26], rlast.at[slot, 0:26], recv_sems.at[2, slot], d, other, level)

    def down_copy(part, from_half, slot, d, h):
        at = slice(*part)
        return remote(3 + h, sdown.at[at], rdown.at[from_half, slot, at],
                      down_sems.at[from_half, slot], d, h, 1 - level)

    def fine_copy():
        return pltpu.make_async_remote_copy(
            src_ref=adj, dst_ref=fine, send_sem=fine_sems.at[0], recv_sem=fine_sems.at[1],
            device_id={"level": 1 - level}, device_id_type=pl.DeviceIdType.MESH)

    far = list(range(1, patches)) + [0]

    def send_rows(act):
        @pl.when(half == 0)
        def _():
            for d in range(1, patches):
                act(first_copy(patch, d))
            act(last_copy(patch, 0))

        @pl.when(half == 1)
        def _():
            for d in range(1, patches):
                act(last_copy(patch, d))
            act(first_copy(patch, 0))

    def send_down(act):
        @pl.when(jnp.logical_and(level == 1, half == 0))
        def _():
            for d in far:
                act(down_copy(FULL, 0, patch, d, 1))
                act(down_copy(ENDS if d else FULL, 0, patch, d, 0))

        @pl.when(jnp.logical_and(level == 1, half == 1))
        def _():
            for d in far:
                act(down_copy(TAIL if d else FULL, 1, patch, d, 0))
                act(down_copy(TAIL if d else FULL, 1, patch, d, 1))

    def send_columns(act):
        for d in range(1, patches):
            act(column_copy(patch, d))

    def receive_columns():
        for d in range(1, patches):
            column_copy(peers[d], d).wait_recv()

    def receive_rows():
        @pl.when(half == 0)
        def _():
            first_copy(patch, 0).wait_recv()
            for d in range(1, patches):
                last_copy(peers[d], d).wait_recv()

        @pl.when(half == 1)
        def _():
            last_copy(patch, 0).wait_recv()
            for d in range(1, patches):
                first_copy(peers[d], d).wait_recv()

    def receive_down():
        @pl.when(jnp.logical_and(level == 0, half == 0))
        def _():
            for d in far:
                down_copy(TAIL if d else FULL, 1, peers[d], d, 0).wait_recv()
                down_copy(ENDS if d else FULL, 0, peers[d], d, 0).wait_recv()

        @pl.when(jnp.logical_and(level == 0, half == 1))
        def _():
            for d in far:
                down_copy(TAIL if d else FULL, 1, peers[d], d, 1).wait_recv()
                down_copy(FULL, 0, peers[d], d, 1).wait_recv()

    pl.semaphore_wait(barrier, 2 * patches - 1 + 2 * patches * level)

    @pl.when(level == 1)
    def _():
        fine_copy().start()

    send_down(lambda copy: copy.start())
    send_rows(lambda copy: copy.start())

    for copy in loads[n_rows:n_tiles]:
        copy.wait()
    tile_lanes = lax.broadcasted_iota(jnp.int32, (rows, LANES), 1)
    mixed = None
    for lane in (head, tail):
        e = E0[0:rows, lane]
        m = W[:, lane].astype(f32)
        km = COURANT * m
        khm = km * H[:, lane]
        p_new = m * P0[:, lane] - km * (pltpu.roll(e, LANES - 1, 1) - e)
        q_new = m * Q0[8:8 + rows, lane] - km * (E0[1:rows + 1, lane] - e)
        qb[8:8 + rows, :] = q_new
        across = q_new - qb[7:7 + rows, :]
        if lane == head:
            parts = ((e, 0), (m * e - khm * (p_new + across), 0), (khm, 0))
        else:
            parts = ((m * P0[:, lane] + km * e, LANES - 1),
                     (m * e - khm * (across - pltpu.roll(p_new, 1, 1)), LANES - 1),
                     (khm, LANES - 1), (e, LANES - 1), (km, LANES - 2))
        for n, (x, at) in enumerate(parts):
            to = n + (0 if lane == head else 3)
            moved = pltpu.roll(x, (to - at) % LANES, 1) if (to - at) % LANES else x
            mixed = moved if mixed is None else jnp.where(tile_lanes == to, moved, mixed)
    scol[...] = jnp.transpose(mixed[:, 0:8])
    send_columns(lambda copy: copy.start())

    for copy in loads[n_tiles:]:
        copy.wait()
    for r in range(0, rows, BLOCK):
        step_rows(r, E0, P0, Q0, H, W, None, E1, P1, Q1)
    for r in range(0, end, BLOCK):
        step_rows(r, E1, P1, Q1, H, W, None, E2, P2, Q2)

    north, south = adj[0, patch, 0], adj[0, patch, 1]
    west, east = adj[0, patch, 2], adj[0, patch, 3]
    south_ok = jnp.logical_or(half == 0, south >= 0)
    north_ok = jnp.logical_or(half == 1, north >= 0)
    south_at = jnp.where(half == 0, patch, jnp.maximum(south, 0))
    north_at = jnp.where(half == 1, patch, jnp.maximum(north, 0))
    west_ok, east_ok = west >= 0, east >= 0
    west_at, east_at = jnp.maximum(west, 0), jnp.maximum(east, 0)

    def beyond(at, ok, side):
        to = adj[0, at, side]
        return jnp.maximum(to, 0), jnp.logical_and(ok, to >= 0)

    nw_at, nw_ok = beyond(north_at, north_ok, 2)
    ne_at, ne_ok = beyond(north_at, north_ok, 3)
    sw_at, sw_ok = beyond(south_at, south_ok, 2)
    se_at, se_ok = beyond(south_at, south_ok, 3)

    def kept(ok, x):
        return jnp.where(ok, x, 0.0)

    receive_columns()
    col_w, col_e = kept(west_ok, rcol[west_at]), kept(east_ok, rcol[east_at])
    khm_w, khm_e = col_w[5:6, :], col_e[2:3, :]
    m_w, m_e = (khm_w > 0.0).astype(f32), (khm_e > 0.0).astype(f32)
    km_w, km_e = COURANT * m_w, COURANT * m_e
    for n, v in enumerate((col_e[0:1, :], col_w[3:4, :], km_w, col_w[4:5, :], khm_w, col_e[1:2, :], khm_e)):
        tmp[n:n + 1, :] = v
    tmp[7:8, :] = jnp.zeros((1, LANES), f32)
    halo = jnp.transpose(tmp[...])

    def next_halo(at, halo, e, p):
        p_edge = halo[:, 1:2] - halo[:, 2:3] * e[:, 0:1]
        halo_out[at, 0:1] = halo[:, 5:6] + halo[:, 6:7] * p[:, LANES - 1:LANES]
        halo_out[at, 1:2] = p_edge + halo[:, 2:3] * (halo[:, 3:4] - halo[:, 4:5] * p_edge)
        halo_out[at, 2:3] = halo[:, 2:3]

    e_head = E0[0:rows, head]
    wet_head = W[:, head].astype(f32)
    p_edge = halo[:, 1:2] - halo[:, 2:3] * e_head[:, 0:1]
    across = Q1[8:8 + rows, head] - Q1[7:7 + rows, head]
    fixed = wet_head * (e_head - COURANT * H[:, head] * ((P1[:, head] - p_edge) + across))
    E1[0:rows, head] = jnp.where(tile_lanes == 0, fixed, E1[0:rows, head])
    e = E0[0:rows, tail]
    wet_tail = W[:, tail].astype(f32)
    p = wet_tail * (P0[:, tail] - COURANT * (halo[:, 0:1] - e))
    p = jnp.where(tile_lanes == LANES - 1, p, P1[:, tail])
    P1[:, tail] = p
    across = Q1[8:8 + rows, tail] - Q1[7:7 + rows, tail]
    fixed = wet_tail * (e - COURANT * H[:, tail] * ((p - pltpu.roll(p, 1, 1)) + across))
    E1[0:rows, tail] = jnp.where(tile_lanes == LANES - 1, fixed, E1[0:rows, tail])
    next_halo(slice(0, rows), halo, e_head, p)
    edge = halo_out[...]
    for lane in (head, tail):
        e = E1[0:rows, lane]
        wet = wet_head if lane == head else wet_tail
        q = wet * (Q1[8:8 + rows, lane] - COURANT * (E1[1:rows + 1, lane] - e))
        Q2[8:8 + rows, lane] = q
        across = q - Q2[7:7 + rows, lane]
        e_east = pltpu.roll(e, LANES - 1, 1)
        if lane == tail:
            e_east = jnp.where(tile_lanes == LANES - 1, edge[:, 0:1], e_east)
        p = wet * (P1[:, lane] - COURANT * (e_east - e))
        p_west = pltpu.roll(p, 1, 1)
        if lane == head:
            p = jnp.where(tile_lanes == LANES - 1, P2[:, lane], p)
            p_west = jnp.where(tile_lanes == 0, edge[:, 1:2] - edge[:, 2:3] * e[:, 0:1], p_west)
        eta = wet * (e - COURANT * H[:, lane] * ((p - p_west) + across))
        E2[0:rows, lane] = jnp.where(tile_lanes == (LANES - 1 if lane == head else 0),
                                     E2[0:rows, lane], eta)
        P2[:, lane] = p

    receive_rows()

    @pl.when(level == 1)
    def _():
        flow[...] = jnp.zeros(flow.shape, f32)
        corner[...] = jnp.zeros(corner.shape, f32)

    @pl.when(level == 0)
    def _():
        fine_copy().wait_recv()
        receive_down()
        ends = slice(*ENDS)

        def above(at, own):
            to = fine[0, at, 0]
            return jnp.where(own, at, jnp.maximum(to, 0)), jnp.logical_or(own, to >= 0)

        def marked(h, at, ok):
            wet = jnp.logical_and(rdown[h, at, 48:56, :] > 0.0, ok)
            return jnp.where(wet, rdown[h, at, 40:48, :], DRY)

        def terms(h, at, x):
            to_w, to_e = fine[0, at, 2], fine[0, at, 3]
            w = kept(to_w >= 0, rdown[h, jnp.maximum(to_w, 0), ends, :])
            e = kept(to_e >= 0, rdown[h, jnp.maximum(to_e, 0), ends, :])
            p_edge = w[1:2, 5:6] + w[1:2, 6:7] * (w[1:2, 4:5] - x[0:1, 4:5])
            return p_edge, COURANT * e[0:1, 4:5]

        strips = ((half, patch, other, above(patch, half == 1)),
                  (other, south_at, half, above(south_at, half == 0)))
        for n, (h, at, up, (up_at, up_ok)) in enumerate(strips):
            first_term, last_term = terms(h, at, rdown[h, at, ends, :])
            index = rdown[h, at, 32:40, :].astype(jnp.int32)
            got = gather(marked(up, up_at, up_ok), index)
            wet = got < 0.5 * DRY
            above_row = jnp.where(wet, got, 0.0)
            above_row += jnp.where(index == 0, first_term, 0.0)
            above_row += jnp.where(index == last, last_term, 0.0)
            flow[2 * n] = rdown[h, at, 0:8, :]
            flow[2 * n + 1] = (rdown[h, at, 8:16, :] + rdown[h, at, 16:24, :] * above_row
                               - jnp.where(wet, rdown[h, at, 24:32, :], 0.0))

        for n, at, r in ((0, west_at, 1), (1, east_at, 0)):
            x = rdown[half, at, ends, :]
            first_term, last_term = terms(half, at, x)
            up_at, up_ok = above(at, half == 1)
            one = slice(r, r + 1)
            index = x[one, 12:13]
            got = jnp.where(cell_ids.astype(f32) == index, marked(other, up_at, up_ok), 0.0)
            got = jnp.sum(jnp.sum(got, axis=0, keepdims=True), axis=1, keepdims=True)
            wet = got < 0.5 * DRY
            value = jnp.where(wet, got, 0.0)
            value += jnp.where(index == 0.0, first_term, 0.0)
            value += jnp.where(index == float(last), last_term, 0.0)
            second = x[one, 9:10] + x[one, 10:11] * value - jnp.where(wet, x[one, 11:12], 0.0)
            for k, v in enumerate((x[one, 7:8], x[one, 8:9], second)):
                corner[3 * n + k:3 * n + k + 1, :] = jnp.broadcast_to(v, (1, LANES))
        corner[6:7, :] = jnp.broadcast_to(rdown[other, sw_at, 57:58, 7:8], (1, LANES))
        corner[7:8, :] = jnp.broadcast_to(rdown[other, se_at, 56:57, 7:8], (1, LANES))

    @pl.when(half == 0)
    def _():
        stack[1:2, :] = rlast[nw_at, 25:26, :]
        stack[2:3, :] = rlast[ne_at, 24:25, :]
        stack[3:4, :] = rlast[sw_at, 25:26, :]
        stack[4:5, :] = rlast[se_at, 24:25, :]

    @pl.when(half == 1)
    def _():
        stack[1:2, :] = rfirst[nw_at, 25:26, :]
        stack[2:3, :] = rfirst[ne_at, 24:25, :]
        stack[3:4, :] = rfirst[sw_at, 25:26, :]
        stack[4:5, :] = rfirst[se_at, 24:25, :]

    n_ends = kept(north_ok, rlast[north_at, 24:25, :])
    nw_ends, ne_ends = kept(nw_ok, stack[1:2, :]), kept(ne_ok, stack[2:3, :])
    sw_ends, se_ends = kept(sw_ok, stack[3:4, :]), kept(se_ok, stack[4:5, :])
    sw_eta = sw_ends[:, 4:5] + kept(sw_ok, corner[6:7, 0:1])
    se_eta = se_ends[:, 4:5] + kept(se_ok, corner[7:8, 0:1])

    e_below = kept(south_ok, rfirst[south_at, 0:8, :] + flow[2])
    khm = kept(south_ok, rfirst[south_at, 16:24, :])
    m = (khm > 0.0).astype(f32)
    km = COURANT * m
    push = km * (e_below - east_of(e_below, se_eta))
    p_out = sw_ends[:, 5:6] + sw_ends[:, 6:7] * (sw_eta - e_below[0:1, 0:1])
    flat = rfirst[south_at, 8:16, :] + push - west_of(push, p_out) + km * e_below
    below = kept(south_ok, m * e_below - khm * kept(south_ok, flat) + flow[3])
    e_here = e_first + flow[0]
    khm_n = kept(north_ok, rlast[north_at, 16:24, :])
    km_n = COURANT * (khm_n > 0.0).astype(f32)
    q_n = kept(north_ok, rlast[north_at, 8:16, :]) - km_n * e_here
    p_out = nw_ends[:, 3:4] - nw_ends[:, 2:3] * n_ends[:, 0:1]
    side = jnp.where(cell_ids == 0, p_out, 0.0)
    side += jnp.where(cell_ids == last, COURANT * ne_ends[:, 0:1], 0.0)
    e_n = kept(north_ok, rlast[north_at, 0:8, :]) - khm_n * (q_n - side)
    for n, x in enumerate((q_n + km_n * e_n, km_n, below, khm, flow[1])):
        line[n] = x
    line[5] = e_below
    line[6] = q_n
    for c in range(chunks):
        lane = slice(c * LANES, (c + 1) * LANES)
        E0[0:1, lane] += flow[0, c:c + 1, :]
        E0[rows:rows + 1, lane] = line[5, c:c + 1, :]
        Q1[7:8, lane] = line[6, c:c + 1, :]

    first_row, second_row, last_row = row_lane == 0, row_lane == 1, row_lane == rows - 1
    in1 = kept(west_ok, corner[0:1, :])
    in2 = kept(west_ok, corner[1:2, :])
    q_nw = nw_ends[:, 1:2] - nw_ends[:, 2:3] * (col_w[6:7, :] + in1)
    tip = m_w * in1 - khm_w * (col_w[7:8, :] * (in1 - in2) + km_w * in1 - q_nw)
    w_share = col_w[3:4, :] + jnp.where(first_row, km_w * in1, 0.0)
    w_eta = col_w[4:5, :] + jnp.where(first_row, tip + kept(west_ok, corner[2:3, :]), 0.0)
    w_eta += jnp.where(last_row, khm_w * km_w * sw_eta, 0.0)
    w_eta += jnp.where(second_row, khm_w * km_w[:, 0:1] * in1, 0.0)
    in1 = kept(east_ok, corner[3:4, :])
    in2 = kept(east_ok, corner[4:5, :])
    q_ne = ne_ends[:, 1:2] - ne_ends[:, 2:3] * (col_e[0:1, :] + in1)
    tip = m_e * in1 + khm_e * (km_e * (in2 - in1) - km_e * in1 + q_ne)
    x_eta = col_e[0:1, :] + jnp.where(first_row, in1, 0.0)
    x_next = col_e[1:2, :] + jnp.where(first_row, tip + kept(east_ok, corner[5:6, :]), 0.0)
    x_next += jnp.where(last_row, khm_e * km_e * se_eta, 0.0)
    x_next += jnp.where(second_row, khm_e * km_e[:, 0:1] * in1, 0.0)
    for n, v in ((0, x_eta), (1, w_share), (3, w_eta), (5, x_next)):
        tmp[n:n + 1, :] = v
    halo = jnp.transpose(tmp[...])
    for r in (0, end):
        at = slice(r, r + BLOCK)
        step_rows(r, E0, P0, Q0, H, W, halo, E1, P1, Q1)
        next_halo(at, halo[at, :], E0[at, head], P1[at, tail])
    for c in range(chunks):
        lane = slice(c * LANES, (c + 1) * LANES)
        e1 = E1[0:1, lane] + line[4, c:c + 1, :]
        E1[0:1, lane] = e1
        E1[rows:rows + 1, lane] = line[2, c:c + 1, :] + line[3, c:c + 1, :] * Q1[rows + 7:rows + 8, lane]
        Q2[7:8, lane] = line[0, c:c + 1, :] - line[1, c:c + 1, :] * e1
    send_columns(lambda copy: copy.wait_send())
    send_rows(lambda copy: copy.wait_send())
    send_down(lambda copy: copy.wait_send())

    @pl.when(level == 1)
    def _():
        fine_copy().wait_send()


def two_level(mesh, adjoint_height, adjoint_momenta, depth, wet_mask, adjacency, nest_gain, nest_index):
    patches = mesh.shape["patch"]
    rows, cols = adjoint_height.shape[1:]
    chunks = cols // LANES
    f32 = jnp.float32
    anywhere = pl.BlockSpec(memory_space=pl.ANY)
    v = pltpu.VMEM
    dma = pltpu.SemaphoreType.DMA
    whole = (v((rows + 8, cols), f32), v((rows, cols), f32), v((rows + 8, cols), f32))
    scratch = [
        pltpu.SMEM(adjacency.shape, jnp.int32), pltpu.SMEM(adjacency.shape, jnp.int32),
        *whole,
        v(nest_gain.shape, f32), v(nest_index.shape, jnp.int32),
        v((16, chunks, LANES), f32), v((16, LANES), f32), v((rows + 8, LANES), f32),
        v((32, LANES), f32), v((32, LANES), f32), v((64, LANES), f32), v((8, LANES), f32),
        v((4, chunks, LANES), f32), v((8, LANES), f32), v((8, LANES), f32),
        dma((28,)), dma((5, patches)), dma((3, patches)), dma((2, patches)), dma((2,)),
        v((patches, 32, LANES), f32), v((patches, 32, LANES), f32), v((patches, 8, LANES), f32),
        v((2, patches, 64, LANES), f32),
    ]
    here = pl.BlockSpec(memory_space=pltpu.VMEM)
    state = pl.pallas_call(
        functools.partial(swap, patches, rows, cols),
        out_shape=(*whole, v((rows, cols), f32), v((rows, cols), jnp.int32), v((rows, 8), f32), *whole),
        in_specs=[anywhere] * 7,
        out_specs=(here,) * 9,
        scratch_shapes=scratch,
        compiler_params=pltpu.CompilerParams(collective_id=0, has_side_effects=True,
                                             vmem_limit_bytes=14 << 20),
    )(*[pltpu.with_memory_space_constraint(x, pltpu.HBM) for x in (
        adjacency, adjoint_height, adjoint_momenta, depth, wet_mask, nest_gain, nest_index)])
    state = [pltpu.with_memory_space_constraint(x, pltpu.VMEM) for x in state]
    return pl.pallas_call(
        functools.partial(settle, rows),
        out_shape=(jax.ShapeDtypeStruct(adjoint_height.shape, f32),
                   jax.ShapeDtypeStruct(adjoint_momenta.shape, f32)),
        in_specs=[here] * 9,
        out_specs=(anywhere, anywhere),
        scratch_shapes=[*whole, dma((9,))],
        compiler_params=pltpu.CompilerParams(vmem_limit_bytes=12 << 20),
    )(*state)


def solution(mesh):
    in_specs = (
        P(("parts", "level"), ("patch", "sub"), None),
        P(None, ("parts", "level"), ("patch", "sub"), None),
        P("level", ("patch", "sub"), None),
        P("level", ("patch", "sub"), None),
        P("level", None, None),
        P(None, ("patch", "sub")),
        P(None, ("patch", "sub")),
    )
    out_specs = (
        P(("parts", "level"), ("patch", "sub"), None),
        P(None, ("parts", "level"), ("patch", "sub"), None),
    )
    run = two_level if mesh.shape["level"] == 2 else body
    return jax.shard_map(functools.partial(run, mesh), mesh=mesh, in_specs=in_specs,
                         out_specs=out_specs, check_vma=False)
```

```python
import functools

import jax
import jax.numpy as jnp
from jax import lax
from jax.experimental import pallas as pl
from jax.experimental.pallas import tpu as pltpu
from jax.sharding import PartitionSpec as P

STEPS = 2
COURANT = 0.45
LANES = 128
BLOCK = 8


def advance(r, E, Pm, Q, H, W, halo, E_to, P_to, Q_to):
    cols = Pm.shape[1]
    lane_ids = lax.broadcasted_iota(jnp.int32, (BLOCK, cols), 1)
    span = slice(r, r + BLOCK)
    e = E[span, :]
    wet = W[span, :].astype(jnp.float32)
    e_south = E[r + 1:r + 1 + BLOCK, :]
    e_east = pltpu.roll(e, cols - 1, 1)
    if halo is not None:
        e_east = jnp.where(lane_ids == cols - 1, halo[span, 0:1], e_east)
    p = wet * (Pm[span, :] - COURANT * (e_east - e))
    q = wet * (Q[8 + r:16 + r, :] - COURANT * (e_south - e))
    p_west = pltpu.roll(p, 1, 1)
    if halo is not None:
        p_edge = halo[span, 1:2] - COURANT * halo[span, 2:3] * e[:, 0:1]
        p_west = jnp.where(lane_ids == 0, p_edge, p_west)
    P_to[span, :] = p
    Q_to[8 + r:16 + r, :] = q
    q_north = Q_to[7 + r:15 + r, :]
    E_to[span, :] = wet * (e - COURANT * H[span, :] * ((p - p_west) + (q - q_north)))


def finish(rows, E, Pm, Q, H, W, halo, E2, P2, Q2, eta_out, mom_out, Ef, Pf, Qf, sems):
    cols = Pm.shape[1]
    end = rows - BLOCK
    mid = slice(BLOCK, end)
    head, tail = slice(0, LANES), slice(cols - LANES, cols)
    before, inner = slice(0, cols - LANES), slice(LANES, cols - LANES)
    stores = []

    def store(src, dst):
        copy = pltpu.make_async_copy(src, dst, sems.at[len(stores)])
        copy.start()
        stores.append(copy)

    eta_to, row_to, col_to = eta_out.at[0], mom_out.at[0, 0], mom_out.at[1, 0]
    store(Q2.at[BLOCK + 8:end + 8], col_to.at[mid])
    store(P2.at[mid, before], row_to.at[mid, before])
    store(E2.at[mid, inner], eta_to.at[mid, inner])
    edges = halo[...]
    lane_ids = lax.broadcasted_iota(jnp.int32, (end - BLOCK, LANES), 1)

    across = Q2[BLOCK + 8:end + 8, head] - Q2[BLOCK + 7:end + 7, head]
    e = E[mid, head]
    wet = W[mid, head].astype(jnp.float32)
    p_edge = edges[mid, 1:2] - COURANT * edges[mid, 2:3] * e[:, 0:1]
    fixed = wet * (e - COURANT * H[mid, head] * ((P2[mid, head] - p_edge) + across))
    Ef[mid, head] = jnp.where(lane_ids == 0, fixed, E2[mid, head])
    store(Ef.at[mid, head], eta_to.at[mid, head])

    across = Q2[BLOCK + 8:end + 8, tail] - Q2[BLOCK + 7:end + 7, tail]
    e = E[mid, tail]
    wet = W[mid, tail].astype(jnp.float32)
    p = wet * (Pm[mid, tail] - COURANT * (edges[mid, 0:1] - e))
    p = jnp.where(lane_ids == LANES - 1, p, P2[mid, tail])
    Pf[mid, tail] = p
    store(Pf.at[mid, tail], row_to.at[mid, tail])
    fixed = wet * (e - COURANT * H[mid, tail] * ((p - pltpu.roll(p, 1, 1)) + across))
    Ef[mid, tail] = jnp.where(lane_ids == LANES - 1, fixed, E2[mid, tail])
    store(Ef.at[mid, tail], eta_to.at[mid, tail])

    for r in (0, end):
        Qf[7 + r:8 + r, :] = (Q if r == 0 else Q2)[7 + r:8 + r, :]
        advance(r, E, Pm, Q, H, W, edges, Ef, Pf, Qf)
        at = slice(r, r + BLOCK)
        store(Pf.at[at], row_to.at[at])
        store(Qf.at[8 + r:16 + r], col_to.at[at])
        store(Ef.at[at], eta_to.at[at])
    for copy in stores:
        copy.wait()


def exchange(patches, levels, rows, cols,
             adj_hbm, eta_hbm, mom_hbm, depth_hbm, wet_hbm, gain_hbm, table_hbm,
             E1, P1, Q1, H, W, halo_out, E2, P2, Q2,
             adj, E0, P0, Q0, gain_v, table_v, f8, idx8, gain8, tmp,
             sfirst, slast, scol, sinf, sew,
             rown, in_sems, send_sems, recv_sems, own_sems, *landing):
    rfirst, rlast, rcol, rnbr, rew = (landing[n * STEPS:(n + 1) * STEPS] for n in range(5))
    fields = ((E0, P0, Q0), (E1, P1, Q1))
    patch = lax.axis_index("patch")
    level = lax.axis_index("level")
    half = lax.axis_index("sub")
    chunks = cols // LANES
    other = 1 - half

    loads = [
        pltpu.make_async_copy(eta_hbm.at[0], E0.at[0:rows], in_sems.at[0]),
        pltpu.make_async_copy(mom_hbm.at[0, 0], P0, in_sems.at[1]),
        pltpu.make_async_copy(mom_hbm.at[1, 0], Q0.at[8:8 + rows], in_sems.at[2]),
        pltpu.make_async_copy(wet_hbm.at[0], W, in_sems.at[3]),
        pltpu.make_async_copy(table_hbm, table_v, in_sems.at[4]),
        pltpu.make_async_copy(gain_hbm, gain_v, in_sems.at[5]),
        pltpu.make_async_copy(adj_hbm, adj, in_sems.at[6]),
        pltpu.make_async_copy(depth_hbm.at[0], H, in_sems.at[7]),
    ]
    barrier = pltpu.get_barrier_semaphore()

    peers = [patch] + [lax.rem(patch + d, patches) for d in range(1, patches)]

    def greet(d, h, lev):
        pl.semaphore_signal(barrier, inc=1, device_id={
            "patch": peers[d], "sub": h, "level": lev},
            device_id_type=pl.DeviceIdType.MESH)

    for d in range(patches - 1, -1, -1):
        greet(d, other, level)
        if d:
            greet(d, half, level)

    @pl.when(level > 0)
    def _():
        for d in range(patches):
            greet(d, half, level - 1)
            greet(d, other, level - 1)

    @pl.when(level < levels - 1)
    def _():
        for d in range(patches):
            greet(d, half, level + 1)
            greet(d, other, level + 1)

    for load in loads:
        load.start()

    for load in loads[:7]:
        load.wait()

    lower = jnp.maximum(level - 1, 0)
    for c in range(chunks):
        lane = slice(c * LANES, (c + 1) * LANES)
        index, gain = table_v[0:1, lane], gain_v[0:1, lane]
        for lev in range(1, levels - 1):
            index = jnp.where(lower == lev, table_v[lev:lev + 1, lane], index)
            gain = jnp.where(lower == lev, gain_v[lev:lev + 1, lane], gain)
        idx8[c:c + 1, :] = index
        gain8[c:c + 1, :] = gain

    def remote(t, kind, src, buf, slot, d, h, lev):
        return pltpu.make_async_remote_copy(
            src_ref=src, dst_ref=buf, send_sem=send_sems.at[t, kind, d],
            recv_sem=recv_sems.at[t, kind, slot],
            device_id={"patch": peers[d], "sub": h, "level": lev},
            device_id_type=pl.DeviceIdType.MESH)

    def last_part(t):
        return slice(0, 2) if t == 0 else slice(t + 1, t + 2)

    def column_copy(t, slot, d):
        return remote(t, 0, scol.at[t, 0:3], rcol[t].at[slot, 0:3], slot, d, half, level)

    def first_copy(t, slot, d):
        return remote(t, 1, sfirst.at[t], rfirst[t].at[slot], slot, d, other, level)

    def last_copy(t, slot, d):
        part = last_part(t)
        return remote(t, 2, slast.at[part], rlast[t].at[slot], slot, d, other, level)

    def beside_copy(t, slot, d):
        return remote(t, 3, sinf.at[t], rnbr[t].at[slot], slot, d, other, lower)

    def ends_copy(t, slot, d):
        return remote(t, 4, sew.at[t], rew[t].at[slot], slot, d, half, lower)

    def per_half(across, inside, act):
        @pl.when(half == across)
        def _():
            for d in range(1, patches):
                act(d)

        @pl.when(half == inside)
        def _():
            act(0)

    def own_copy(t):
        return pltpu.make_async_remote_copy(
            src_ref=sinf.at[t], dst_ref=rown.at[t], send_sem=own_sems.at[t, 0],
            recv_sem=own_sems.at[t, 1], device_id={"level": lower},
            device_id_type=pl.DeviceIdType.MESH)

    def make_inflow(t):
        E = fields[t][0]
        for c in range(chunks):
            f8[c:c + 1, :] = E[0:1, c * LANES:(c + 1) * LANES]
        index = idx8[...]
        inside = jnp.bitwise_and(index, LANES - 1)
        which = lax.shift_right_logical(index, 7)
        picked = jnp.zeros((chunks, LANES), jnp.float32)
        for c in range(chunks):
            source = jnp.broadcast_to(f8[c:c + 1, :], (chunks, LANES))
            got = jnp.take_along_axis(source, inside, axis=1, mode="promise_in_bounds")
            picked = jnp.where(which == c, got, picked)
        inflow = gain8[...] * picked
        sinf[t] = inflow
        sew[t, 0:1, :] = inflow[0:1, :]
        sew[t, 1:2, :] = pltpu.roll(inflow[chunks - 1:chunks, :], 1, 1)

    def send_inflow(t):
        own_copy(t).start()
        per_half(0, 1, lambda d: beside_copy(t, patch, d).start())
        for d in range(1, patches):
            ends_copy(t, patch, d).start()

    def inflow_waits(t):
        per_half(1, 0, lambda d: beside_copy(t, peers[d], d).wait_recv())
        for d in range(1, patches):
            ends_copy(t, peers[d], d).wait_recv()

    def inflow_send_waits(t):
        own_copy(t).wait_send()
        per_half(0, 1, lambda d: beside_copy(t, patch, d).wait_send())
        for d in range(1, patches):
            ends_copy(t, patch, d).wait_send()

    def send_halos(t, act):
        send_rows(t, act)
        send_columns(t, act)

    def send_columns(t, act):
        for d in range(1, patches):
            act(column_copy(t, patch, d))

    def send_rows(t, act):
        @pl.when(half == 0)
        def _():
            for d in range(1, patches):
                act(first_copy(t, patch, d))
            act(last_copy(t, patch, 0))

        @pl.when(half == 1)
        def _():
            for d in range(1, patches):
                act(last_copy(t, patch, d))
            act(first_copy(t, patch, 0))

    def receive_halos(t):
        @pl.when(half == 0)
        def _():
            first_copy(t, peers[0], 0).wait_recv()
            for d in range(1, patches):
                last_copy(t, peers[d], d).wait_recv()

        @pl.when(half == 1)
        def _():
            last_copy(t, peers[0], 0).wait_recv()
            for d in range(1, patches):
                first_copy(t, peers[d], d).wait_recv()

        for d in range(1, patches):
            column_copy(t, peers[d], d).wait_recv()

    north = adj[0, patch, 0]
    south = adj[0, patch, 1]
    west = adj[0, patch, 2]
    east = adj[0, patch, 3]
    south_ok = jnp.logical_or(half == 0, south >= 0)
    north_ok = jnp.logical_or(half == 1, north >= 0)
    south_at = jnp.where(half == 0, patch, jnp.maximum(south, 0))
    north_at = jnp.where(half == 1, patch, jnp.maximum(north, 0))
    west_at = jnp.maximum(west, 0)
    east_at = jnp.maximum(east, 0)
    finer = level < levels - 1
    lane_ids = lax.broadcasted_iota(jnp.int32, (rows, LANES), 1)
    first_lane = lax.broadcasted_iota(jnp.int32, (1, LANES), 1) == 0
    tail = slice(cols - LANES, cols)
    end = rows - 1

    def make_messages(t):
        @pl.when(level == levels - 1)
        def _():
            make_inflow(t)

        make_rows(t)
        make_columns(t)

    def make_rows(t):
        E, Pm, Q = fields[t]
        sfirst[t] = E[0:1, :]
        wet_row = W[end:rows, :].astype(jnp.float32)
        slast[t + 1] = wet_row * (Q[8 + end:8 + rows, :] + COURANT * E[end:rows, :])
        if t == 0:
            slast[0] = wet_row

    def make_columns(t):
        E, Pm, Q = fields[t]
        wet_tail = W[:, tail].astype(jnp.float32)
        share = wet_tail * (Pm[:, tail] + COURANT * E[0:rows, tail])
        mixed = jnp.where(lane_ids == 0, E[0:rows, 0:LANES],
                          jnp.where(lane_ids == 1, pltpu.roll(share, 2, 1),
                                    pltpu.roll(wet_tail, 3, 1)))
        scol[t] = jnp.transpose(mixed[:, 0:8])

    def send_messages(t):
        @pl.when(level == levels - 1)
        def _():
            send_inflow(t)

        send_halos(t, lambda copy: copy.start())

    def receive(t):
        E, Pm, Q = fields[t]

        @pl.when(finer)
        def _():
            own_copy(t).wait_recv()
            for c in range(chunks):
                lane = slice(c * LANES, (c + 1) * LANES)
                E[0:1, lane] += rown[t, c:c + 1, :]

        if levels > 2:
            @pl.when(jnp.logical_and(level > 0, level < levels - 1))
            def _():
                make_inflow(t)
                send_inflow(t)

        receive_halos(t)

        @pl.when(finer)
        def _():
            inflow_waits(t)

        east_row = rcol[t][east_at][0:1, :]
        east_row += jnp.where(jnp.logical_and(first_lane, finer), rew[t][east_at][0:1, :], 0.0)
        west_cols = rcol[t][west_at]
        share = west_cols[1:2, :]
        wet_w = west_cols[2:3, :]
        share += jnp.where(jnp.logical_and(first_lane, finer),
                           COURANT * wet_w * rew[t][west_at][1:2, :], 0.0)
        tmp[0:1, :] = jnp.where(east >= 0, east_row, 0.0)
        tmp[1:2, :] = jnp.where(west >= 0, share, 0.0)
        tmp[2:3, :] = jnp.where(west >= 0, wet_w, 0.0)
        beside = rnbr[t][south_at]
        below = rfirst[t][south_at]
        for c in range(chunks):
            lane = slice(c * LANES, (c + 1) * LANES)
            value = below[:, lane] + jnp.where(finer, beside[c:c + 1, :], 0.0)
            E[rows:rows + 1, lane] = jnp.where(south_ok, value, 0.0)
        share_n = rlast[t][north_at, 1 if t == 0 else 0]
        wet_n = rlast[0][north_at, 0]
        Q_to = Q1
        Q_to[7:8, :] = jnp.where(north_ok, share_n - COURANT * wet_n * E[0:1, :], 0.0)
        return jnp.transpose(tmp[...])

    make_messages(0)
    sides = (level > 0).astype(jnp.int32) + (level < levels - 1).astype(jnp.int32)
    pl.semaphore_wait(barrier, 2 * patches - 1 + 2 * patches * sides)
    send_messages(0)
    loads[7].wait()
    for r in range(0, rows - BLOCK, BLOCK):
        advance(r, E0, P0, Q0, H, W, None, E1, P1, Q1)
    halo = receive(0)
    for r in (0, rows - BLOCK):
        advance(r, E0, P0, Q0, H, W, None, E1, P1, Q1)
    head = slice(0, LANES)
    e = E0[0:rows, head]
    wet = W[:, head].astype(jnp.float32)
    p_edge = halo[:, 1:2] - COURANT * halo[:, 2:3] * e[:, 0:1]
    across = Q1[8:8 + rows, head] - Q1[7:7 + rows, head]
    fixed = wet * (e - COURANT * H[:, head] * ((P1[:, head] - p_edge) + across))
    E1[0:rows, head] = jnp.where(lane_ids == 0, fixed, E1[0:rows, head])
    e = E0[0:rows, tail]
    wet = W[:, tail].astype(jnp.float32)
    p = wet * (P0[:, tail] - COURANT * (halo[:, 0:1] - e))
    p = jnp.where(lane_ids == LANES - 1, p, P1[:, tail])
    P1[:, tail] = p
    across = Q1[8:8 + rows, tail] - Q1[7:7 + rows, tail]
    fixed = wet * (e - COURANT * H[:, tail] * ((p - pltpu.roll(p, 1, 1)) + across))
    E1[0:rows, tail] = jnp.where(lane_ids == LANES - 1, fixed, E1[0:rows, tail])

    @pl.when(level == levels - 1)
    def _():
        make_inflow(1)
        send_inflow(1)

    make_rows(1)
    send_rows(1, lambda copy: copy.start())
    make_columns(1)
    send_columns(1, lambda copy: copy.start())
    for r in range(0, rows - BLOCK, BLOCK):
        advance(r, E1, P1, Q1, H, W, None, E2, P2, Q2)
    halo_out[...] = receive(1)
    for t in range(STEPS):
        send_halos(t, lambda copy: copy.wait_send())

        @pl.when(level > 0)
        def _():
            inflow_send_waits(t)


def body(mesh, adjoint_height, adjoint_momenta, depth, wet_mask, adjacency, nest_gain, nest_index):
    patches, levels = mesh.shape["patch"], mesh.shape["level"]
    rows, cols = adjoint_height.shape[1:]
    chunks = cols // LANES
    f32 = jnp.float32
    anywhere = pl.BlockSpec(memory_space=pl.ANY)
    v = pltpu.VMEM
    dma = pltpu.SemaphoreType.DMA
    whole = (v((rows + 8, cols), f32), v((rows, cols), f32), v((rows + 8, cols), f32))
    scratch = [
        pltpu.SMEM(adjacency.shape, jnp.int32),
        *whole,
        v(nest_gain.shape, f32), v(nest_index.shape, jnp.int32),
        v((chunks, LANES), f32), v((chunks, LANES), jnp.int32), v((chunks, LANES), f32),
        v((8, LANES), f32),
        v((STEPS, 1, cols), f32), v((STEPS + 1, 1, cols), f32), v((STEPS, 8, LANES), f32),
        v((STEPS, chunks, LANES), f32), v((STEPS, 2, LANES), f32),
        v((STEPS, chunks, LANES), f32),
        dma((8,)), dma((STEPS, 5, patches)), dma((STEPS, 5, patches)), dma((STEPS, 2)),
    ]
    scratch += [v((patches, 1, cols), f32)] * STEPS
    scratch += [v((patches, 2 if t == 0 else 1, 1, cols), f32) for t in range(STEPS)]
    scratch += [v((patches, 8, LANES), f32)] * STEPS
    scratch += [v((patches, chunks, LANES), f32)] * STEPS
    scratch += [v((patches, 2, LANES), f32)] * STEPS
    here = pl.BlockSpec(memory_space=pltpu.VMEM)
    state = pl.pallas_call(
        functools.partial(exchange, patches, levels, rows, cols),
        out_shape=(*whole, v((rows, cols), f32), v((rows, cols), jnp.int32), v((rows, 8), f32), *whole),
        in_specs=[anywhere] * 7,
        out_specs=(here,) * 9,
        scratch_shapes=scratch,
        compiler_params=pltpu.CompilerParams(collective_id=0, has_side_effects=True,
                                             vmem_limit_bytes=12 << 20),
    )(*[pltpu.with_memory_space_constraint(x, pltpu.HBM) for x in (
        adjacency, adjoint_height, adjoint_momenta, depth, wet_mask, nest_gain, nest_index)])
    state = [pltpu.with_memory_space_constraint(x, pltpu.VMEM) for x in state]
    return pl.pallas_call(
        functools.partial(finish, rows),
        out_shape=(jax.ShapeDtypeStruct(adjoint_height.shape, f32),
                   jax.ShapeDtypeStruct(adjoint_momenta.shape, f32)),
        in_specs=[here] * 9,
        out_specs=(anywhere, anywhere),
        scratch_shapes=[*whole, dma((12,))],
        compiler_params=pltpu.CompilerParams(vmem_limit_bytes=12 << 20),
    )(*state)


FULL, TAIL, ENDS = (0, 42), (24, 42), (40, 42)
DRY = 1e30


def step_rows(r, E, Pm, Q, H, W, edge, E_to, P_to, Q_to):
    cols = Pm.shape[1]
    lane_ids = lax.broadcasted_iota(jnp.int32, (BLOCK, cols), 1)
    span = slice(r, r + BLOCK)
    e = E[span, :]
    wet = W[span, :].astype(jnp.float32)
    e_south = E[r + 1:r + 1 + BLOCK, :]
    e_east = pltpu.roll(e, cols - 1, 1)
    if edge is not None:
        e_east = jnp.where(lane_ids == cols - 1, edge[span, 0:1], e_east)
    p = wet * (Pm[span, :] - COURANT * (e_east - e))
    q = wet * (Q[8 + r:16 + r, :] - COURANT * (e_south - e))
    p_west = pltpu.roll(p, 1, 1)
    if edge is not None:
        p_west = jnp.where(lane_ids == 0, edge[span, 1:2] - edge[span, 2:3] * e[:, 0:1], p_west)
    P_to[span, :] = p
    Q_to[8 + r:16 + r, :] = q
    q_north = Q_to[7 + r:15 + r, :]
    E_to[span, :] = wet * (e - COURANT * H[span, :] * ((p - p_west) + (q - q_north)))


def settle(rows, E, Pm, Q, H, W, halo, E2, P2, Q2, eta_out, mom_out, Ef, Pf, Qf, sems):
    end = rows - BLOCK
    mid = slice(BLOCK, end)
    stores = []

    def store(src, dst):
        copy = pltpu.make_async_copy(src, dst, sems.at[len(stores)])
        copy.start()
        stores.append(copy)

    eta_to, row_to, col_to = eta_out.at[0], mom_out.at[0, 0], mom_out.at[1, 0]
    store(Q2.at[BLOCK + 8:end + 8], col_to.at[mid])
    store(P2.at[mid], row_to.at[mid])
    store(E2.at[mid], eta_to.at[mid])
    edge = halo[...]

    def ends(r):
        step_rows(r, E, Pm, Q, H, W, edge, Ef, Pf, Qf)
        at = slice(r, r + BLOCK)
        store(Pf.at[at], row_to.at[at])
        store(Qf.at[8 + r:16 + r], col_to.at[at])
        store(Ef.at[at], eta_to.at[at])

    for r in (0, end):
        Qf[7 + r:8 + r, :] = Q2[7 + r:8 + r, :]
        ends(r)
    for copy in stores:
        copy.wait()


def swap(patches, rows, cols,
         adj_hbm, eta_hbm, mom_hbm, depth_hbm, wet_hbm, gain_hbm, table_hbm,
         E1, P1, Q1, H, W, halo_out, E2, P2, Q2,
         adj, fine, E0, P0, Q0, gain_v, table_v, line, stack, qb, sfirst, slast, sdown, scol,
         flow, corner, tmp, in_sems, send_sems, recv_sems, down_sems, fine_sems,
         rfirst, rlast, rcol, rdown):
    f32 = jnp.float32
    patch = lax.axis_index("patch")
    level = lax.axis_index("level")
    half = lax.axis_index("sub")
    other = 1 - half
    chunks = cols // LANES
    last = cols - 1
    end = rows - BLOCK
    head, tail = slice(0, LANES), slice(cols - LANES, cols)
    inner = slice(LANES, cols - LANES)
    mid = slice(BLOCK, end)
    loads = []

    def load(src, dst):
        copy = pltpu.make_async_copy(src, dst, in_sems.at[len(loads)])
        copy.start()
        loads.append(copy)

    fields = ((eta_hbm.at[0], E0, 0), (mom_hbm.at[0, 0], P0, 0), (mom_hbm.at[1, 0], Q0, 8),
              (wet_hbm.at[0], W, 0), (depth_hbm.at[0], H, 0))

    def load_part(at, lane):
        for src, dst, shift in fields:
            load(src.at[at, lane], dst.at[at.start + shift:at.stop + shift, lane])

    for at in (slice(0, BLOCK), slice(end, rows)):
        load_part(at, slice(0, cols))
    load(adj_hbm, adj)
    load(table_hbm, table_v)
    load(gain_hbm, gain_v)
    n_rows = len(loads)

    barrier = pltpu.get_barrier_semaphore()
    peers = [patch] + [jnp.where(patch < d, d, d - 1) for d in range(1, patches)]

    def greet(d, h, lev):
        pl.semaphore_signal(barrier, inc=1, device_id={
            "patch": peers[d], "sub": h, "level": lev},
            device_id_type=pl.DeviceIdType.MESH)

    for d in range(1, patches):
        greet(d, other, level)
        greet(d, half, level)
    greet(0, other, level)

    @pl.when(level == 0)
    def _():
        for d in list(range(1, patches)) + [0]:
            greet(d, half, 1)
            greet(d, other, 1)

    for lane in (head, tail):
        load_part(mid, lane)
    n_tiles = len(loads)
    load_part(mid, inner)

    E0[rows:rows + 8, :] = jnp.zeros((8, cols), f32)
    qb[0:8, :] = jnp.zeros((8, LANES), f32)
    lane_ids = lax.broadcasted_iota(jnp.int32, (chunks, LANES), 1)
    cell_ids = lax.broadcasted_iota(jnp.int32, (chunks, LANES), 0) * LANES + lane_ids
    row_lane = lax.broadcasted_iota(jnp.int32, (1, LANES), 1)

    def east_of(x, beyond):
        y = pltpu.roll(x, LANES - 1, 1)
        y = jnp.where(lane_ids == LANES - 1, pltpu.roll(y, chunks - 1, 0), y)
        return jnp.where(cell_ids == last, beyond, y)

    def west_of(x, beyond):
        y = pltpu.roll(x, 1, 1)
        y = jnp.where(lane_ids == 0, pltpu.roll(y, 1, 0), y)
        return jnp.where(cell_ids == 0, beyond, y)

    def gather(x, index):
        inside = jnp.bitwise_and(index, LANES - 1)
        which = lax.shift_right_logical(index, 7)
        picked = jnp.zeros((chunks, LANES), f32)
        for c in range(chunks):
            source = jnp.broadcast_to(x[c:c + 1, :], (chunks, LANES))
            got = jnp.take_along_axis(source, inside, axis=1, mode="promise_in_bounds")
            picked = jnp.where(which == c, got, picked)
        return picked

    for copy in loads[:n_rows]:
        copy.wait()

    def lines(n, ref, r):
        for c in range(chunks):
            line[n, c:c + 1, :] = ref[r:r + 1, c * LANES:(c + 1) * LANES].astype(f32)

    for n, (ref, r) in enumerate((
            (E0, 0), (E0, 1), (P0, 0), (Q0, 8), (W, 0), (H, 0),
            (E0, rows - 1), (P0, rows - 1), (Q0, rows + 7), (W, rows - 1), (H, rows - 1),
            (E0, rows - 2), (Q0, rows + 6), (W, rows - 2))):
        lines(n, ref, r)

    e, p, q, m = line[0], line[2], line[3], line[4]
    e_first = e
    km = COURANT * m
    khm = km * line[5]
    mp = m * p
    sfirst[0:8, :] = e
    sfirst[8:16, :] = mp - west_of(mp, 0.0) + (m * q - km * line[1])
    sfirst[16:24, :] = khm
    stack[4:5, :] = jnp.where(row_lane < 64, e[0:1, :], e[chunks - 1:chunks, :])
    stack[5:6, :] = jnp.where(row_lane < 64, mp[0:1, :], mp[chunks - 1:chunks, :])
    stack[6:7, :] = jnp.where(row_lane < 64, km[0:1, :], km[chunks - 1:chunks, :])
    el, ml = line[6], line[9]
    kml = COURANT * ml
    khml = kml * line[10]
    pl_new = ml * line[7] - kml * (east_of(el, 0.0) - el)
    q_above = line[13] * (line[12] - COURANT * (el - line[11]))
    aq = ml * line[8] + kml * el
    ap = ml * line[7] + kml * el
    slast[0:8, :] = ml * el - khml * (pl_new - west_of(pl_new, 0.0) - q_above)
    slast[8:16, :] = aq
    slast[16:24, :] = khml
    sdown[24:32, :] = aq
    sdown[32:40, :] = khml
    for n, x in enumerate((el, aq, kml, ap)):
        stack[n:n + 1, :] = jnp.where(row_lane < 64, x[0:1, :], x[chunks - 1:chunks, :])
    stack[13:16, :] = jnp.zeros((3, LANES), f32)

    @pl.when(level == 0)
    def _():
        stack[7:13, :] = jnp.zeros((6, LANES), f32)

    for c in range(chunks):
        lane = slice(c * LANES, (c + 1) * LANES)
        line[14, c:c + 1, :] = gain_v[0:1, lane]
        line[15, c:c + 1, :] = table_v[0:1, lane].astype(f32)
    gain, index = line[14], line[15].astype(jnp.int32)
    sfirst[32:40, :] = gain
    sfirst[40:48, :] = line[15]

    @pl.when(level == 1)
    def _():
        p_new = mp - km * (east_of(e, 0.0) - e)
        q_new = m * q - km * (line[1] - e)
        there = m * e - khm * (p_new - west_of(p_new, 0.0) + q_new)
        parts = [gather(x, index) for x in (e, there, khm)]
        for n, x in enumerate(parts):
            sdown[8 * n:8 * n + 8, :] = x
        inflow = gain * parts[0]
        rows_of = (inflow, None, gain * parts[1], gain * parts[2],
                   COURANT * parts[2] * inflow, line[15])
        for n, x in enumerate(rows_of):
            if x is None:
                low = pltpu.roll(inflow, LANES - 1, 1)[0:1, :]
                high = pltpu.roll(inflow, 1, 1)[chunks - 1:chunks, :]
            else:
                low, high = x[0:1, :], x[chunks - 1:chunks, :]
            stack[7 + n:8 + n, :] = jnp.where(row_lane < 64, low, high)

    turned = jnp.transpose(stack[...])
    for ref, at in ((sfirst, 24), (slast, 24), (sdown, 40)):
        ref[at:at + 1, 0:16] = turned[0:1, :]
        ref[at + 1:at + 2, 0:16] = turned[LANES - 1:LANES, :]

    def remote(kind, src, dst, recv_sem, d, h, lev):
        return pltpu.make_async_remote_copy(
            src_ref=src, dst_ref=dst, send_sem=send_sems.at[kind, d], recv_sem=recv_sem,
            device_id={"patch": peers[d], "sub": h, "level": lev},
            device_id_type=pl.DeviceIdType.MESH)

    def column_copy(slot, d):
        return remote(0, scol, rcol.at[slot], recv_sems.at[0, slot], d, half, level)

    def first_copy(slot, d, size):
        return remote(1, sfirst.at[0:size], rfirst.at[slot, 0:size], recv_sems.at[1, slot], d, other, level)

    def by_level(act):
        for lev, size in enumerate((48, 26)):
            @pl.when(level == lev)
            def _():
                act(size)

    def last_copy(slot, d):
        return remote(2, slast.at[0:26], rlast.at[slot, 0:26], recv_sems.at[2, slot], d, other, level)

    def down_copy(part, from_half, slot, d, h):
        at = slice(*part)
        return remote(3 + h, sdown.at[at], rdown.at[from_half, slot, at],
                      down_sems.at[from_half, slot], d, h, 1 - level)

    def fine_copy():
        return pltpu.make_async_remote_copy(
            src_ref=adj, dst_ref=fine, send_sem=fine_sems.at[0], recv_sem=fine_sems.at[1],
            device_id={"level": 1 - level}, device_id_type=pl.DeviceIdType.MESH)

    far = list(range(1, patches)) + [0]

    def send_rows(act):
        @pl.when(half == 0)
        def _():
            def firsts(size):
                for d in range(1, patches):
                    act(first_copy(patch, d, size))

            by_level(firsts)
            act(last_copy(patch, 0))

        @pl.when(half == 1)
        def _():
            for d in range(1, patches):
                act(last_copy(patch, d))
            by_level(lambda size: act(first_copy(patch, 0, size)))

    def send_down(act):
        @pl.when(jnp.logical_and(level == 1, half == 0))
        def _():
            for d in far:
                act(down_copy(FULL if d else TAIL, 0, patch, d, 1))
                act(down_copy(ENDS if d else FULL, 0, patch, d, 0))

        @pl.when(jnp.logical_and(level == 1, half == 1))
        def _():
            for d in far:
                act(down_copy(TAIL if d else FULL, 1, patch, d, 0))
                act(down_copy(TAIL if d else FULL, 1, patch, d, 1))

    def send_columns(act):
        for d in range(1, patches):
            act(column_copy(patch, d))

    def receive_columns():
        for d in range(1, patches):
            column_copy(peers[d], d).wait_recv()

    def receive_rows():
        @pl.when(half == 0)
        def _():
            by_level(lambda size: first_copy(patch, 0, size).wait_recv())
            for d in range(1, patches):
                last_copy(peers[d], d).wait_recv()

        @pl.when(half == 1)
        def _():
            def firsts(size):
                for d in range(1, patches):
                    first_copy(peers[d], d, size).wait_recv()

            last_copy(patch, 0).wait_recv()
            by_level(firsts)

    def receive_down():
        @pl.when(jnp.logical_and(level == 0, half == 0))
        def _():
            for d in far:
                down_copy(TAIL if d else FULL, 1, peers[d], d, 0).wait_recv()
                down_copy(ENDS if d else FULL, 0, peers[d], d, 0).wait_recv()

        @pl.when(jnp.logical_and(level == 0, half == 1))
        def _():
            for d in far:
                down_copy(TAIL if d else FULL, 1, peers[d], d, 1).wait_recv()
                down_copy(FULL if d else TAIL, 0, peers[d], d, 1).wait_recv()

    pl.semaphore_wait(barrier, 2 * patches - 1 + 2 * patches * level)

    @pl.when(level == 1)
    def _():
        fine_copy().start()

    send_down(lambda copy: copy.start())
    send_rows(lambda copy: copy.start())

    for copy in loads[n_rows:n_tiles]:
        copy.wait()
    tile_lanes = lax.broadcasted_iota(jnp.int32, (rows, LANES), 1)
    mixed = None
    for lane in (head, tail):
        e = E0[0:rows, lane]
        m = W[:, lane].astype(f32)
        km = COURANT * m
        khm = km * H[:, lane]
        p_new = m * P0[:, lane] - km * (pltpu.roll(e, LANES - 1, 1) - e)
        q_new = m * Q0[8:8 + rows, lane] - km * (E0[1:rows + 1, lane] - e)
        qb[8:8 + rows, :] = q_new
        across = q_new - qb[7:7 + rows, :]
        if lane == head:
            parts = ((e, 0), (m * e - khm * (p_new + across), 0), (khm, 0))
        else:
            parts = ((m * P0[:, lane] + km * e, LANES - 1),
                     (m * e - khm * (across - pltpu.roll(p_new, 1, 1)), LANES - 1),
                     (khm, LANES - 1), (e, LANES - 1), (km, LANES - 2))
        for n, (x, at) in enumerate(parts):
            to = n + (0 if lane == head else 3)
            moved = pltpu.roll(x, (to - at) % LANES, 1) if (to - at) % LANES else x
            mixed = moved if mixed is None else jnp.where(tile_lanes == to, moved, mixed)
    scol[...] = jnp.transpose(mixed[:, 0:8])
    send_columns(lambda copy: copy.start())

    for copy in loads[n_tiles:]:
        copy.wait()
    for r in range(0, rows, BLOCK):
        step_rows(r, E0, P0, Q0, H, W, None, E1, P1, Q1)
    for r in range(0, end, BLOCK):
        step_rows(r, E1, P1, Q1, H, W, None, E2, P2, Q2)

    north, south = adj[0, patch, 0], adj[0, patch, 1]
    west, east = adj[0, patch, 2], adj[0, patch, 3]
    south_ok = jnp.logical_or(half == 0, south >= 0)
    north_ok = jnp.logical_or(half == 1, north >= 0)
    south_at = jnp.where(half == 0, patch, jnp.maximum(south, 0))
    north_at = jnp.where(half == 1, patch, jnp.maximum(north, 0))
    west_ok, east_ok = west >= 0, east >= 0
    west_at, east_at = jnp.maximum(west, 0), jnp.maximum(east, 0)

    def beyond(at, ok, side):
        to = adj[0, at, side]
        return jnp.maximum(to, 0), jnp.logical_and(ok, to >= 0)

    nw_at, nw_ok = beyond(north_at, north_ok, 2)
    ne_at, ne_ok = beyond(north_at, north_ok, 3)
    sw_at, sw_ok = beyond(south_at, south_ok, 2)
    se_at, se_ok = beyond(south_at, south_ok, 3)

    def kept(ok, x):
        return jnp.where(ok, x, 0.0)

    receive_columns()
    col_w, col_e = kept(west_ok, rcol[west_at]), kept(east_ok, rcol[east_at])
    khm_w, khm_e = col_w[5:6, :], col_e[2:3, :]
    m_w, m_e = (khm_w > 0.0).astype(f32), (khm_e > 0.0).astype(f32)
    km_w, km_e = COURANT * m_w, COURANT * m_e
    for n, v in enumerate((col_e[0:1, :], col_w[3:4, :], km_w, col_w[4:5, :], khm_w, col_e[1:2, :], khm_e)):
        tmp[n:n + 1, :] = v
    tmp[7:8, :] = jnp.zeros((1, LANES), f32)
    halo = jnp.transpose(tmp[...])

    def next_halo(at, halo, e, p):
        p_edge = halo[:, 1:2] - halo[:, 2:3] * e[:, 0:1]
        halo_out[at, 0:1] = halo[:, 5:6] + halo[:, 6:7] * p[:, LANES - 1:LANES]
        halo_out[at, 1:2] = p_edge + halo[:, 2:3] * (halo[:, 3:4] - halo[:, 4:5] * p_edge)
        halo_out[at, 2:3] = halo[:, 2:3]

    e_head = E0[0:rows, head]
    wet_head = W[:, head].astype(f32)
    p_edge = halo[:, 1:2] - halo[:, 2:3] * e_head[:, 0:1]
    across = Q1[8:8 + rows, head] - Q1[7:7 + rows, head]
    fixed = wet_head * (e_head - COURANT * H[:, head] * ((P1[:, head] - p_edge) + across))
    E1[0:rows, head] = jnp.where(tile_lanes == 0, fixed, E1[0:rows, head])
    e = E0[0:rows, tail]
    wet_tail = W[:, tail].astype(f32)
    p = wet_tail * (P0[:, tail] - COURANT * (halo[:, 0:1] - e))
    p = jnp.where(tile_lanes == LANES - 1, p, P1[:, tail])
    P1[:, tail] = p
    across = Q1[8:8 + rows, tail] - Q1[7:7 + rows, tail]
    fixed = wet_tail * (e - COURANT * H[:, tail] * ((p - pltpu.roll(p, 1, 1)) + across))
    E1[0:rows, tail] = jnp.where(tile_lanes == LANES - 1, fixed, E1[0:rows, tail])
    next_halo(slice(0, rows), halo, e_head, p)
    edge = halo_out[...]
    for lane in (head, tail):
        e = E1[0:rows, lane]
        wet = wet_head if lane == head else wet_tail
        q = wet * (Q1[8:8 + rows, lane] - COURANT * (E1[1:rows + 1, lane] - e))
        Q2[8:8 + rows, lane] = q
        across = q - Q2[7:7 + rows, lane]
        e_east = pltpu.roll(e, LANES - 1, 1)
        if lane == tail:
            e_east = jnp.where(tile_lanes == LANES - 1, edge[:, 0:1], e_east)
        p = wet * (P1[:, lane] - COURANT * (e_east - e))
        p_west = pltpu.roll(p, 1, 1)
        if lane == head:
            p = jnp.where(tile_lanes == LANES - 1, P2[:, lane], p)
            p_west = jnp.where(tile_lanes == 0, edge[:, 1:2] - edge[:, 2:3] * e[:, 0:1], p_west)
        eta = wet * (e - COURANT * H[:, lane] * ((p - p_west) + across))
        E2[0:rows, lane] = jnp.where(tile_lanes == (LANES - 1 if lane == head else 0),
                                     E2[0:rows, lane], eta)
        P2[:, lane] = p

    receive_rows()

    @pl.when(level == 1)
    def _():
        flow[...] = jnp.zeros(flow.shape, f32)
        corner[...] = jnp.zeros(corner.shape, f32)

    @pl.when(level == 0)
    def _():
        fine_copy().wait_recv()
        receive_down()
        ends = slice(*ENDS)

        def above(at, own):
            to = fine[0, at, 0]
            return jnp.where(own, at, jnp.maximum(to, 0)), jnp.logical_or(own, to >= 0)

        def marked(h, at, ok):
            wet = jnp.logical_and(rdown[h, at, 32:40, :] > 0.0, ok)
            return jnp.where(wet, rdown[h, at, 24:32, :], DRY)

        def terms(h, at, x):
            to_w, to_e = fine[0, at, 2], fine[0, at, 3]
            w = kept(to_w >= 0, rdown[h, jnp.maximum(to_w, 0), ends, :])
            e = kept(to_e >= 0, rdown[h, jnp.maximum(to_e, 0), ends, :])
            p_edge = w[1:2, 5:6] + w[1:2, 6:7] * (w[1:2, 4:5] - x[0:1, 4:5])
            return p_edge, COURANT * e[0:1, 4:5]

        strips = ((half, patch, other, above(patch, half == 1), line[14], line[15]),
                  (other, south_at, half, above(south_at, half == 0),
                   rfirst[south_at, 32:40, :], rfirst[south_at, 40:48, :]))
        for n, (h, at, up, (up_at, up_ok), gain, index) in enumerate(strips):
            first_term, last_term = terms(h, at, rdown[h, at, ends, :])
            index = index.astype(jnp.int32)
            got = gather(marked(up, up_at, up_ok), index)
            eta_at = rdown[h, at, 0:8, :]
            change = jnp.where(got < 0.5 * DRY, got - COURANT * eta_at, 0.0)
            change += jnp.where(index == 0, first_term, 0.0)
            change += jnp.where(index == last, last_term, 0.0)
            flow[2 * n] = gain * eta_at
            flow[2 * n + 1] = gain * (rdown[h, at, 8:16, :] + rdown[h, at, 16:24, :] * change)

        for n, at, r in ((0, west_at, 1), (1, east_at, 0)):
            x = rdown[half, at, ends, :]
            first_term, last_term = terms(half, at, x)
            up_at, up_ok = above(at, half == 1)
            one = slice(r, r + 1)
            index = x[one, 12:13]
            got = jnp.where(cell_ids.astype(f32) == index, marked(other, up_at, up_ok), 0.0)
            got = jnp.sum(jnp.sum(got, axis=0, keepdims=True), axis=1, keepdims=True)
            wet = got < 0.5 * DRY
            value = jnp.where(wet, got, 0.0)
            value += jnp.where(index == 0.0, first_term, 0.0)
            value += jnp.where(index == float(last), last_term, 0.0)
            second = x[one, 9:10] + x[one, 10:11] * value - jnp.where(wet, x[one, 11:12], 0.0)
            for k, v in enumerate((x[one, 7:8], x[one, 8:9], second)):
                corner[3 * n + k:3 * n + k + 1, :] = jnp.broadcast_to(v, (1, LANES))
        corner[6:7, :] = jnp.broadcast_to(rdown[other, sw_at, 41:42, 7:8], (1, LANES))
        corner[7:8, :] = jnp.broadcast_to(rdown[other, se_at, 40:41, 7:8], (1, LANES))

    @pl.when(half == 0)
    def _():
        stack[1:2, :] = rlast[nw_at, 25:26, :]
        stack[2:3, :] = rlast[ne_at, 24:25, :]
        stack[3:4, :] = rlast[sw_at, 25:26, :]
        stack[4:5, :] = rlast[se_at, 24:25, :]

    @pl.when(half == 1)
    def _():
        stack[1:2, :] = rfirst[nw_at, 25:26, :]
        stack[2:3, :] = rfirst[ne_at, 24:25, :]
        stack[3:4, :] = rfirst[sw_at, 25:26, :]
        stack[4:5, :] = rfirst[se_at, 24:25, :]

    n_ends = kept(north_ok, rlast[north_at, 24:25, :])
    nw_ends, ne_ends = kept(nw_ok, stack[1:2, :]), kept(ne_ok, stack[2:3, :])
    sw_ends, se_ends = kept(sw_ok, stack[3:4, :]), kept(se_ok, stack[4:5, :])
    sw_eta = sw_ends[:, 4:5] + kept(sw_ok, corner[6:7, 0:1])
    se_eta = se_ends[:, 4:5] + kept(se_ok, corner[7:8, 0:1])

    e_below = kept(south_ok, rfirst[south_at, 0:8, :] + flow[2])
    khm = kept(south_ok, rfirst[south_at, 16:24, :])
    m = (khm > 0.0).astype(f32)
    km = COURANT * m
    push = km * (e_below - east_of(e_below, se_eta))
    p_out = sw_ends[:, 5:6] + sw_ends[:, 6:7] * (sw_eta - e_below[0:1, 0:1])
    flat = rfirst[south_at, 8:16, :] + push - west_of(push, p_out) + km * e_below
    below = kept(south_ok, m * e_below - khm * kept(south_ok, flat) + flow[3])
    e_here = e_first + flow[0]
    khm_n = kept(north_ok, rlast[north_at, 16:24, :])
    km_n = COURANT * (khm_n > 0.0).astype(f32)
    q_n = kept(north_ok, rlast[north_at, 8:16, :]) - km_n * e_here
    p_out = nw_ends[:, 3:4] - nw_ends[:, 2:3] * n_ends[:, 0:1]
    side = jnp.where(cell_ids == 0, p_out, 0.0)
    side += jnp.where(cell_ids == last, COURANT * ne_ends[:, 0:1], 0.0)
    e_n = kept(north_ok, rlast[north_at, 0:8, :]) - khm_n * (q_n - side)
    for n, x in enumerate((q_n + km_n * e_n, km_n, below, khm, flow[1])):
        line[n] = x
    line[5] = e_below
    line[6] = q_n
    for c in range(chunks):
        lane = slice(c * LANES, (c + 1) * LANES)
        E0[0:1, lane] += flow[0, c:c + 1, :]
        E0[rows:rows + 1, lane] = line[5, c:c + 1, :]
        Q1[7:8, lane] = line[6, c:c + 1, :]

    first_row, second_row, last_row = row_lane == 0, row_lane == 1, row_lane == rows - 1
    in1 = kept(west_ok, corner[0:1, :])
    in2 = kept(west_ok, corner[1:2, :])
    q_nw = nw_ends[:, 1:2] - nw_ends[:, 2:3] * (col_w[6:7, :] + in1)
    tip = m_w * in1 - khm_w * (col_w[7:8, :] * (in1 - in2) + km_w * in1 - q_nw)
    w_share = col_w[3:4, :] + jnp.where(first_row, km_w * in1, 0.0)
    w_eta = col_w[4:5, :] + jnp.where(first_row, tip + kept(west_ok, corner[2:3, :]), 0.0)
    w_eta += jnp.where(last_row, khm_w * km_w * sw_eta, 0.0)
    w_eta += jnp.where(second_row, khm_w * km_w[:, 0:1] * in1, 0.0)
    in1 = kept(east_ok, corner[3:4, :])
    in2 = kept(east_ok, corner[4:5, :])
    q_ne = ne_ends[:, 1:2] - ne_ends[:, 2:3] * (col_e[0:1, :] + in1)
    tip = m_e * in1 + khm_e * (km_e * (in2 - in1) - km_e * in1 + q_ne)
    x_eta = col_e[0:1, :] + jnp.where(first_row, in1, 0.0)
    x_next = col_e[1:2, :] + jnp.where(first_row, tip + kept(east_ok, corner[5:6, :]), 0.0)
    x_next += jnp.where(last_row, khm_e * km_e * se_eta, 0.0)
    x_next += jnp.where(second_row, khm_e * km_e[:, 0:1] * in1, 0.0)
    for n, v in ((0, x_eta), (1, w_share), (3, w_eta), (5, x_next)):
        tmp[n:n + 1, :] = v
    halo = jnp.transpose(tmp[...])
    for r in (0, end):
        at = slice(r, r + BLOCK)
        step_rows(r, E0, P0, Q0, H, W, halo, E1, P1, Q1)
        next_halo(at, halo[at, :], E0[at, head], P1[at, tail])
    for c in range(chunks):
        lane = slice(c * LANES, (c + 1) * LANES)
        e1 = E1[0:1, lane] + line[4, c:c + 1, :]
        E1[0:1, lane] = e1
        E1[rows:rows + 1, lane] = line[2, c:c + 1, :] + line[3, c:c + 1, :] * Q1[rows + 7:rows + 8, lane]
        Q2[7:8, lane] = line[0, c:c + 1, :] - line[1, c:c + 1, :] * e1
    send_columns(lambda copy: copy.wait_send())
    send_rows(lambda copy: copy.wait_send())
    send_down(lambda copy: copy.wait_send())

    @pl.when(level == 1)
    def _():
        fine_copy().wait_send()


def two_level(mesh, adjoint_height, adjoint_momenta, depth, wet_mask, adjacency, nest_gain, nest_index):
    patches = mesh.shape["patch"]
    rows, cols = adjoint_height.shape[1:]
    chunks = cols // LANES
    f32 = jnp.float32
    anywhere = pl.BlockSpec(memory_space=pl.ANY)
    v = pltpu.VMEM
    dma = pltpu.SemaphoreType.DMA
    whole = (v((rows + 8, cols), f32), v((rows, cols), f32), v((rows + 8, cols), f32))
    scratch = [
        pltpu.SMEM(adjacency.shape, jnp.int32), pltpu.SMEM(adjacency.shape, jnp.int32),
        *whole,
        v(nest_gain.shape, f32), v(nest_index.shape, jnp.int32),
        v((16, chunks, LANES), f32), v((16, LANES), f32), v((rows + 8, LANES), f32),
        v((48, LANES), f32), v((32, LANES), f32), v((48, LANES), f32), v((8, LANES), f32),
        v((4, chunks, LANES), f32), v((8, LANES), f32), v((8, LANES), f32),
        dma((28,)), dma((5, patches)), dma((3, patches)), dma((2, patches)), dma((2,)),
        v((patches, 48, LANES), f32), v((patches, 32, LANES), f32), v((patches, 8, LANES), f32),
        v((2, patches, 48, LANES), f32),
    ]
    here = pl.BlockSpec(memory_space=pltpu.VMEM)
    state = pl.pallas_call(
        functools.partial(swap, patches, rows, cols),
        out_shape=(*whole, v((rows, cols), f32), v((rows, cols), jnp.int32), v((rows, 8), f32), *whole),
        in_specs=[anywhere] * 7,
        out_specs=(here,) * 9,
        scratch_shapes=scratch,
        compiler_params=pltpu.CompilerParams(collective_id=0, has_side_effects=True,
                                             vmem_limit_bytes=14 << 20),
    )(*[pltpu.with_memory_space_constraint(x, pltpu.HBM) for x in (
        adjacency, adjoint_height, adjoint_momenta, depth, wet_mask, nest_gain, nest_index)])
    state = [pltpu.with_memory_space_constraint(x, pltpu.VMEM) for x in state]
    return pl.pallas_call(
        functools.partial(settle, rows),
        out_shape=(jax.ShapeDtypeStruct(adjoint_height.shape, f32),
                   jax.ShapeDtypeStruct(adjoint_momenta.shape, f32)),
        in_specs=[here] * 9,
        out_specs=(anywhere, anywhere),
        scratch_shapes=[*whole, dma((9,))],
        compiler_params=pltpu.CompilerParams(vmem_limit_bytes=12 << 20),
    )(*state)


def solution(mesh):
    in_specs = (
        P(("parts", "level"), ("patch", "sub"), None),
        P(None, ("parts", "level"), ("patch", "sub"), None),
        P("level", ("patch", "sub"), None),
        P("level", ("patch", "sub"), None),
        P("level", None, None),
        P(None, ("patch", "sub")),
        P(None, ("patch", "sub")),
    )
    out_specs = (
        P(("parts", "level"), ("patch", "sub"), None),
        P(None, ("parts", "level"), ("patch", "sub"), None),
    )
    run = two_level if mesh.shape["level"] == 2 else body
    return jax.shard_map(functools.partial(run, mesh), mesh=mesh, in_specs=in_specs,
                         out_specs=out_specs, check_vma=False)
```

```python
import functools

import jax
import jax.numpy as jnp
from jax import lax
from jax.experimental import pallas as pl
from jax.experimental.pallas import tpu as pltpu
from jax.sharding import PartitionSpec as P

STEPS = 2
COURANT = 0.45
LANES = 128
BLOCK = 8


def advance(r, E, Pm, Q, H, W, halo, E_to, P_to, Q_to):
    cols = Pm.shape[1]
    lane_ids = lax.broadcasted_iota(jnp.int32, (BLOCK, cols), 1)
    span = slice(r, r + BLOCK)
    e = E[span, :]
    wet = W[span, :].astype(jnp.float32)
    e_south = E[r + 1:r + 1 + BLOCK, :]
    e_east = pltpu.roll(e, cols - 1, 1)
    if halo is not None:
        e_east = jnp.where(lane_ids == cols - 1, halo[span, 0:1], e_east)
    p = wet * (Pm[span, :] - COURANT * (e_east - e))
    q = wet * (Q[8 + r:16 + r, :] - COURANT * (e_south - e))
    p_west = pltpu.roll(p, 1, 1)
    if halo is not None:
        p_edge = halo[span, 1:2] - COURANT * halo[span, 2:3] * e[:, 0:1]
        p_west = jnp.where(lane_ids == 0, p_edge, p_west)
    P_to[span, :] = p
    Q_to[8 + r:16 + r, :] = q
    q_north = Q_to[7 + r:15 + r, :]
    E_to[span, :] = wet * (e - COURANT * H[span, :] * ((p - p_west) + (q - q_north)))


def finish(rows, E, Pm, Q, H, W, halo, E2, P2, Q2, eta_out, mom_out, Ef, Pf, Qf, sems):
    cols = Pm.shape[1]
    end = rows - BLOCK
    mid = slice(BLOCK, end)
    head, tail = slice(0, LANES), slice(cols - LANES, cols)
    before, inner = slice(0, cols - LANES), slice(LANES, cols - LANES)
    stores = []

    def store(src, dst):
        copy = pltpu.make_async_copy(src, dst, sems.at[len(stores)])
        copy.start()
        stores.append(copy)

    eta_to, row_to, col_to = eta_out.at[0], mom_out.at[0, 0], mom_out.at[1, 0]
    store(Q2.at[BLOCK + 8:end + 8], col_to.at[mid])
    store(P2.at[mid, before], row_to.at[mid, before])
    store(E2.at[mid, inner], eta_to.at[mid, inner])
    edges = halo[...]
    lane_ids = lax.broadcasted_iota(jnp.int32, (end - BLOCK, LANES), 1)

    across = Q2[BLOCK + 8:end + 8, head] - Q2[BLOCK + 7:end + 7, head]
    e = E[mid, head]
    wet = W[mid, head].astype(jnp.float32)
    p_edge = edges[mid, 1:2] - COURANT * edges[mid, 2:3] * e[:, 0:1]
    fixed = wet * (e - COURANT * H[mid, head] * ((P2[mid, head] - p_edge) + across))
    Ef[mid, head] = jnp.where(lane_ids == 0, fixed, E2[mid, head])
    store(Ef.at[mid, head], eta_to.at[mid, head])

    across = Q2[BLOCK + 8:end + 8, tail] - Q2[BLOCK + 7:end + 7, tail]
    e = E[mid, tail]
    wet = W[mid, tail].astype(jnp.float32)
    p = wet * (Pm[mid, tail] - COURANT * (edges[mid, 0:1] - e))
    p = jnp.where(lane_ids == LANES - 1, p, P2[mid, tail])
    Pf[mid, tail] = p
    store(Pf.at[mid, tail], row_to.at[mid, tail])
    fixed = wet * (e - COURANT * H[mid, tail] * ((p - pltpu.roll(p, 1, 1)) + across))
    Ef[mid, tail] = jnp.where(lane_ids == LANES - 1, fixed, E2[mid, tail])
    store(Ef.at[mid, tail], eta_to.at[mid, tail])

    for r in (0, end):
        Qf[7 + r:8 + r, :] = (Q if r == 0 else Q2)[7 + r:8 + r, :]
        advance(r, E, Pm, Q, H, W, edges, Ef, Pf, Qf)
        at = slice(r, r + BLOCK)
        store(Pf.at[at], row_to.at[at])
        store(Qf.at[8 + r:16 + r], col_to.at[at])
        store(Ef.at[at], eta_to.at[at])
    for copy in stores:
        copy.wait()


def exchange(patches, levels, rows, cols,
             adj_hbm, eta_hbm, mom_hbm, depth_hbm, wet_hbm, gain_hbm, table_hbm,
             E1, P1, Q1, H, W, halo_out, E2, P2, Q2,
             adj, E0, P0, Q0, gain_v, table_v, f8, idx8, gain8, tmp,
             sfirst, slast, scol, sinf, sew,
             rown, in_sems, send_sems, recv_sems, own_sems, *landing):
    rfirst, rlast, rcol, rnbr, rew = (landing[n * STEPS:(n + 1) * STEPS] for n in range(5))
    fields = ((E0, P0, Q0), (E1, P1, Q1))
    patch = lax.axis_index("patch")
    level = lax.axis_index("level")
    half = lax.axis_index("sub")
    chunks = cols // LANES
    other = 1 - half

    loads = [
        pltpu.make_async_copy(eta_hbm.at[0], E0.at[0:rows], in_sems.at[0]),
        pltpu.make_async_copy(mom_hbm.at[0, 0], P0, in_sems.at[1]),
        pltpu.make_async_copy(mom_hbm.at[1, 0], Q0.at[8:8 + rows], in_sems.at[2]),
        pltpu.make_async_copy(wet_hbm.at[0], W, in_sems.at[3]),
        pltpu.make_async_copy(table_hbm, table_v, in_sems.at[4]),
        pltpu.make_async_copy(gain_hbm, gain_v, in_sems.at[5]),
        pltpu.make_async_copy(adj_hbm, adj, in_sems.at[6]),
        pltpu.make_async_copy(depth_hbm.at[0], H, in_sems.at[7]),
    ]
    barrier = pltpu.get_barrier_semaphore()

    peers = [patch] + [lax.rem(patch + d, patches) for d in range(1, patches)]

    def greet(d, h, lev):
        pl.semaphore_signal(barrier, inc=1, device_id={
            "patch": peers[d], "sub": h, "level": lev},
            device_id_type=pl.DeviceIdType.MESH)

    for d in range(patches - 1, -1, -1):
        greet(d, other, level)
        if d:
            greet(d, half, level)

    @pl.when(level > 0)
    def _():
        for d in range(patches):
            greet(d, half, level - 1)
            greet(d, other, level - 1)

    @pl.when(level < levels - 1)
    def _():
        for d in range(patches):
            greet(d, half, level + 1)
            greet(d, other, level + 1)

    for load in loads:
        load.start()

    for load in loads[:7]:
        load.wait()

    lower = jnp.maximum(level - 1, 0)
    for c in range(chunks):
        lane = slice(c * LANES, (c + 1) * LANES)
        index, gain = table_v[0:1, lane], gain_v[0:1, lane]
        for lev in range(1, levels - 1):
            index = jnp.where(lower == lev, table_v[lev:lev + 1, lane], index)
            gain = jnp.where(lower == lev, gain_v[lev:lev + 1, lane], gain)
        idx8[c:c + 1, :] = index
        gain8[c:c + 1, :] = gain

    def remote(t, kind, src, buf, slot, d, h, lev):
        return pltpu.make_async_remote_copy(
            src_ref=src, dst_ref=buf, send_sem=send_sems.at[t, kind, d],
            recv_sem=recv_sems.at[t, kind, slot],
            device_id={"patch": peers[d], "sub": h, "level": lev},
            device_id_type=pl.DeviceIdType.MESH)

    def last_part(t):
        return slice(0, 2) if t == 0 else slice(t + 1, t + 2)

    def column_copy(t, slot, d):
        return remote(t, 0, scol.at[t, 0:3], rcol[t].at[slot, 0:3], slot, d, half, level)

    def first_copy(t, slot, d):
        return remote(t, 1, sfirst.at[t], rfirst[t].at[slot], slot, d, other, level)

    def last_copy(t, slot, d):
        part = last_part(t)
        return remote(t, 2, slast.at[part], rlast[t].at[slot], slot, d, other, level)

    def beside_copy(t, slot, d):
        return remote(t, 3, sinf.at[t], rnbr[t].at[slot], slot, d, other, lower)

    def ends_copy(t, slot, d):
        return remote(t, 4, sew.at[t], rew[t].at[slot], slot, d, half, lower)

    def per_half(across, inside, act):
        @pl.when(half == across)
        def _():
            for d in range(1, patches):
                act(d)

        @pl.when(half == inside)
        def _():
            act(0)

    def own_copy(t):
        return pltpu.make_async_remote_copy(
            src_ref=sinf.at[t], dst_ref=rown.at[t], send_sem=own_sems.at[t, 0],
            recv_sem=own_sems.at[t, 1], device_id={"level": lower},
            device_id_type=pl.DeviceIdType.MESH)

    def make_inflow(t):
        E = fields[t][0]
        for c in range(chunks):
            f8[c:c + 1, :] = E[0:1, c * LANES:(c + 1) * LANES]
        index = idx8[...]
        inside = jnp.bitwise_and(index, LANES - 1)
        which = lax.shift_right_logical(index, 7)
        picked = jnp.zeros((chunks, LANES), jnp.float32)
        for c in range(chunks):
            source = jnp.broadcast_to(f8[c:c + 1, :], (chunks, LANES))
            got = jnp.take_along_axis(source, inside, axis=1, mode="promise_in_bounds")
            picked = jnp.where(which == c, got, picked)
        inflow = gain8[...] * picked
        sinf[t] = inflow
        sew[t, 0:1, :] = inflow[0:1, :]
        sew[t, 1:2, :] = pltpu.roll(inflow[chunks - 1:chunks, :], 1, 1)

    def send_inflow(t):
        own_copy(t).start()
        per_half(0, 1, lambda d: beside_copy(t, patch, d).start())
        for d in range(1, patches):
            ends_copy(t, patch, d).start()

    def inflow_waits(t):
        per_half(1, 0, lambda d: beside_copy(t, peers[d], d).wait_recv())
        for d in range(1, patches):
            ends_copy(t, peers[d], d).wait_recv()

    def inflow_send_waits(t):
        own_copy(t).wait_send()
        per_half(0, 1, lambda d: beside_copy(t, patch, d).wait_send())
        for d in range(1, patches):
            ends_copy(t, patch, d).wait_send()

    def send_halos(t, act):
        send_rows(t, act)
        send_columns(t, act)

    def send_columns(t, act):
        for d in range(1, patches):
            act(column_copy(t, patch, d))

    def send_rows(t, act):
        @pl.when(half == 0)
        def _():
            for d in range(1, patches):
                act(first_copy(t, patch, d))
            act(last_copy(t, patch, 0))

        @pl.when(half == 1)
        def _():
            for d in range(1, patches):
                act(last_copy(t, patch, d))
            act(first_copy(t, patch, 0))

    def receive_halos(t):
        @pl.when(half == 0)
        def _():
            first_copy(t, peers[0], 0).wait_recv()
            for d in range(1, patches):
                last_copy(t, peers[d], d).wait_recv()

        @pl.when(half == 1)
        def _():
            last_copy(t, peers[0], 0).wait_recv()
            for d in range(1, patches):
                first_copy(t, peers[d], d).wait_recv()

        for d in range(1, patches):
            column_copy(t, peers[d], d).wait_recv()

    north = adj[0, patch, 0]
    south = adj[0, patch, 1]
    west = adj[0, patch, 2]
    east = adj[0, patch, 3]
    south_ok = jnp.logical_or(half == 0, south >= 0)
    north_ok = jnp.logical_or(half == 1, north >= 0)
    south_at = jnp.where(half == 0, patch, jnp.maximum(south, 0))
    north_at = jnp.where(half == 1, patch, jnp.maximum(north, 0))
    west_at = jnp.maximum(west, 0)
    east_at = jnp.maximum(east, 0)
    finer = level < levels - 1
    lane_ids = lax.broadcasted_iota(jnp.int32, (rows, LANES), 1)
    first_lane = lax.broadcasted_iota(jnp.int32, (1, LANES), 1) == 0
    tail = slice(cols - LANES, cols)
    end = rows - 1

    def make_messages(t):
        @pl.when(level == levels - 1)
        def _():
            make_inflow(t)

        make_rows(t)
        make_columns(t)

    def make_rows(t):
        E, Pm, Q = fields[t]
        sfirst[t] = E[0:1, :]
        wet_row = W[end:rows, :].astype(jnp.float32)
        slast[t + 1] = wet_row * (Q[8 + end:8 + rows, :] + COURANT * E[end:rows, :])
        if t == 0:
            slast[0] = wet_row

    def make_columns(t):
        E, Pm, Q = fields[t]
        wet_tail = W[:, tail].astype(jnp.float32)
        share = wet_tail * (Pm[:, tail] + COURANT * E[0:rows, tail])
        mixed = jnp.where(lane_ids == 0, E[0:rows, 0:LANES],
                          jnp.where(lane_ids == 1, pltpu.roll(share, 2, 1),
                                    pltpu.roll(wet_tail, 3, 1)))
        scol[t] = jnp.transpose(mixed[:, 0:8])

    def send_messages(t):
        @pl.when(level == levels - 1)
        def _():
            send_inflow(t)

        send_halos(t, lambda copy: copy.start())

    def receive(t):
        E, Pm, Q = fields[t]

        @pl.when(finer)
        def _():
            own_copy(t).wait_recv()
            for c in range(chunks):
                lane = slice(c * LANES, (c + 1) * LANES)
                E[0:1, lane] += rown[t, c:c + 1, :]

        if levels > 2:
            @pl.when(jnp.logical_and(level > 0, level < levels - 1))
            def _():
                make_inflow(t)
                send_inflow(t)

        receive_halos(t)

        @pl.when(finer)
        def _():
            inflow_waits(t)

        east_row = rcol[t][east_at][0:1, :]
        east_row += jnp.where(jnp.logical_and(first_lane, finer), rew[t][east_at][0:1, :], 0.0)
        west_cols = rcol[t][west_at]
        share = west_cols[1:2, :]
        wet_w = west_cols[2:3, :]
        share += jnp.where(jnp.logical_and(first_lane, finer),
                           COURANT * wet_w * rew[t][west_at][1:2, :], 0.0)
        tmp[0:1, :] = jnp.where(east >= 0, east_row, 0.0)
        tmp[1:2, :] = jnp.where(west >= 0, share, 0.0)
        tmp[2:3, :] = jnp.where(west >= 0, wet_w, 0.0)
        beside = rnbr[t][south_at]
        below = rfirst[t][south_at]
        for c in range(chunks):
            lane = slice(c * LANES, (c + 1) * LANES)
            value = below[:, lane] + jnp.where(finer, beside[c:c + 1, :], 0.0)
            E[rows:rows + 1, lane] = jnp.where(south_ok, value, 0.0)
        share_n = rlast[t][north_at, 1 if t == 0 else 0]
        wet_n = rlast[0][north_at, 0]
        Q_to = Q1
        Q_to[7:8, :] = jnp.where(north_ok, share_n - COURANT * wet_n * E[0:1, :], 0.0)
        return jnp.transpose(tmp[...])

    make_messages(0)
    sides = (level > 0).astype(jnp.int32) + (level < levels - 1).astype(jnp.int32)
    pl.semaphore_wait(barrier, 2 * patches - 1 + 2 * patches * sides)
    send_messages(0)
    loads[7].wait()
    for r in range(0, rows - BLOCK, BLOCK):
        advance(r, E0, P0, Q0, H, W, None, E1, P1, Q1)
    halo = receive(0)
    for r in (0, rows - BLOCK):
        advance(r, E0, P0, Q0, H, W, None, E1, P1, Q1)
    head = slice(0, LANES)
    e = E0[0:rows, head]
    wet = W[:, head].astype(jnp.float32)
    p_edge = halo[:, 1:2] - COURANT * halo[:, 2:3] * e[:, 0:1]
    across = Q1[8:8 + rows, head] - Q1[7:7 + rows, head]
    fixed = wet * (e - COURANT * H[:, head] * ((P1[:, head] - p_edge) + across))
    E1[0:rows, head] = jnp.where(lane_ids == 0, fixed, E1[0:rows, head])
    e = E0[0:rows, tail]
    wet = W[:, tail].astype(jnp.float32)
    p = wet * (P0[:, tail] - COURANT * (halo[:, 0:1] - e))
    p = jnp.where(lane_ids == LANES - 1, p, P1[:, tail])
    P1[:, tail] = p
    across = Q1[8:8 + rows, tail] - Q1[7:7 + rows, tail]
    fixed = wet * (e - COURANT * H[:, tail] * ((p - pltpu.roll(p, 1, 1)) + across))
    E1[0:rows, tail] = jnp.where(lane_ids == LANES - 1, fixed, E1[0:rows, tail])

    @pl.when(level == levels - 1)
    def _():
        make_inflow(1)
        send_inflow(1)

    make_rows(1)
    send_rows(1, lambda copy: copy.start())
    make_columns(1)
    send_columns(1, lambda copy: copy.start())
    for r in range(0, rows - BLOCK, BLOCK):
        advance(r, E1, P1, Q1, H, W, None, E2, P2, Q2)
    halo_out[...] = receive(1)
    for t in range(STEPS):
        send_halos(t, lambda copy: copy.wait_send())

        @pl.when(level > 0)
        def _():
            inflow_send_waits(t)


def body(mesh, adjoint_height, adjoint_momenta, depth, wet_mask, adjacency, nest_gain, nest_index):
    patches, levels = mesh.shape["patch"], mesh.shape["level"]
    rows, cols = adjoint_height.shape[1:]
    chunks = cols // LANES
    f32 = jnp.float32
    anywhere = pl.BlockSpec(memory_space=pl.ANY)
    v = pltpu.VMEM
    dma = pltpu.SemaphoreType.DMA
    whole = (v((rows + 8, cols), f32), v((rows, cols), f32), v((rows + 8, cols), f32))
    scratch = [
        pltpu.SMEM(adjacency.shape, jnp.int32),
        *whole,
        v(nest_gain.shape, f32), v(nest_index.shape, jnp.int32),
        v((chunks, LANES), f32), v((chunks, LANES), jnp.int32), v((chunks, LANES), f32),
        v((8, LANES), f32),
        v((STEPS, 1, cols), f32), v((STEPS + 1, 1, cols), f32), v((STEPS, 8, LANES), f32),
        v((STEPS, chunks, LANES), f32), v((STEPS, 2, LANES), f32),
        v((STEPS, chunks, LANES), f32),
        dma((8,)), dma((STEPS, 5, patches)), dma((STEPS, 5, patches)), dma((STEPS, 2)),
    ]
    scratch += [v((patches, 1, cols), f32)] * STEPS
    scratch += [v((patches, 2 if t == 0 else 1, 1, cols), f32) for t in range(STEPS)]
    scratch += [v((patches, 8, LANES), f32)] * STEPS
    scratch += [v((patches, chunks, LANES), f32)] * STEPS
    scratch += [v((patches, 2, LANES), f32)] * STEPS
    here = pl.BlockSpec(memory_space=pltpu.VMEM)
    state = pl.pallas_call(
        functools.partial(exchange, patches, levels, rows, cols),
        out_shape=(*whole, v((rows, cols), f32), v((rows, cols), jnp.int32), v((rows, 8), f32), *whole),
        in_specs=[anywhere] * 7,
        out_specs=(here,) * 9,
        scratch_shapes=scratch,
        compiler_params=pltpu.CompilerParams(collective_id=0, has_side_effects=True,
                                             vmem_limit_bytes=12 << 20),
    )(*[pltpu.with_memory_space_constraint(x, pltpu.HBM) for x in (
        adjacency, adjoint_height, adjoint_momenta, depth, wet_mask, nest_gain, nest_index)])
    state = [pltpu.with_memory_space_constraint(x, pltpu.VMEM) for x in state]
    return pl.pallas_call(
        functools.partial(finish, rows),
        out_shape=(jax.ShapeDtypeStruct(adjoint_height.shape, f32),
                   jax.ShapeDtypeStruct(adjoint_momenta.shape, f32)),
        in_specs=[here] * 9,
        out_specs=(anywhere, anywhere),
        scratch_shapes=[*whole, dma((12,))],
        compiler_params=pltpu.CompilerParams(vmem_limit_bytes=12 << 20),
    )(*state)


FULL, TAIL, ENDS = (0, 42), (24, 42), (40, 42)
DRY = 1e30


def step_rows(r, E, Pm, Q, H, W, edge, E_to, P_to, Q_to):
    cols = Pm.shape[1]
    lane_ids = lax.broadcasted_iota(jnp.int32, (BLOCK, cols), 1)
    span = slice(r, r + BLOCK)
    e = E[span, :]
    wet = W[span, :].astype(jnp.float32)
    e_south = E[r + 1:r + 1 + BLOCK, :]
    e_east = pltpu.roll(e, cols - 1, 1)
    if edge is not None:
        e_east = jnp.where(lane_ids == cols - 1, edge[span, 0:1], e_east)
    p = wet * (Pm[span, :] - COURANT * (e_east - e))
    q = wet * (Q[8 + r:16 + r, :] - COURANT * (e_south - e))
    p_west = pltpu.roll(p, 1, 1)
    if edge is not None:
        p_west = jnp.where(lane_ids == 0, edge[span, 1:2] - edge[span, 2:3] * e[:, 0:1], p_west)
    P_to[span, :] = p
    Q_to[8 + r:16 + r, :] = q
    q_north = Q_to[7 + r:15 + r, :]
    E_to[span, :] = wet * (e - COURANT * H[span, :] * ((p - p_west) + (q - q_north)))


def settle(rows, E, Pm, Q, H, W, halo, E2, P2, Q2, eta_out, mom_out, Ef, Pf, Qf, sems):
    end = rows - BLOCK
    mid = slice(BLOCK, end)
    stores = []

    def store(src, dst):
        copy = pltpu.make_async_copy(src, dst, sems.at[len(stores)])
        copy.start()
        stores.append(copy)

    eta_to, row_to, col_to = eta_out.at[0], mom_out.at[0, 0], mom_out.at[1, 0]
    store(Q2.at[BLOCK + 8:end + 8], col_to.at[mid])
    store(P2.at[mid], row_to.at[mid])
    store(E2.at[mid], eta_to.at[mid])
    edge = halo[...]

    def ends(r):
        step_rows(r, E, Pm, Q, H, W, edge, Ef, Pf, Qf)
        at = slice(r, r + BLOCK)
        store(Pf.at[at], row_to.at[at])
        store(Qf.at[8 + r:16 + r], col_to.at[at])
        store(Ef.at[at], eta_to.at[at])

    for r in (0, end):
        Qf[7 + r:8 + r, :] = Q2[7 + r:8 + r, :]
        ends(r)
    for copy in stores:
        copy.wait()


def swap(patches, rows, cols,
         adj_hbm, eta_hbm, mom_hbm, depth_hbm, wet_hbm, gain_hbm, table_hbm,
         E1, P1, Q1, H, W, halo_out, E2, P2, Q2,
         adj, fine, E0, P0, Q0, gain_v, table_v, line, stack, qb, sfirst, slast, sdown, scol,
         flow, corner, tmp, in_sems, send_sems, recv_sems, down_sems, fine_sems,
         rfirst, rlast, rcol, rdown):
    f32 = jnp.float32
    patch = lax.axis_index("patch")
    level = lax.axis_index("level")
    half = lax.axis_index("sub")
    other = 1 - half
    chunks = cols // LANES
    last = cols - 1
    end = rows - BLOCK
    head, tail = slice(0, LANES), slice(cols - LANES, cols)
    inner = slice(LANES, cols - LANES)
    mid = slice(BLOCK, end)
    loads = []

    def load(src, dst):
        copy = pltpu.make_async_copy(src, dst, in_sems.at[len(loads)])
        copy.start()
        loads.append(copy)

    fields = ((eta_hbm.at[0], E0, 0), (mom_hbm.at[0, 0], P0, 0), (mom_hbm.at[1, 0], Q0, 8),
              (wet_hbm.at[0], W, 0), (depth_hbm.at[0], H, 0))

    def load_part(at, lane):
        for src, dst, shift in fields:
            load(src.at[at, lane], dst.at[at.start + shift:at.stop + shift, lane])

    for at in (slice(0, BLOCK), slice(end, rows)):
        load_part(at, slice(0, cols))
    load(adj_hbm, adj)
    load(table_hbm, table_v)
    load(gain_hbm, gain_v)
    n_rows = len(loads)

    barrier = pltpu.get_barrier_semaphore()
    peers = [patch] + [jnp.where(patch < d, d, d - 1) for d in range(1, patches)]

    def greet(d, h, lev):
        pl.semaphore_signal(barrier, inc=1, device_id={
            "patch": peers[d], "sub": h, "level": lev},
            device_id_type=pl.DeviceIdType.MESH)

    for d in range(1, patches):
        greet(d, other, level)
        greet(d, half, level)
    greet(0, other, level)

    @pl.when(level == 0)
    def _():
        for d in list(range(1, patches)) + [0]:
            greet(d, half, 1)
            greet(d, other, 1)

    for lane in (head, tail):
        load_part(mid, lane)
    n_tiles = len(loads)
    load_part(mid, inner)

    E0[rows:rows + 8, :] = jnp.zeros((8, cols), f32)
    qb[0:8, :] = jnp.zeros((8, LANES), f32)
    lane_ids = lax.broadcasted_iota(jnp.int32, (chunks, LANES), 1)
    cell_ids = lax.broadcasted_iota(jnp.int32, (chunks, LANES), 0) * LANES + lane_ids
    row_lane = lax.broadcasted_iota(jnp.int32, (1, LANES), 1)

    def east_of(x, beyond):
        y = pltpu.roll(x, LANES - 1, 1)
        y = jnp.where(lane_ids == LANES - 1, pltpu.roll(y, chunks - 1, 0), y)
        return jnp.where(cell_ids == last, beyond, y)

    def west_of(x, beyond):
        y = pltpu.roll(x, 1, 1)
        y = jnp.where(lane_ids == 0, pltpu.roll(y, 1, 0), y)
        return jnp.where(cell_ids == 0, beyond, y)

    def gather(x, index):
        inside = jnp.bitwise_and(index, LANES - 1)
        which = lax.shift_right_logical(index, 7)
        picked = jnp.zeros((chunks, LANES), f32)
        for c in range(chunks):
            source = jnp.broadcast_to(x[c:c + 1, :], (chunks, LANES))
            got = jnp.take_along_axis(source, inside, axis=1, mode="promise_in_bounds")
            picked = jnp.where(which == c, got, picked)
        return picked

    for copy in loads[:n_rows]:
        copy.wait()

    def lines(n, ref, r):
        for c in range(chunks):
            line[n, c:c + 1, :] = ref[r:r + 1, c * LANES:(c + 1) * LANES].astype(f32)

    for n, (ref, r) in enumerate((
            (E0, 0), (E0, 1), (P0, 0), (Q0, 8), (W, 0), (H, 0),
            (E0, rows - 1), (P0, rows - 1), (Q0, rows + 7), (W, rows - 1), (H, rows - 1))):
        lines(n, ref, r)

    e, p, q, m = line[0], line[2], line[3], line[4]
    e_first = e
    km = COURANT * m
    khm = km * line[5]
    mp = m * p
    stack[4:5, :] = jnp.where(row_lane < 64, e[0:1, :], e[chunks - 1:chunks, :])
    stack[5:6, :] = jnp.where(row_lane < 64, mp[0:1, :], mp[chunks - 1:chunks, :])
    stack[6:7, :] = jnp.where(row_lane < 64, km[0:1, :], km[chunks - 1:chunks, :])
    el, ml = line[6], line[9]
    kml = COURANT * ml
    khml = kml * line[10]
    aq = ml * line[8] + kml * el
    ap = ml * line[7] + kml * el
    sdown[24:32, :] = aq
    sdown[32:40, :] = khml
    for n, x in enumerate((el, aq, kml, ap)):
        stack[n:n + 1, :] = jnp.where(row_lane < 64, x[0:1, :], x[chunks - 1:chunks, :])
    stack[13:16, :] = jnp.zeros((3, LANES), f32)

    @pl.when(level == 0)
    def _():
        stack[7:13, :] = jnp.zeros((6, LANES), f32)

    for c in range(chunks):
        lane = slice(c * LANES, (c + 1) * LANES)
        line[14, c:c + 1, :] = gain_v[0:1, lane]
        line[15, c:c + 1, :] = table_v[0:1, lane].astype(f32)
    gain, index = line[14], line[15].astype(jnp.int32)

    @pl.when(level == 1)
    def _():
        p_new = mp - km * (east_of(e, 0.0) - e)
        q_new = m * q - km * (line[1] - e)
        there = m * e - khm * (p_new - west_of(p_new, 0.0) + q_new)
        parts = [gather(x, index) for x in (e, there, khm)]
        for n, x in enumerate(parts):
            sdown[8 * n:8 * n + 8, :] = x
        inflow = gain * parts[0]
        rows_of = (inflow, None, gain * parts[1], gain * parts[2],
                   COURANT * parts[2] * inflow, line[15])
        for n, x in enumerate(rows_of):
            if x is None:
                low = pltpu.roll(inflow, LANES - 1, 1)[0:1, :]
                high = pltpu.roll(inflow, 1, 1)[chunks - 1:chunks, :]
            else:
                low, high = x[0:1, :], x[chunks - 1:chunks, :]
            stack[7 + n:8 + n, :] = jnp.where(row_lane < 64, low, high)

    turned = jnp.transpose(stack[...])
    for ref, at in ((sfirst, 24), (slast, 24), (sdown, 40)):
        ref[at:at + 1, 0:16] = turned[0:1, :]
        ref[at + 1:at + 2, 0:16] = turned[LANES - 1:LANES, :]

    def row_messages():
        for n, (ref, r) in enumerate(((E0, rows - 2), (Q0, rows + 6), (W, rows - 2))):
            lines(11 + n, ref, r)
        sfirst[0:8, :] = e
        sfirst[8:16, :] = mp - west_of(mp, 0.0) + (m * q - km * line[1])
        sfirst[16:24, :] = khm
        sfirst[32:40, :] = gain
        sfirst[40:48, :] = line[15]
        p_new = ml * line[7] - kml * (east_of(el, 0.0) - el)
        q_above = line[13] * (line[12] - COURANT * (el - line[11]))
        slast[0:8, :] = ml * el - khml * (p_new - west_of(p_new, 0.0) - q_above)
        slast[8:16, :] = aq
        slast[16:24, :] = khml

    def remote(kind, src, dst, recv_sem, d, h, lev):
        return pltpu.make_async_remote_copy(
            src_ref=src, dst_ref=dst, send_sem=send_sems.at[kind, d], recv_sem=recv_sem,
            device_id={"patch": peers[d], "sub": h, "level": lev},
            device_id_type=pl.DeviceIdType.MESH)

    def column_copy(slot, d):
        return remote(0, scol, rcol.at[slot], recv_sems.at[0, slot], d, half, level)

    def first_copy(slot, d, size):
        return remote(1, sfirst.at[0:size], rfirst.at[slot, 0:size], recv_sems.at[1, slot], d, other, level)

    def by_level(act):
        for lev, size in enumerate((48, 26)):
            @pl.when(level == lev)
            def _():
                act(size)

    def last_copy(slot, d):
        return remote(2, slast.at[0:26], rlast.at[slot, 0:26], recv_sems.at[2, slot], d, other, level)

    def down_copy(part, from_half, slot, d, h):
        at = slice(*part)
        return remote(3 + h, sdown.at[at], rdown.at[from_half, slot, at],
                      down_sems.at[from_half, slot], d, h, 1 - level)

    def fine_copy():
        return pltpu.make_async_remote_copy(
            src_ref=adj, dst_ref=fine, send_sem=fine_sems.at[0], recv_sem=fine_sems.at[1],
            device_id={"level": 1 - level}, device_id_type=pl.DeviceIdType.MESH)

    far = list(range(1, patches)) + [0]

    def send_rows(act):
        @pl.when(half == 0)
        def _():
            def firsts(size):
                for d in range(1, patches):
                    act(first_copy(patch, d, size))

            by_level(firsts)
            act(last_copy(patch, 0))

        @pl.when(half == 1)
        def _():
            for d in range(1, patches):
                act(last_copy(patch, d))
            by_level(lambda size: act(first_copy(patch, 0, size)))

    def send_down(act):
        @pl.when(jnp.logical_and(level == 1, half == 0))
        def _():
            for d in far:
                act(down_copy(ENDS if d else FULL, 0, patch, d, 0))
                act(down_copy(FULL if d else TAIL, 0, patch, d, 1))

        @pl.when(jnp.logical_and(level == 1, half == 1))
        def _():
            for d in far:
                act(down_copy(TAIL if d else FULL, 1, patch, d, 0))
                act(down_copy(TAIL if d else FULL, 1, patch, d, 1))

    def send_columns(act):
        for d in range(1, patches):
            act(column_copy(patch, d))

    def receive_columns():
        for d in range(1, patches):
            column_copy(peers[d], d).wait_recv()

    def receive_rows():
        @pl.when(half == 0)
        def _():
            by_level(lambda size: first_copy(patch, 0, size).wait_recv())
            for d in range(1, patches):
                last_copy(peers[d], d).wait_recv()

        @pl.when(half == 1)
        def _():
            def firsts(size):
                for d in range(1, patches):
                    first_copy(peers[d], d, size).wait_recv()

            last_copy(patch, 0).wait_recv()
            by_level(firsts)

    def receive_down():
        @pl.when(jnp.logical_and(level == 0, half == 0))
        def _():
            for d in far:
                down_copy(TAIL if d else FULL, 1, peers[d], d, 0).wait_recv()
                down_copy(ENDS if d else FULL, 0, peers[d], d, 0).wait_recv()

        @pl.when(jnp.logical_and(level == 0, half == 1))
        def _():
            for d in far:
                down_copy(TAIL if d else FULL, 1, peers[d], d, 1).wait_recv()
                down_copy(FULL if d else TAIL, 0, peers[d], d, 1).wait_recv()

    @pl.when(level == 0)
    def _():
        row_messages()

    pl.semaphore_wait(barrier, 2 * patches - 1 + 2 * patches * level)

    @pl.when(level == 1)
    def _():
        fine_copy().start()

    send_down(lambda copy: copy.start())

    @pl.when(level == 1)
    def _():
        row_messages()

    send_rows(lambda copy: copy.start())
    for copy in loads[n_rows:n_tiles]:
        copy.wait()
    tile_lanes = lax.broadcasted_iota(jnp.int32, (rows, LANES), 1)
    mixed = None
    for lane in (head, tail):
        e = E0[0:rows, lane]
        m = W[:, lane].astype(f32)
        km = COURANT * m
        khm = km * H[:, lane]
        p_new = m * P0[:, lane] - km * (pltpu.roll(e, LANES - 1, 1) - e)
        q_new = m * Q0[8:8 + rows, lane] - km * (E0[1:rows + 1, lane] - e)
        qb[8:8 + rows, :] = q_new
        across = q_new - qb[7:7 + rows, :]
        if lane == head:
            parts = ((e, 0), (m * e - khm * (p_new + across), 0), (khm, 0))
        else:
            parts = ((m * P0[:, lane] + km * e, LANES - 1),
                     (m * e - khm * (across - pltpu.roll(p_new, 1, 1)), LANES - 1),
                     (khm, LANES - 1), (e, LANES - 1), (km, LANES - 2))
        for n, (x, at) in enumerate(parts):
            to = n + (0 if lane == head else 3)
            moved = pltpu.roll(x, (to - at) % LANES, 1) if (to - at) % LANES else x
            mixed = moved if mixed is None else jnp.where(tile_lanes == to, moved, mixed)
    scol[...] = jnp.transpose(mixed[:, 0:8])
    send_columns(lambda copy: copy.start())

    for copy in loads[n_tiles:]:
        copy.wait()
    for r in range(0, rows, BLOCK):
        step_rows(r, E0, P0, Q0, H, W, None, E1, P1, Q1)
    for r in range(0, end, BLOCK):
        step_rows(r, E1, P1, Q1, H, W, None, E2, P2, Q2)

    north, south = adj[0, patch, 0], adj[0, patch, 1]
    west, east = adj[0, patch, 2], adj[0, patch, 3]
    south_ok = jnp.logical_or(half == 0, south >= 0)
    north_ok = jnp.logical_or(half == 1, north >= 0)
    south_at = jnp.where(half == 0, patch, jnp.maximum(south, 0))
    north_at = jnp.where(half == 1, patch, jnp.maximum(north, 0))
    west_ok, east_ok = west >= 0, east >= 0
    west_at, east_at = jnp.maximum(west, 0), jnp.maximum(east, 0)

    def beyond(at, ok, side):
        to = adj[0, at, side]
        return jnp.maximum(to, 0), jnp.logical_and(ok, to >= 0)

    nw_at, nw_ok = beyond(north_at, north_ok, 2)
    ne_at, ne_ok = beyond(north_at, north_ok, 3)
    sw_at, sw_ok = beyond(south_at, south_ok, 2)
    se_at, se_ok = beyond(south_at, south_ok, 3)

    def kept(ok, x):
        return jnp.where(ok, x, 0.0)

    receive_columns()
    col_w, col_e = kept(west_ok, rcol[west_at]), kept(east_ok, rcol[east_at])
    khm_w, khm_e = col_w[5:6, :], col_e[2:3, :]
    m_w, m_e = (khm_w > 0.0).astype(f32), (khm_e > 0.0).astype(f32)
    km_w, km_e = COURANT * m_w, COURANT * m_e
    for n, v in enumerate((col_e[0:1, :], col_w[3:4, :], km_w, col_w[4:5, :], khm_w, col_e[1:2, :], khm_e)):
        tmp[n:n + 1, :] = v
    tmp[7:8, :] = jnp.zeros((1, LANES), f32)
    halo = jnp.transpose(tmp[...])

    def next_halo(at, halo, e, p):
        p_edge = halo[:, 1:2] - halo[:, 2:3] * e[:, 0:1]
        halo_out[at, 0:1] = halo[:, 5:6] + halo[:, 6:7] * p[:, LANES - 1:LANES]
        halo_out[at, 1:2] = p_edge + halo[:, 2:3] * (halo[:, 3:4] - halo[:, 4:5] * p_edge)
        halo_out[at, 2:3] = halo[:, 2:3]

    e_head = E0[0:rows, head]
    wet_head = W[:, head].astype(f32)
    p_edge = halo[:, 1:2] - halo[:, 2:3] * e_head[:, 0:1]
    across = Q1[8:8 + rows, head] - Q1[7:7 + rows, head]
    fixed = wet_head * (e_head - COURANT * H[:, head] * ((P1[:, head] - p_edge) + across))
    E1[0:rows, head] = jnp.where(tile_lanes == 0, fixed, E1[0:rows, head])
    e = E0[0:rows, tail]
    wet_tail = W[:, tail].astype(f32)
    p = wet_tail * (P0[:, tail] - COURANT * (halo[:, 0:1] - e))
    p = jnp.where(tile_lanes == LANES - 1, p, P1[:, tail])
    P1[:, tail] = p
    across = Q1[8:8 + rows, tail] - Q1[7:7 + rows, tail]
    fixed = wet_tail * (e - COURANT * H[:, tail] * ((p - pltpu.roll(p, 1, 1)) + across))
    E1[0:rows, tail] = jnp.where(tile_lanes == LANES - 1, fixed, E1[0:rows, tail])
    next_halo(slice(0, rows), halo, e_head, p)
    edge = halo_out[...]
    for lane in (head, tail):
        e = E1[0:rows, lane]
        wet = wet_head if lane == head else wet_tail
        q = wet * (Q1[8:8 + rows, lane] - COURANT * (E1[1:rows + 1, lane] - e))
        Q2[8:8 + rows, lane] = q
        across = q - Q2[7:7 + rows, lane]
        e_east = pltpu.roll(e, LANES - 1, 1)
        if lane == tail:
            e_east = jnp.where(tile_lanes == LANES - 1, edge[:, 0:1], e_east)
        p = wet * (P1[:, lane] - COURANT * (e_east - e))
        p_west = pltpu.roll(p, 1, 1)
        if lane == head:
            p = jnp.where(tile_lanes == LANES - 1, P2[:, lane], p)
            p_west = jnp.where(tile_lanes == 0, edge[:, 1:2] - edge[:, 2:3] * e[:, 0:1], p_west)
        eta = wet * (e - COURANT * H[:, lane] * ((p - p_west) + across))
        E2[0:rows, lane] = jnp.where(tile_lanes == (LANES - 1 if lane == head else 0),
                                     E2[0:rows, lane], eta)
        P2[:, lane] = p

    receive_rows()

    @pl.when(level == 1)
    def _():
        flow[...] = jnp.zeros(flow.shape, f32)
        corner[...] = jnp.zeros(corner.shape, f32)

    @pl.when(level == 0)
    def _():
        fine_copy().wait_recv()
        receive_down()
        ends = slice(*ENDS)

        def above(at, own):
            to = fine[0, at, 0]
            return jnp.where(own, at, jnp.maximum(to, 0)), jnp.logical_or(own, to >= 0)

        def marked(h, at, ok):
            wet = jnp.logical_and(rdown[h, at, 32:40, :] > 0.0, ok)
            return jnp.where(wet, rdown[h, at, 24:32, :], DRY)

        def terms(h, at, x):
            to_w, to_e = fine[0, at, 2], fine[0, at, 3]
            w = kept(to_w >= 0, rdown[h, jnp.maximum(to_w, 0), ends, :])
            e = kept(to_e >= 0, rdown[h, jnp.maximum(to_e, 0), ends, :])
            p_edge = w[1:2, 5:6] + w[1:2, 6:7] * (w[1:2, 4:5] - x[0:1, 4:5])
            return p_edge, COURANT * e[0:1, 4:5]

        strips = ((half, patch, other, above(patch, half == 1), line[14], line[15]),
                  (other, south_at, half, above(south_at, half == 0),
                   rfirst[south_at, 32:40, :], rfirst[south_at, 40:48, :]))
        for n, (h, at, up, (up_at, up_ok), gain, index) in enumerate(strips):
            first_term, last_term = terms(h, at, rdown[h, at, ends, :])
            index = index.astype(jnp.int32)
            got = gather(marked(up, up_at, up_ok), index)
            eta_at = rdown[h, at, 0:8, :]
            change = jnp.where(got < 0.5 * DRY, got - COURANT * eta_at, 0.0)
            change += jnp.where(index == 0, first_term, 0.0)
            change += jnp.where(index == last, last_term, 0.0)
            flow[2 * n] = gain * eta_at
            flow[2 * n + 1] = gain * (rdown[h, at, 8:16, :] + rdown[h, at, 16:24, :] * change)

        def spread(v):
            return jnp.broadcast_to(v, (1, LANES))

        row_ids = lax.broadcasted_iota(jnp.int32, (chunks, LANES), 0)
        for n, at, r in ((0, west_at, 1), (1, east_at, 0)):
            x = rdown[half, at, ends, :]
            first_term, last_term = terms(half, at, x)
            up_at, up_ok = above(at, half == 1)
            one = slice(r, r + 1)
            index = spread(x[one, 12:13]).astype(jnp.int32)
            inside = jnp.broadcast_to(jnp.bitwise_and(index, LANES - 1), (chunks, LANES))
            which = lax.shift_right_logical(index, 7)
            got = jnp.take_along_axis(marked(other, up_at, up_ok), inside, axis=1,
                                      mode="promise_in_bounds")
            got = jnp.sum(jnp.where(row_ids == which, got, 0.0), axis=0, keepdims=True)
            wet = got < 0.5 * DRY
            value = jnp.where(wet, got, 0.0)
            value += jnp.where(index == 0, first_term, 0.0)
            value += jnp.where(index == last, last_term, 0.0)
            second = x[one, 9:10] + x[one, 10:11] * value - jnp.where(wet, x[one, 11:12], 0.0)
            for k, v in enumerate((spread(x[one, 7:8]), spread(x[one, 8:9]), second)):
                corner[3 * n + k:3 * n + k + 1, :] = v
        corner[6:7, :] = jnp.broadcast_to(rdown[other, sw_at, 41:42, 7:8], (1, LANES))
        corner[7:8, :] = jnp.broadcast_to(rdown[other, se_at, 40:41, 7:8], (1, LANES))

    @pl.when(half == 0)
    def _():
        stack[1:2, :] = rlast[nw_at, 25:26, :]
        stack[2:3, :] = rlast[ne_at, 24:25, :]
        stack[3:4, :] = rlast[sw_at, 25:26, :]
        stack[4:5, :] = rlast[se_at, 24:25, :]

    @pl.when(half == 1)
    def _():
        stack[1:2, :] = rfirst[nw_at, 25:26, :]
        stack[2:3, :] = rfirst[ne_at, 24:25, :]
        stack[3:4, :] = rfirst[sw_at, 25:26, :]
        stack[4:5, :] = rfirst[se_at, 24:25, :]

    n_ends = kept(north_ok, rlast[north_at, 24:25, :])
    nw_ends, ne_ends = kept(nw_ok, stack[1:2, :]), kept(ne_ok, stack[2:3, :])
    sw_ends, se_ends = kept(sw_ok, stack[3:4, :]), kept(se_ok, stack[4:5, :])
    sw_eta = sw_ends[:, 4:5] + kept(sw_ok, corner[6:7, 0:1])
    se_eta = se_ends[:, 4:5] + kept(se_ok, corner[7:8, 0:1])

    e_below = kept(south_ok, rfirst[south_at, 0:8, :] + flow[2])
    khm = kept(south_ok, rfirst[south_at, 16:24, :])
    m = (khm > 0.0).astype(f32)
    km = COURANT * m
    push = km * (e_below - east_of(e_below, se_eta))
    p_out = sw_ends[:, 5:6] + sw_ends[:, 6:7] * (sw_eta - e_below[0:1, 0:1])
    flat = rfirst[south_at, 8:16, :] + push - west_of(push, p_out) + km * e_below
    below = kept(south_ok, m * e_below - khm * kept(south_ok, flat) + flow[3])
    e_here = e_first + flow[0]
    khm_n = kept(north_ok, rlast[north_at, 16:24, :])
    km_n = COURANT * (khm_n > 0.0).astype(f32)
    q_n = kept(north_ok, rlast[north_at, 8:16, :]) - km_n * e_here
    p_out = nw_ends[:, 3:4] - nw_ends[:, 2:3] * n_ends[:, 0:1]
    side = jnp.where(cell_ids == 0, p_out, 0.0)
    side += jnp.where(cell_ids == last, COURANT * ne_ends[:, 0:1], 0.0)
    e_n = kept(north_ok, rlast[north_at, 0:8, :]) - khm_n * (q_n - side)
    for n, x in enumerate((q_n + km_n * e_n, km_n, below, khm, flow[1])):
        line[n] = x
    line[5] = e_below
    line[6] = q_n
    for c in range(chunks):
        lane = slice(c * LANES, (c + 1) * LANES)
        E0[0:1, lane] += flow[0, c:c + 1, :]
        E0[rows:rows + 1, lane] = line[5, c:c + 1, :]
        Q1[7:8, lane] = line[6, c:c + 1, :]

    first_row, second_row, last_row = row_lane == 0, row_lane == 1, row_lane == rows - 1
    in1 = kept(west_ok, corner[0:1, :])
    in2 = kept(west_ok, corner[1:2, :])
    q_nw = nw_ends[:, 1:2] - nw_ends[:, 2:3] * (col_w[6:7, :] + in1)
    tip = m_w * in1 - khm_w * (col_w[7:8, :] * (in1 - in2) + km_w * in1 - q_nw)
    w_share = col_w[3:4, :] + jnp.where(first_row, km_w * in1, 0.0)
    w_eta = col_w[4:5, :] + jnp.where(first_row, tip + kept(west_ok, corner[2:3, :]), 0.0)
    w_eta += jnp.where(last_row, khm_w * km_w * sw_eta, 0.0)
    w_eta += jnp.where(second_row, khm_w * km_w[:, 0:1] * in1, 0.0)
    in1 = kept(east_ok, corner[3:4, :])
    in2 = kept(east_ok, corner[4:5, :])
    q_ne = ne_ends[:, 1:2] - ne_ends[:, 2:3] * (col_e[0:1, :] + in1)
    tip = m_e * in1 + khm_e * (km_e * (in2 - in1) - km_e * in1 + q_ne)
    x_eta = col_e[0:1, :] + jnp.where(first_row, in1, 0.0)
    x_next = col_e[1:2, :] + jnp.where(first_row, tip + kept(east_ok, corner[5:6, :]), 0.0)
    x_next += jnp.where(last_row, khm_e * km_e * se_eta, 0.0)
    x_next += jnp.where(second_row, khm_e * km_e[:, 0:1] * in1, 0.0)
    for n, v in ((0, x_eta), (1, w_share), (3, w_eta), (5, x_next)):
        tmp[n:n + 1, :] = v
    halo = jnp.transpose(tmp[...])
    for r in (0, end):
        at = slice(r, r + BLOCK)
        step_rows(r, E0, P0, Q0, H, W, halo, E1, P1, Q1)
        next_halo(at, halo[at, :], E0[at, head], P1[at, tail])
    for c in range(chunks):
        lane = slice(c * LANES, (c + 1) * LANES)
        e1 = E1[0:1, lane] + line[4, c:c + 1, :]
        E1[0:1, lane] = e1
        E1[rows:rows + 1, lane] = line[2, c:c + 1, :] + line[3, c:c + 1, :] * Q1[rows + 7:rows + 8, lane]
        Q2[7:8, lane] = line[0, c:c + 1, :] - line[1, c:c + 1, :] * e1
    send_columns(lambda copy: copy.wait_send())
    send_rows(lambda copy: copy.wait_send())
    send_down(lambda copy: copy.wait_send())

    @pl.when(level == 1)
    def _():
        fine_copy().wait_send()


def two_level(mesh, adjoint_height, adjoint_momenta, depth, wet_mask, adjacency, nest_gain, nest_index):
    patches = mesh.shape["patch"]
    rows, cols = adjoint_height.shape[1:]
    chunks = cols // LANES
    f32 = jnp.float32
    anywhere = pl.BlockSpec(memory_space=pl.ANY)
    v = pltpu.VMEM
    dma = pltpu.SemaphoreType.DMA
    whole = (v((rows + 8, cols), f32), v((rows, cols), f32), v((rows + 8, cols), f32))
    scratch = [
        pltpu.SMEM(adjacency.shape, jnp.int32), pltpu.SMEM(adjacency.shape, jnp.int32),
        *whole,
        v(nest_gain.shape, f32), v(nest_index.shape, jnp.int32),
        v((16, chunks, LANES), f32), v((16, LANES), f32), v((rows + 8, LANES), f32),
        v((48, LANES), f32), v((32, LANES), f32), v((48, LANES), f32), v((8, LANES), f32),
        v((4, chunks, LANES), f32), v((8, LANES), f32), v((8, LANES), f32),
        dma((28,)), dma((5, patches)), dma((3, patches)), dma((2, patches)), dma((2,)),
        v((patches, 48, LANES), f32), v((patches, 32, LANES), f32), v((patches, 8, LANES), f32),
        v((2, patches, 48, LANES), f32),
    ]
    here = pl.BlockSpec(memory_space=pltpu.VMEM)
    state = pl.pallas_call(
        functools.partial(swap, patches, rows, cols),
        out_shape=(*whole, v((rows, cols), f32), v((rows, cols), jnp.int32), v((rows, 8), f32), *whole),
        in_specs=[anywhere] * 7,
        out_specs=(here,) * 9,
        scratch_shapes=scratch,
        compiler_params=pltpu.CompilerParams(collective_id=0, has_side_effects=True,
                                             vmem_limit_bytes=14 << 20),
    )(*[pltpu.with_memory_space_constraint(x, pltpu.HBM) for x in (
        adjacency, adjoint_height, adjoint_momenta, depth, wet_mask, nest_gain, nest_index)])
    state = [pltpu.with_memory_space_constraint(x, pltpu.VMEM) for x in state]
    return pl.pallas_call(
        functools.partial(settle, rows),
        out_shape=(jax.ShapeDtypeStruct(adjoint_height.shape, f32),
                   jax.ShapeDtypeStruct(adjoint_momenta.shape, f32)),
        in_specs=[here] * 9,
        out_specs=(anywhere, anywhere),
        scratch_shapes=[*whole, dma((9,))],
        compiler_params=pltpu.CompilerParams(vmem_limit_bytes=12 << 20),
    )(*state)


def solution(mesh):
    in_specs = (
        P(("parts", "level"), ("patch", "sub"), None),
        P(None, ("parts", "level"), ("patch", "sub"), None),
        P("level", ("patch", "sub"), None),
        P("level", ("patch", "sub"), None),
        P("level", None, None),
        P(None, ("patch", "sub")),
        P(None, ("patch", "sub")),
    )
    out_specs = (
        P(("parts", "level"), ("patch", "sub"), None),
        P(None, ("parts", "level"), ("patch", "sub"), None),
    )
    run = two_level if mesh.shape["level"] == 2 else body
    return jax.shard_map(functools.partial(run, mesh), mesh=mesh, in_specs=in_specs,
                         out_specs=out_specs, check_vma=False)
```

```python
import functools

import jax
import jax.numpy as jnp
from jax import lax
from jax.experimental import pallas as pl
from jax.experimental.pallas import tpu as pltpu
from jax.sharding import PartitionSpec as P

STEPS = 2
COURANT = 0.45
LANES = 128
BLOCK = 8


def advance(r, E, Pm, Q, H, W, halo, E_to, P_to, Q_to):
    cols = Pm.shape[1]
    lane_ids = lax.broadcasted_iota(jnp.int32, (BLOCK, cols), 1)
    span = slice(r, r + BLOCK)
    e = E[span, :]
    wet = W[span, :].astype(jnp.float32)
    e_south = E[r + 1:r + 1 + BLOCK, :]
    e_east = pltpu.roll(e, cols - 1, 1)
    if halo is not None:
        e_east = jnp.where(lane_ids == cols - 1, halo[span, 0:1], e_east)
    p = wet * (Pm[span, :] - COURANT * (e_east - e))
    q = wet * (Q[8 + r:16 + r, :] - COURANT * (e_south - e))
    p_west = pltpu.roll(p, 1, 1)
    if halo is not None:
        p_edge = halo[span, 1:2] - COURANT * halo[span, 2:3] * e[:, 0:1]
        p_west = jnp.where(lane_ids == 0, p_edge, p_west)
    P_to[span, :] = p
    Q_to[8 + r:16 + r, :] = q
    q_north = Q_to[7 + r:15 + r, :]
    E_to[span, :] = wet * (e - COURANT * H[span, :] * ((p - p_west) + (q - q_north)))


def finish(rows, E, Pm, Q, H, W, halo, E2, P2, Q2, eta_out, mom_out, Ef, Pf, Qf, sems):
    cols = Pm.shape[1]
    end = rows - BLOCK
    mid = slice(BLOCK, end)
    head, tail = slice(0, LANES), slice(cols - LANES, cols)
    before, inner = slice(0, cols - LANES), slice(LANES, cols - LANES)
    stores = []

    def store(src, dst):
        copy = pltpu.make_async_copy(src, dst, sems.at[len(stores)])
        copy.start()
        stores.append(copy)

    eta_to, row_to, col_to = eta_out.at[0], mom_out.at[0, 0], mom_out.at[1, 0]
    store(Q2.at[BLOCK + 8:end + 8], col_to.at[mid])
    store(P2.at[mid, before], row_to.at[mid, before])
    store(E2.at[mid, inner], eta_to.at[mid, inner])
    edges = halo[...]
    lane_ids = lax.broadcasted_iota(jnp.int32, (end - BLOCK, LANES), 1)

    across = Q2[BLOCK + 8:end + 8, head] - Q2[BLOCK + 7:end + 7, head]
    e = E[mid, head]
    wet = W[mid, head].astype(jnp.float32)
    p_edge = edges[mid, 1:2] - COURANT * edges[mid, 2:3] * e[:, 0:1]
    fixed = wet * (e - COURANT * H[mid, head] * ((P2[mid, head] - p_edge) + across))
    Ef[mid, head] = jnp.where(lane_ids == 0, fixed, E2[mid, head])
    store(Ef.at[mid, head], eta_to.at[mid, head])

    across = Q2[BLOCK + 8:end + 8, tail] - Q2[BLOCK + 7:end + 7, tail]
    e = E[mid, tail]
    wet = W[mid, tail].astype(jnp.float32)
    p = wet * (Pm[mid, tail] - COURANT * (edges[mid, 0:1] - e))
    p = jnp.where(lane_ids == LANES - 1, p, P2[mid, tail])
    Pf[mid, tail] = p
    store(Pf.at[mid, tail], row_to.at[mid, tail])
    fixed = wet * (e - COURANT * H[mid, tail] * ((p - pltpu.roll(p, 1, 1)) + across))
    Ef[mid, tail] = jnp.where(lane_ids == LANES - 1, fixed, E2[mid, tail])
    store(Ef.at[mid, tail], eta_to.at[mid, tail])

    for r in (0, end):
        Qf[7 + r:8 + r, :] = (Q if r == 0 else Q2)[7 + r:8 + r, :]
        advance(r, E, Pm, Q, H, W, edges, Ef, Pf, Qf)
        at = slice(r, r + BLOCK)
        store(Pf.at[at], row_to.at[at])
        store(Qf.at[8 + r:16 + r], col_to.at[at])
        store(Ef.at[at], eta_to.at[at])
    for copy in stores:
        copy.wait()


def exchange(patches, levels, rows, cols,
             adj_hbm, eta_hbm, mom_hbm, depth_hbm, wet_hbm, gain_hbm, table_hbm,
             E1, P1, Q1, H, W, halo_out, E2, P2, Q2,
             adj, E0, P0, Q0, gain_v, table_v, f8, idx8, gain8, tmp,
             sfirst, slast, scol, sinf, sew,
             rown, in_sems, send_sems, recv_sems, own_sems, *landing):
    rfirst, rlast, rcol, rnbr, rew = (landing[n * STEPS:(n + 1) * STEPS] for n in range(5))
    fields = ((E0, P0, Q0), (E1, P1, Q1))
    patch = lax.axis_index("patch")
    level = lax.axis_index("level")
    half = lax.axis_index("sub")
    chunks = cols // LANES
    other = 1 - half

    loads = [
        pltpu.make_async_copy(eta_hbm.at[0], E0.at[0:rows], in_sems.at[0]),
        pltpu.make_async_copy(mom_hbm.at[0, 0], P0, in_sems.at[1]),
        pltpu.make_async_copy(mom_hbm.at[1, 0], Q0.at[8:8 + rows], in_sems.at[2]),
        pltpu.make_async_copy(wet_hbm.at[0], W, in_sems.at[3]),
        pltpu.make_async_copy(table_hbm, table_v, in_sems.at[4]),
        pltpu.make_async_copy(gain_hbm, gain_v, in_sems.at[5]),
        pltpu.make_async_copy(adj_hbm, adj, in_sems.at[6]),
        pltpu.make_async_copy(depth_hbm.at[0], H, in_sems.at[7]),
    ]
    barrier = pltpu.get_barrier_semaphore()

    peers = [patch] + [lax.rem(patch + d, patches) for d in range(1, patches)]

    def greet(d, h, lev):
        pl.semaphore_signal(barrier, inc=1, device_id={
            "patch": peers[d], "sub": h, "level": lev},
            device_id_type=pl.DeviceIdType.MESH)

    for d in range(patches - 1, -1, -1):
        greet(d, other, level)
        if d:
            greet(d, half, level)

    @pl.when(level > 0)
    def _():
        for d in range(patches):
            greet(d, half, level - 1)
            greet(d, other, level - 1)

    @pl.when(level < levels - 1)
    def _():
        for d in range(patches):
            greet(d, half, level + 1)
            greet(d, other, level + 1)

    for load in loads:
        load.start()

    for load in loads[:7]:
        load.wait()

    lower = jnp.maximum(level - 1, 0)
    for c in range(chunks):
        lane = slice(c * LANES, (c + 1) * LANES)
        index, gain = table_v[0:1, lane], gain_v[0:1, lane]
        for lev in range(1, levels - 1):
            index = jnp.where(lower == lev, table_v[lev:lev + 1, lane], index)
            gain = jnp.where(lower == lev, gain_v[lev:lev + 1, lane], gain)
        idx8[c:c + 1, :] = index
        gain8[c:c + 1, :] = gain

    def remote(t, kind, src, buf, slot, d, h, lev):
        return pltpu.make_async_remote_copy(
            src_ref=src, dst_ref=buf, send_sem=send_sems.at[t, kind, d],
            recv_sem=recv_sems.at[t, kind, slot],
            device_id={"patch": peers[d], "sub": h, "level": lev},
            device_id_type=pl.DeviceIdType.MESH)

    def last_part(t):
        return slice(0, 2) if t == 0 else slice(t + 1, t + 2)

    def column_copy(t, slot, d):
        return remote(t, 0, scol.at[t, 0:3], rcol[t].at[slot, 0:3], slot, d, half, level)

    def first_copy(t, slot, d):
        return remote(t, 1, sfirst.at[t], rfirst[t].at[slot], slot, d, other, level)

    def last_copy(t, slot, d):
        part = last_part(t)
        return remote(t, 2, slast.at[part], rlast[t].at[slot], slot, d, other, level)

    def beside_copy(t, slot, d):
        return remote(t, 3, sinf.at[t], rnbr[t].at[slot], slot, d, other, lower)

    def ends_copy(t, slot, d):
        return remote(t, 4, sew.at[t], rew[t].at[slot], slot, d, half, lower)

    def per_half(across, inside, act):
        @pl.when(half == across)
        def _():
            for d in range(1, patches):
                act(d)

        @pl.when(half == inside)
        def _():
            act(0)

    def own_copy(t):
        return pltpu.make_async_remote_copy(
            src_ref=sinf.at[t], dst_ref=rown.at[t], send_sem=own_sems.at[t, 0],
            recv_sem=own_sems.at[t, 1], device_id={"level": lower},
            device_id_type=pl.DeviceIdType.MESH)

    def make_inflow(t):
        E = fields[t][0]
        for c in range(chunks):
            f8[c:c + 1, :] = E[0:1, c * LANES:(c + 1) * LANES]
        index = idx8[...]
        inside = jnp.bitwise_and(index, LANES - 1)
        which = lax.shift_right_logical(index, 7)
        picked = jnp.zeros((chunks, LANES), jnp.float32)
        for c in range(chunks):
            source = jnp.broadcast_to(f8[c:c + 1, :], (chunks, LANES))
            got = jnp.take_along_axis(source, inside, axis=1, mode="promise_in_bounds")
            picked = jnp.where(which == c, got, picked)
        inflow = gain8[...] * picked
        sinf[t] = inflow
        sew[t, 0:1, :] = inflow[0:1, :]
        sew[t, 1:2, :] = pltpu.roll(inflow[chunks - 1:chunks, :], 1, 1)

    def send_inflow(t):
        own_copy(t).start()
        per_half(0, 1, lambda d: beside_copy(t, patch, d).start())
        for d in range(1, patches):
            ends_copy(t, patch, d).start()

    def inflow_waits(t):
        per_half(1, 0, lambda d: beside_copy(t, peers[d], d).wait_recv())
        for d in range(1, patches):
            ends_copy(t, peers[d], d).wait_recv()

    def inflow_send_waits(t):
        own_copy(t).wait_send()
        per_half(0, 1, lambda d: beside_copy(t, patch, d).wait_send())
        for d in range(1, patches):
            ends_copy(t, patch, d).wait_send()

    def send_halos(t, act):
        send_rows(t, act)
        send_columns(t, act)

    def send_columns(t, act):
        for d in range(1, patches):
            act(column_copy(t, patch, d))

    def send_rows(t, act):
        @pl.when(half == 0)
        def _():
            for d in range(1, patches):
                act(first_copy(t, patch, d))
            act(last_copy(t, patch, 0))

        @pl.when(half == 1)
        def _():
            for d in range(1, patches):
                act(last_copy(t, patch, d))
            act(first_copy(t, patch, 0))

    def receive_halos(t):
        @pl.when(half == 0)
        def _():
            first_copy(t, peers[0], 0).wait_recv()
            for d in range(1, patches):
                last_copy(t, peers[d], d).wait_recv()

        @pl.when(half == 1)
        def _():
            last_copy(t, peers[0], 0).wait_recv()
            for d in range(1, patches):
                first_copy(t, peers[d], d).wait_recv()

        for d in range(1, patches):
            column_copy(t, peers[d], d).wait_recv()

    north = adj[0, patch, 0]
    south = adj[0, patch, 1]
    west = adj[0, patch, 2]
    east = adj[0, patch, 3]
    south_ok = jnp.logical_or(half == 0, south >= 0)
    north_ok = jnp.logical_or(half == 1, north >= 0)
    south_at = jnp.where(half == 0, patch, jnp.maximum(south, 0))
    north_at = jnp.where(half == 1, patch, jnp.maximum(north, 0))
    west_at = jnp.maximum(west, 0)
    east_at = jnp.maximum(east, 0)
    finer = level < levels - 1
    lane_ids = lax.broadcasted_iota(jnp.int32, (rows, LANES), 1)
    first_lane = lax.broadcasted_iota(jnp.int32, (1, LANES), 1) == 0
    tail = slice(cols - LANES, cols)
    end = rows - 1

    def make_messages(t):
        @pl.when(level == levels - 1)
        def _():
            make_inflow(t)

        make_rows(t)
        make_columns(t)

    def make_rows(t):
        E, Pm, Q = fields[t]
        sfirst[t] = E[0:1, :]
        wet_row = W[end:rows, :].astype(jnp.float32)
        slast[t + 1] = wet_row * (Q[8 + end:8 + rows, :] + COURANT * E[end:rows, :])
        if t == 0:
            slast[0] = wet_row

    def make_columns(t):
        E, Pm, Q = fields[t]
        wet_tail = W[:, tail].astype(jnp.float32)
        share = wet_tail * (Pm[:, tail] + COURANT * E[0:rows, tail])
        mixed = jnp.where(lane_ids == 0, E[0:rows, 0:LANES],
                          jnp.where(lane_ids == 1, pltpu.roll(share, 2, 1),
                                    pltpu.roll(wet_tail, 3, 1)))
        scol[t] = jnp.transpose(mixed[:, 0:8])

    def send_messages(t):
        @pl.when(level == levels - 1)
        def _():
            send_inflow(t)

        send_halos(t, lambda copy: copy.start())

    def receive(t):
        E, Pm, Q = fields[t]

        @pl.when(finer)
        def _():
            own_copy(t).wait_recv()
            for c in range(chunks):
                lane = slice(c * LANES, (c + 1) * LANES)
                E[0:1, lane] += rown[t, c:c + 1, :]

        if levels > 2:
            @pl.when(jnp.logical_and(level > 0, level < levels - 1))
            def _():
                make_inflow(t)
                send_inflow(t)

        receive_halos(t)

        @pl.when(finer)
        def _():
            inflow_waits(t)

        east_row = rcol[t][east_at][0:1, :]
        east_row += jnp.where(jnp.logical_and(first_lane, finer), rew[t][east_at][0:1, :], 0.0)
        west_cols = rcol[t][west_at]
        share = west_cols[1:2, :]
        wet_w = west_cols[2:3, :]
        share += jnp.where(jnp.logical_and(first_lane, finer),
                           COURANT * wet_w * rew[t][west_at][1:2, :], 0.0)
        tmp[0:1, :] = jnp.where(east >= 0, east_row, 0.0)
        tmp[1:2, :] = jnp.where(west >= 0, share, 0.0)
        tmp[2:3, :] = jnp.where(west >= 0, wet_w, 0.0)
        beside = rnbr[t][south_at]
        below = rfirst[t][south_at]
        for c in range(chunks):
            lane = slice(c * LANES, (c + 1) * LANES)
            value = below[:, lane] + jnp.where(finer, beside[c:c + 1, :], 0.0)
            E[rows:rows + 1, lane] = jnp.where(south_ok, value, 0.0)
        share_n = rlast[t][north_at, 1 if t == 0 else 0]
        wet_n = rlast[0][north_at, 0]
        Q_to = Q1
        Q_to[7:8, :] = jnp.where(north_ok, share_n - COURANT * wet_n * E[0:1, :], 0.0)
        return jnp.transpose(tmp[...])

    make_messages(0)
    sides = (level > 0).astype(jnp.int32) + (level < levels - 1).astype(jnp.int32)
    pl.semaphore_wait(barrier, 2 * patches - 1 + 2 * patches * sides)
    send_messages(0)
    loads[7].wait()
    for r in range(0, rows - BLOCK, BLOCK):
        advance(r, E0, P0, Q0, H, W, None, E1, P1, Q1)
    halo = receive(0)
    for r in (0, rows - BLOCK):
        advance(r, E0, P0, Q0, H, W, None, E1, P1, Q1)
    head = slice(0, LANES)
    e = E0[0:rows, head]
    wet = W[:, head].astype(jnp.float32)
    p_edge = halo[:, 1:2] - COURANT * halo[:, 2:3] * e[:, 0:1]
    across = Q1[8:8 + rows, head] - Q1[7:7 + rows, head]
    fixed = wet * (e - COURANT * H[:, head] * ((P1[:, head] - p_edge) + across))
    E1[0:rows, head] = jnp.where(lane_ids == 0, fixed, E1[0:rows, head])
    e = E0[0:rows, tail]
    wet = W[:, tail].astype(jnp.float32)
    p = wet * (P0[:, tail] - COURANT * (halo[:, 0:1] - e))
    p = jnp.where(lane_ids == LANES - 1, p, P1[:, tail])
    P1[:, tail] = p
    across = Q1[8:8 + rows, tail] - Q1[7:7 + rows, tail]
    fixed = wet * (e - COURANT * H[:, tail] * ((p - pltpu.roll(p, 1, 1)) + across))
    E1[0:rows, tail] = jnp.where(lane_ids == LANES - 1, fixed, E1[0:rows, tail])

    @pl.when(level == levels - 1)
    def _():
        make_inflow(1)
        send_inflow(1)

    make_rows(1)
    send_rows(1, lambda copy: copy.start())
    make_columns(1)
    send_columns(1, lambda copy: copy.start())
    for r in range(0, rows - BLOCK, BLOCK):
        advance(r, E1, P1, Q1, H, W, None, E2, P2, Q2)
    halo_out[...] = receive(1)
    for t in range(STEPS):
        send_halos(t, lambda copy: copy.wait_send())

        @pl.when(level > 0)
        def _():
            inflow_send_waits(t)


def body(mesh, adjoint_height, adjoint_momenta, depth, wet_mask, adjacency, nest_gain, nest_index):
    patches, levels = mesh.shape["patch"], mesh.shape["level"]
    rows, cols = adjoint_height.shape[1:]
    chunks = cols // LANES
    f32 = jnp.float32
    anywhere = pl.BlockSpec(memory_space=pl.ANY)
    v = pltpu.VMEM
    dma = pltpu.SemaphoreType.DMA
    whole = (v((rows + 8, cols), f32), v((rows, cols), f32), v((rows + 8, cols), f32))
    scratch = [
        pltpu.SMEM(adjacency.shape, jnp.int32),
        *whole,
        v(nest_gain.shape, f32), v(nest_index.shape, jnp.int32),
        v((chunks, LANES), f32), v((chunks, LANES), jnp.int32), v((chunks, LANES), f32),
        v((8, LANES), f32),
        v((STEPS, 1, cols), f32), v((STEPS + 1, 1, cols), f32), v((STEPS, 8, LANES), f32),
        v((STEPS, chunks, LANES), f32), v((STEPS, 2, LANES), f32),
        v((STEPS, chunks, LANES), f32),
        dma((8,)), dma((STEPS, 5, patches)), dma((STEPS, 5, patches)), dma((STEPS, 2)),
    ]
    scratch += [v((patches, 1, cols), f32)] * STEPS
    scratch += [v((patches, 2 if t == 0 else 1, 1, cols), f32) for t in range(STEPS)]
    scratch += [v((patches, 8, LANES), f32)] * STEPS
    scratch += [v((patches, chunks, LANES), f32)] * STEPS
    scratch += [v((patches, 2, LANES), f32)] * STEPS
    here = pl.BlockSpec(memory_space=pltpu.VMEM)
    state = pl.pallas_call(
        functools.partial(exchange, patches, levels, rows, cols),
        out_shape=(*whole, v((rows, cols), f32), v((rows, cols), jnp.int32), v((rows, 8), f32), *whole),
        in_specs=[anywhere] * 7,
        out_specs=(here,) * 9,
        scratch_shapes=scratch,
        compiler_params=pltpu.CompilerParams(collective_id=0, has_side_effects=True,
                                             vmem_limit_bytes=12 << 20),
    )(*[pltpu.with_memory_space_constraint(x, pltpu.HBM) for x in (
        adjacency, adjoint_height, adjoint_momenta, depth, wet_mask, nest_gain, nest_index)])
    state = [pltpu.with_memory_space_constraint(x, pltpu.VMEM) for x in state]
    return pl.pallas_call(
        functools.partial(finish, rows),
        out_shape=(jax.ShapeDtypeStruct(adjoint_height.shape, f32),
                   jax.ShapeDtypeStruct(adjoint_momenta.shape, f32)),
        in_specs=[here] * 9,
        out_specs=(anywhere, anywhere),
        scratch_shapes=[*whole, dma((12,))],
        compiler_params=pltpu.CompilerParams(vmem_limit_bytes=12 << 20),
    )(*state)


FULL, TAIL, ENDS = (0, 42), (24, 42), (40, 42)
DRY = 1e30


def step_rows(r, E, Pm, Q, H, W, edge, E_to, P_to, Q_to):
    cols = Pm.shape[1]
    lane_ids = lax.broadcasted_iota(jnp.int32, (BLOCK, cols), 1)
    span = slice(r, r + BLOCK)
    e = E[span, :]
    wet = W[span, :].astype(jnp.float32)
    e_south = E[r + 1:r + 1 + BLOCK, :]
    e_east = pltpu.roll(e, cols - 1, 1)
    if edge is not None:
        e_east = jnp.where(lane_ids == cols - 1, edge[:, 0:1], e_east)
    p = wet * (Pm[span, :] - COURANT * (e_east - e))
    q = wet * (Q[8 + r:16 + r, :] - COURANT * (e_south - e))
    p_west = pltpu.roll(p, 1, 1)
    if edge is not None:
        p_west = jnp.where(lane_ids == 0, edge[:, 1:2] - edge[:, 2:3] * e[:, 0:1], p_west)
    P_to[span, :] = p
    Q_to[8 + r:16 + r, :] = q
    q_north = Q_to[7 + r:15 + r, :]
    E_to[span, :] = wet * (e - COURANT * H[span, :] * ((p - p_west) + (q - q_north)))


def settle(rows, E, Pm, Q, H, W, halo, E2, P2, Q2, eta_out, mom_out, Ef, Pf, Qf, sems):
    end = rows - BLOCK
    mid = slice(BLOCK, end)
    stores = []

    def store(src, dst):
        copy = pltpu.make_async_copy(src, dst, sems.at[len(stores)])
        copy.start()
        stores.append(copy)

    eta_to, row_to, col_to = eta_out.at[0], mom_out.at[0, 0], mom_out.at[1, 0]
    store(Q2.at[BLOCK + 8:end + 8], col_to.at[mid])
    store(P2.at[mid], row_to.at[mid])
    store(E2.at[mid], eta_to.at[mid])
    def ends(r):
        at = slice(r, r + BLOCK)
        step_rows(r, E, Pm, Q, H, W, halo[at, :], Ef, Pf, Qf)
        store(Pf.at[at], row_to.at[at])
        store(Qf.at[8 + r:16 + r], col_to.at[at])
        store(Ef.at[at], eta_to.at[at])

    for r in (0, end):
        Qf[7 + r:8 + r, :] = Q2[7 + r:8 + r, :]
        ends(r)
    for copy in stores:
        copy.wait()


def swap(patches, rows, cols,
         adj_hbm, eta_hbm, mom_hbm, depth_hbm, wet_hbm, gain_hbm, table_hbm,
         E1, P1, Q1, H, W, halo_out, E2, P2, Q2,
         adj, fine, E0, P0, Q0, gain_v, table_v, line, stack, qb, sfirst, slast, sdown, scol,
         tmp, in_sems, send_sems, recv_sems, down_sems, fine_sems,
         rfirst, rlast, rcol, rdown):
    f32 = jnp.float32
    patch = lax.axis_index("patch")
    level = lax.axis_index("level")
    half = lax.axis_index("sub")
    other = 1 - half
    chunks = cols // LANES
    last = cols - 1
    end = rows - BLOCK
    head, tail = slice(0, LANES), slice(cols - LANES, cols)
    inner = slice(LANES, cols - LANES)
    mid = slice(BLOCK, end)
    loads = []

    def load(src, dst):
        copy = pltpu.make_async_copy(src, dst, in_sems.at[len(loads)])
        copy.start()
        loads.append(copy)

    fields = ((eta_hbm.at[0], E0, 0), (mom_hbm.at[0, 0], P0, 0), (mom_hbm.at[1, 0], Q0, 8),
              (wet_hbm.at[0], W, 0), (depth_hbm.at[0], H, 0))

    def load_part(at, lane):
        for src, dst, shift in fields:
            load(src.at[at, lane], dst.at[at.start + shift:at.stop + shift, lane])

    barrier = pltpu.get_barrier_semaphore()
    peers = [patch] + [jnp.where(patch < d, d, d - 1) for d in range(1, patches)]

    def greet(d, h, lev):
        pl.semaphore_signal(barrier, inc=1, device_id={
            "patch": peers[d], "sub": h, "level": lev},
            device_id_type=pl.DeviceIdType.MESH)

    for d in range(1, patches):
        greet(d, other, level)
        greet(d, half, level)
    greet(0, other, level)

    @pl.when(level == 0)
    def _():
        for d in list(range(1, patches)) + [0]:
            greet(d, half, 1)
            greet(d, other, 1)

    for at in (slice(0, BLOCK), slice(end, rows)):
        load_part(at, slice(0, cols))
    load(adj_hbm, adj)
    load(table_hbm, table_v)
    load(gain_hbm, gain_v)
    n_rows = len(loads)

    for lane in (head, tail):
        load_part(mid, lane)
    n_tiles = len(loads)
    load_part(mid, inner)

    E0[rows:rows + 8, :] = jnp.zeros((8, cols), f32)
    qb[0:8, :] = jnp.zeros((8, LANES), f32)
    lane_ids = lax.broadcasted_iota(jnp.int32, (chunks, LANES), 1)
    cell_ids = lax.broadcasted_iota(jnp.int32, (chunks, LANES), 0) * LANES + lane_ids
    row_lane = lax.broadcasted_iota(jnp.int32, (1, LANES), 1)

    def east_of(x, beyond):
        y = pltpu.roll(x, LANES - 1, 1)
        y = jnp.where(lane_ids == LANES - 1, pltpu.roll(y, chunks - 1, 0), y)
        return jnp.where(cell_ids == last, beyond, y)

    def west_of(x, beyond):
        y = pltpu.roll(x, 1, 1)
        y = jnp.where(lane_ids == 0, pltpu.roll(y, 1, 0), y)
        return jnp.where(cell_ids == 0, beyond, y)

    def gather(x, index):
        inside = jnp.bitwise_and(index, LANES - 1)
        which = lax.shift_right_logical(index, 7)
        picked = jnp.zeros((chunks, LANES), f32)
        for c in range(chunks):
            source = jnp.broadcast_to(x[c:c + 1, :], (chunks, LANES))
            got = jnp.take_along_axis(source, inside, axis=1, mode="promise_in_bounds")
            picked = jnp.where(which == c, got, picked)
        return picked

    for copy in loads[:n_rows]:
        copy.wait()

    def lines(n, ref, r):
        for c in range(chunks):
            line[n, c:c + 1, :] = ref[r:r + 1, c * LANES:(c + 1) * LANES].astype(f32)

    for n, (ref, r) in enumerate((
            (E0, 0), (E0, 1), (P0, 0), (Q0, 8), (W, 0), (H, 0),
            (E0, rows - 1), (P0, rows - 1), (Q0, rows + 7), (W, rows - 1), (H, rows - 1))):
        lines(n, ref, r)

    e, p, q, m = line[0], line[2], line[3], line[4]
    e_first = e
    km = COURANT * m
    khm = km * line[5]
    mp = m * p
    stack[4:5, :] = jnp.where(row_lane < 64, e[0:1, :], e[chunks - 1:chunks, :])
    stack[5:6, :] = jnp.where(row_lane < 64, mp[0:1, :], mp[chunks - 1:chunks, :])
    stack[6:7, :] = jnp.where(row_lane < 64, km[0:1, :], km[chunks - 1:chunks, :])
    el, ml = line[6], line[9]
    kml = COURANT * ml
    khml = kml * line[10]
    aq = ml * line[8] + kml * el
    ap = ml * line[7] + kml * el
    sdown[24:32, :] = aq
    sdown[32:40, :] = khml
    for n, x in enumerate((el, aq, kml, ap)):
        stack[n:n + 1, :] = jnp.where(row_lane < 64, x[0:1, :], x[chunks - 1:chunks, :])
    stack[13:16, :] = jnp.zeros((3, LANES), f32)

    @pl.when(level == 0)
    def _():
        stack[7:13, :] = jnp.zeros((6, LANES), f32)

    for c in range(chunks):
        lane = slice(c * LANES, (c + 1) * LANES)
        line[14, c:c + 1, :] = gain_v[0:1, lane]
        line[15, c:c + 1, :] = table_v[0:1, lane].astype(f32)
    gain, index = line[14], line[15].astype(jnp.int32)

    @pl.when(level == 1)
    def _():
        p_new = mp - km * (east_of(e, 0.0) - e)
        q_new = m * q - km * (line[1] - e)
        there = m * e - khm * (p_new - west_of(p_new, 0.0) + q_new)
        parts = [gather(x, index) for x in (e, there, khm)]
        for n, x in enumerate(parts):
            sdown[8 * n:8 * n + 8, :] = x
        inflow = gain * parts[0]
        rows_of = (inflow, None, gain * parts[1], gain * parts[2],
                   COURANT * parts[2] * inflow, line[15])
        for n, x in enumerate(rows_of):
            if x is None:
                low = pltpu.roll(inflow, LANES - 1, 1)[0:1, :]
                high = pltpu.roll(inflow, 1, 1)[chunks - 1:chunks, :]
            else:
                low, high = x[0:1, :], x[chunks - 1:chunks, :]
            stack[7 + n:8 + n, :] = jnp.where(row_lane < 64, low, high)

    turned = jnp.transpose(stack[...])
    for ref, at in ((sfirst, 24), (slast, 24), (sdown, 40)):
        ref[at:at + 1, 0:16] = turned[0:1, :]
        ref[at + 1:at + 2, 0:16] = turned[LANES - 1:LANES, :]

    def row_messages():
        for n, (ref, r) in enumerate(((E0, rows - 2), (Q0, rows + 6), (W, rows - 2))):
            lines(11 + n, ref, r)
        sfirst[0:8, :] = e
        sfirst[8:16, :] = mp - west_of(mp, 0.0) + (m * q - km * line[1])
        sfirst[16:24, :] = khm
        sfirst[32:40, :] = gain
        sfirst[40:48, :] = line[15]
        p_new = ml * line[7] - kml * (east_of(el, 0.0) - el)
        q_above = line[13] * (line[12] - COURANT * (el - line[11]))
        slast[0:8, :] = ml * el - khml * (p_new - west_of(p_new, 0.0) - q_above)
        slast[8:16, :] = aq
        slast[16:24, :] = khml

    tile_lanes = lax.broadcasted_iota(jnp.int32, (rows, LANES), 1)

    def column_message():
        for copy in loads[n_rows:n_tiles]:
            copy.wait()
        mixed = None
        for lane in (head, tail):
            e = E0[0:rows, lane]
            m = W[:, lane].astype(f32)
            km = COURANT * m
            khm = km * H[:, lane]
            p_new = m * P0[:, lane] - km * (pltpu.roll(e, LANES - 1, 1) - e)
            q_new = m * Q0[8:8 + rows, lane] - km * (E0[1:rows + 1, lane] - e)
            qb[8:8 + rows, :] = q_new
            across = q_new - qb[7:7 + rows, :]
            if lane == head:
                parts = ((e, 0), (m * e - khm * (p_new + across), 0), (khm, 0))
            else:
                parts = ((m * P0[:, lane] + km * e, LANES - 1),
                         (m * e - khm * (across - pltpu.roll(p_new, 1, 1)), LANES - 1),
                         (khm, LANES - 1), (e, LANES - 1), (km, LANES - 2))
            for n, (x, at) in enumerate(parts):
                to = n + (0 if lane == head else 3)
                moved = pltpu.roll(x, (to - at) % LANES, 1) if (to - at) % LANES else x
                mixed = moved if mixed is None else jnp.where(tile_lanes == to, moved, mixed)
        scol[...] = jnp.transpose(mixed[:, 0:8])

    def remote(kind, src, dst, recv_sem, d, h, lev):
        return pltpu.make_async_remote_copy(
            src_ref=src, dst_ref=dst, send_sem=send_sems.at[kind, d], recv_sem=recv_sem,
            device_id={"patch": peers[d], "sub": h, "level": lev},
            device_id_type=pl.DeviceIdType.MESH)

    def column_copy(slot, d):
        return remote(0, scol, rcol.at[slot], recv_sems.at[0, slot], d, half, level)

    def first_copy(slot, d, size):
        return remote(1, sfirst.at[0:size], rfirst.at[slot, 0:size], recv_sems.at[1, slot], d, other, level)

    def by_level(act):
        for lev, size in enumerate((48, 26)):
            @pl.when(level == lev)
            def _():
                act(size)

    def last_copy(slot, d):
        return remote(2, slast.at[0:26], rlast.at[slot, 0:26], recv_sems.at[2, slot], d, other, level)

    def down_copy(part, from_half, slot, d, h):
        at = slice(*part)
        return remote(3 + h, sdown.at[at], rdown.at[from_half, slot, at],
                      down_sems.at[from_half, slot], d, h, 1 - level)

    def fine_copy():
        return pltpu.make_async_remote_copy(
            src_ref=adj, dst_ref=fine, send_sem=fine_sems.at[0], recv_sem=fine_sems.at[1],
            device_id={"level": 1 - level}, device_id_type=pl.DeviceIdType.MESH)

    far = list(range(1, patches)) + [0]

    def send_rows(act):
        @pl.when(half == 0)
        def _():
            def firsts(size):
                for d in range(1, patches):
                    act(first_copy(patch, d, size))

            by_level(firsts)
            act(last_copy(patch, 0))

        @pl.when(half == 1)
        def _():
            for d in range(1, patches):
                act(last_copy(patch, d))
            by_level(lambda size: act(first_copy(patch, 0, size)))

    def send_down(act):
        @pl.when(jnp.logical_and(level == 1, half == 0))
        def _():
            for d in far:
                act(down_copy(ENDS if d else FULL, 0, patch, d, 0))
                act(down_copy(FULL if d else TAIL, 0, patch, d, 1))

        @pl.when(jnp.logical_and(level == 1, half == 1))
        def _():
            for d in far:
                act(down_copy(TAIL if d else FULL, 1, patch, d, 0))
                act(down_copy(TAIL if d else FULL, 1, patch, d, 1))

    def send_columns(act):
        for d in range(1, patches):
            act(column_copy(patch, d))

    def receive_columns():
        for d in range(1, patches):
            column_copy(peers[d], d).wait_recv()

    def receive_rows():
        @pl.when(half == 0)
        def _():
            by_level(lambda size: first_copy(patch, 0, size).wait_recv())
            for d in range(1, patches):
                last_copy(peers[d], d).wait_recv()

        @pl.when(half == 1)
        def _():
            def firsts(size):
                for d in range(1, patches):
                    first_copy(peers[d], d, size).wait_recv()

            last_copy(patch, 0).wait_recv()
            by_level(firsts)

    def receive_down():
        @pl.when(jnp.logical_and(level == 0, half == 0))
        def _():
            for d in far:
                down_copy(TAIL if d else FULL, 1, peers[d], d, 0).wait_recv()
                down_copy(ENDS if d else FULL, 0, peers[d], d, 0).wait_recv()

        @pl.when(jnp.logical_and(level == 0, half == 1))
        def _():
            for d in far:
                down_copy(TAIL if d else FULL, 1, peers[d], d, 1).wait_recv()
                down_copy(FULL if d else TAIL, 0, peers[d], d, 1).wait_recv()

    column_message()

    @pl.when(level == 0)
    def _():
        row_messages()

    pl.semaphore_wait(barrier, 2 * patches - 1 + 2 * patches * level)

    @pl.when(level == 1)
    def _():
        fine_copy().start()

    send_down(lambda copy: copy.start())

    @pl.when(level == 1)
    def _():
        row_messages()

    send_columns(lambda copy: copy.start())
    send_rows(lambda copy: copy.start())

    for copy in loads[n_tiles:]:
        copy.wait()
    for r in range(0, rows, BLOCK):
        step_rows(r, E0, P0, Q0, H, W, None, E1, P1, Q1)
    for r in range(0, end, BLOCK):
        step_rows(r, E1, P1, Q1, H, W, None, E2, P2, Q2)

    north, south = adj[0, patch, 0], adj[0, patch, 1]
    west, east = adj[0, patch, 2], adj[0, patch, 3]
    south_ok = jnp.logical_or(half == 0, south >= 0)
    north_ok = jnp.logical_or(half == 1, north >= 0)
    south_at = jnp.where(half == 0, patch, jnp.maximum(south, 0))
    north_at = jnp.where(half == 1, patch, jnp.maximum(north, 0))
    west_ok, east_ok = west >= 0, east >= 0
    west_at, east_at = jnp.maximum(west, 0), jnp.maximum(east, 0)

    def beyond(at, ok, side):
        to = adj[0, at, side]
        return jnp.maximum(to, 0), jnp.logical_and(ok, to >= 0)

    nw_at, nw_ok = beyond(north_at, north_ok, 2)
    ne_at, ne_ok = beyond(north_at, north_ok, 3)
    sw_at, sw_ok = beyond(south_at, south_ok, 2)
    se_at, se_ok = beyond(south_at, south_ok, 3)

    def kept(ok, x):
        return jnp.where(ok, x, 0.0)

    receive_columns()
    col_w, col_e = kept(west_ok, rcol[west_at]), kept(east_ok, rcol[east_at])
    khm_w, khm_e = col_w[5:6, :], col_e[2:3, :]
    m_w, m_e = (khm_w > 0.0).astype(f32), (khm_e > 0.0).astype(f32)
    km_w, km_e = COURANT * m_w, COURANT * m_e
    for n, v in enumerate((col_e[0:1, :], col_w[3:4, :], km_w, col_w[4:5, :], khm_w, col_e[1:2, :], khm_e)):
        tmp[n:n + 1, :] = v
    tmp[7:8, :] = jnp.zeros((1, LANES), f32)
    halo = jnp.transpose(tmp[...])

    def next_halo(at, halo, e, p):
        p_edge = halo[:, 1:2] - halo[:, 2:3] * e[:, 0:1]
        halo_out[at, 0:1] = halo[:, 5:6] + halo[:, 6:7] * p[:, LANES - 1:LANES]
        halo_out[at, 1:2] = p_edge + halo[:, 2:3] * (halo[:, 3:4] - halo[:, 4:5] * p_edge)
        halo_out[at, 2:3] = halo[:, 2:3]

    e_head = E0[0:rows, head]
    wet_head = W[:, head].astype(f32)
    p_edge = halo[:, 1:2] - halo[:, 2:3] * e_head[:, 0:1]
    across = Q1[8:8 + rows, head] - Q1[7:7 + rows, head]
    fixed = wet_head * (e_head - COURANT * H[:, head] * ((P1[:, head] - p_edge) + across))
    E1[0:rows, head] = jnp.where(tile_lanes == 0, fixed, E1[0:rows, head])
    e = E0[0:rows, tail]
    wet_tail = W[:, tail].astype(f32)
    p = wet_tail * (P0[:, tail] - COURANT * (halo[:, 0:1] - e))
    p = jnp.where(tile_lanes == LANES - 1, p, P1[:, tail])
    P1[:, tail] = p
    across = Q1[8:8 + rows, tail] - Q1[7:7 + rows, tail]
    fixed = wet_tail * (e - COURANT * H[:, tail] * ((p - pltpu.roll(p, 1, 1)) + across))
    E1[0:rows, tail] = jnp.where(tile_lanes == LANES - 1, fixed, E1[0:rows, tail])
    next_halo(slice(0, rows), halo, e_head, p)
    edge = halo_out[...]
    for lane in (head, tail):
        e = E1[0:rows, lane]
        wet = wet_head if lane == head else wet_tail
        q = wet * (Q1[8:8 + rows, lane] - COURANT * (E1[1:rows + 1, lane] - e))
        Q2[8:8 + rows, lane] = q
        across = q - Q2[7:7 + rows, lane]
        e_east = pltpu.roll(e, LANES - 1, 1)
        if lane == tail:
            e_east = jnp.where(tile_lanes == LANES - 1, edge[:, 0:1], e_east)
        p = wet * (P1[:, lane] - COURANT * (e_east - e))
        p_west = pltpu.roll(p, 1, 1)
        if lane == head:
            p = jnp.where(tile_lanes == LANES - 1, P2[:, lane], p)
            p_west = jnp.where(tile_lanes == 0, edge[:, 1:2] - edge[:, 2:3] * e[:, 0:1], p_west)
        eta = wet * (e - COURANT * H[:, lane] * ((p - p_west) + across))
        E2[0:rows, lane] = jnp.where(tile_lanes == (LANES - 1 if lane == head else 0),
                                     E2[0:rows, lane], eta)
        P2[:, lane] = p

    receive_rows()

    def complete(coarse):
        flow = [jnp.zeros((chunks, LANES), f32)] * 4
        corner = [jnp.zeros((1, 1), f32)] * 8
        if coarse:
            ends = slice(*ENDS)

            def above(at, own):
                to = fine[0, at, 0]
                return jnp.where(own, at, jnp.maximum(to, 0)), jnp.logical_or(own, to >= 0)

            def marked(h, at, ok):
                wet = jnp.logical_and(rdown[h, at, 32:40, :] > 0.0, ok)
                return jnp.where(wet, rdown[h, at, 24:32, :], DRY)

            def terms(h, at, x):
                to_w, to_e = fine[0, at, 2], fine[0, at, 3]
                w = kept(to_w >= 0, rdown[h, jnp.maximum(to_w, 0), ends, :])
                e = kept(to_e >= 0, rdown[h, jnp.maximum(to_e, 0), ends, :])
                p_edge = w[1:2, 5:6] + w[1:2, 6:7] * (w[1:2, 4:5] - x[0:1, 4:5])
                return p_edge, COURANT * e[0:1, 4:5]

            strips = ((half, patch, other, above(patch, half == 1), line[14], line[15]),
                      (other, south_at, half, above(south_at, half == 0),
                       rfirst[south_at, 32:40, :], rfirst[south_at, 40:48, :]))
            for n, (h, at, up, (up_at, up_ok), gain, index) in enumerate(strips):
                first_term, last_term = terms(h, at, rdown[h, at, ends, :])
                index = index.astype(jnp.int32)
                got = gather(marked(up, up_at, up_ok), index)
                eta_at = rdown[h, at, 0:8, :]
                change = jnp.where(got < 0.5 * DRY, got - COURANT * eta_at, 0.0)
                change += jnp.where(index == 0, first_term, 0.0)
                change += jnp.where(index == last, last_term, 0.0)
                flow[2 * n] = gain * eta_at
                flow[2 * n + 1] = gain * (rdown[h, at, 8:16, :] + rdown[h, at, 16:24, :] * change)

            def spread(v):
                return jnp.broadcast_to(v, (1, LANES))

            row_ids = lax.broadcasted_iota(jnp.int32, (chunks, LANES), 0)
            for n, at, r in ((0, west_at, 1), (1, east_at, 0)):
                x = rdown[half, at, ends, :]
                first_term, last_term = terms(half, at, x)
                up_at, up_ok = above(at, half == 1)
                one = slice(r, r + 1)
                index = spread(x[one, 12:13]).astype(jnp.int32)
                inside = jnp.broadcast_to(jnp.bitwise_and(index, LANES - 1), (chunks, LANES))
                which = lax.shift_right_logical(index, 7)
                got = jnp.take_along_axis(marked(other, up_at, up_ok), inside, axis=1,
                                          mode="promise_in_bounds")
                got = jnp.sum(jnp.where(row_ids == which, got, 0.0), axis=0, keepdims=True)
                wet = got < 0.5 * DRY
                value = jnp.where(wet, got, 0.0)
                value += jnp.where(index == 0, first_term, 0.0)
                value += jnp.where(index == last, last_term, 0.0)
                second = x[one, 9:10] + x[one, 10:11] * value - jnp.where(wet, x[one, 11:12], 0.0)
                ok = (west_ok, east_ok)[n]
                corner[3 * n:3 * n + 3] = [kept(ok, v) for v in (x[one, 7:8], x[one, 8:9], second[:, 0:1])]
            corner[6] = kept(sw_ok, rdown[other, sw_at, 41:42, 7:8])
            corner[7] = kept(se_ok, rdown[other, se_at, 40:41, 7:8])

        def beside(at, row):
            return jnp.where(half == 0, rlast[at, row, :], rfirst[at, row, :])

        low_end, high_end = slice(24, 25), slice(25, 26)
        n_ends = kept(north_ok, rlast[north_at, 24:25, :])
        nw_ends, ne_ends = kept(nw_ok, beside(nw_at, high_end)), kept(ne_ok, beside(ne_at, low_end))
        sw_ends, se_ends = kept(sw_ok, beside(sw_at, high_end)), kept(se_ok, beside(se_at, low_end))
        sw_eta = sw_ends[:, 4:5] + corner[6]
        se_eta = se_ends[:, 4:5] + corner[7]

        e_below = kept(south_ok, rfirst[south_at, 0:8, :] + flow[2])
        khm = kept(south_ok, rfirst[south_at, 16:24, :])
        m = (khm > 0.0).astype(f32)
        km = COURANT * m
        push = km * (e_below - east_of(e_below, se_eta))
        p_out = sw_ends[:, 5:6] + sw_ends[:, 6:7] * (sw_eta - e_below[0:1, 0:1])
        flat = rfirst[south_at, 8:16, :] + push - west_of(push, p_out) + km * e_below
        below = kept(south_ok, m * e_below - khm * kept(south_ok, flat) + flow[3])
        e_here = e_first + flow[0]
        khm_n = kept(north_ok, rlast[north_at, 16:24, :])
        km_n = COURANT * (khm_n > 0.0).astype(f32)
        q_n = kept(north_ok, rlast[north_at, 8:16, :]) - km_n * e_here
        p_out = nw_ends[:, 3:4] - nw_ends[:, 2:3] * n_ends[:, 0:1]
        side = jnp.where(cell_ids == 0, p_out, 0.0)
        side += jnp.where(cell_ids == last, COURANT * ne_ends[:, 0:1], 0.0)
        e_n = kept(north_ok, rlast[north_at, 0:8, :]) - khm_n * (q_n - side)
        for n, x in enumerate((q_n + km_n * e_n, km_n, below, khm, flow[1], e_below, q_n, e_here)):
            line[n] = x
        for c in range(chunks):
            lane = slice(c * LANES, (c + 1) * LANES)
            if coarse:
                E0[0:1, lane] = line[7, c:c + 1, :]
            E0[rows:rows + 1, lane] = line[5, c:c + 1, :]
            Q1[7:8, lane] = line[6, c:c + 1, :]

        side_lane = lax.broadcasted_iota(jnp.int32, (BLOCK, 8), 1)
        side_row = lax.broadcasted_iota(jnp.int32, (BLOCK, 8), 0)

        def put(block, terms):
            for r, n, v in terms:
                here = jnp.logical_and(side_row == r, side_lane == n)
                block += jnp.where(here, v, 0.0)
            return block

        one = slice(0, 1)
        in1 = corner[0]
        in2 = corner[1]
        km0 = km_w[:, one]
        q_nw = nw_ends[:, 1:2] - nw_ends[:, 2:3] * (col_w[6:7, one] + in1)
        tip = m_w[:, one] * in1 - khm_w[:, one] * (col_w[7:8, one] * (in1 - in2) + km0 * in1 - q_nw)
        terms_up = [(0, 1, km0 * in1), (0, 3, tip + corner[2]),
                    (1, 3, khm_w[:, 1:2] * km0 * in1)]
        in1 = corner[3]
        in2 = corner[4]
        km0 = km_e[:, one]
        q_ne = ne_ends[:, 1:2] - ne_ends[:, 2:3] * (col_e[0:1, one] + in1)
        tip = m_e[:, one] * in1 + khm_e[:, one] * (km0 * (in2 - in1) - km0 * in1 + q_ne)
        terms_up += [(0, 0, in1), (0, 5, tip + corner[5]),
                     (1, 5, khm_e[:, 1:2] * km0 * in1)]
        low = slice(rows - 1, rows)
        terms_low = [(BLOCK - 1, 3, khm_w[:, low] * km_w[:, low] * sw_eta),
                     (BLOCK - 1, 5, khm_e[:, low] * km_e[:, low] * se_eta)]
        for r, terms_at in ((0, terms_up), (end, terms_low)):
            at = slice(r, r + BLOCK)
            block = put(halo[at, :], terms_at)
            step_rows(r, E0, P0, Q0, H, W, block, E1, P1, Q1)
            next_halo(at, block, E0[at, head], P1[at, tail])
        for c in range(chunks):
            lane = slice(c * LANES, (c + 1) * LANES)
            e1 = E1[0:1, lane]
            if coarse:
                e1 += line[4, c:c + 1, :]
                E1[0:1, lane] = e1
            E1[rows:rows + 1, lane] = line[2, c:c + 1, :] + line[3, c:c + 1, :] * Q1[rows + 7:rows + 8, lane]
            Q2[7:8, lane] = line[0, c:c + 1, :] - line[1, c:c + 1, :] * e1

    @pl.when(level == 1)
    def _():
        complete(False)

    @pl.when(level == 0)
    def _():
        fine_copy().wait_recv()
        receive_down()
        complete(True)

    send_columns(lambda copy: copy.wait_send())
    send_rows(lambda copy: copy.wait_send())
    send_down(lambda copy: copy.wait_send())

    @pl.when(level == 1)
    def _():
        fine_copy().wait_send()


def two_level(mesh, adjoint_height, adjoint_momenta, depth, wet_mask, adjacency, nest_gain, nest_index):
    patches = mesh.shape["patch"]
    rows, cols = adjoint_height.shape[1:]
    chunks = cols // LANES
    f32 = jnp.float32
    anywhere = pl.BlockSpec(memory_space=pl.ANY)
    v = pltpu.VMEM
    dma = pltpu.SemaphoreType.DMA
    whole = (v((rows + 8, cols), f32), v((rows, cols), f32), v((rows + 8, cols), f32))
    scratch = [
        pltpu.SMEM(adjacency.shape, jnp.int32), pltpu.SMEM(adjacency.shape, jnp.int32),
        *whole,
        v(nest_gain.shape, f32), v(nest_index.shape, jnp.int32),
        v((16, chunks, LANES), f32), v((16, LANES), f32), v((rows + 8, LANES), f32),
        v((48, LANES), f32), v((32, LANES), f32), v((48, LANES), f32), v((8, LANES), f32),
        v((8, LANES), f32),
        dma((28,)), dma((5, patches)), dma((3, patches)), dma((2, patches)), dma((2,)),
        v((patches, 48, LANES), f32), v((patches, 32, LANES), f32), v((patches, 8, LANES), f32),
        v((2, patches, 48, LANES), f32),
    ]
    here = pl.BlockSpec(memory_space=pltpu.VMEM)
    state = pl.pallas_call(
        functools.partial(swap, patches, rows, cols),
        out_shape=(*whole, v((rows, cols), f32), v((rows, cols), jnp.int32), v((rows, 8), f32), *whole),
        in_specs=[anywhere] * 7,
        out_specs=(here,) * 9,
        scratch_shapes=scratch,
        compiler_params=pltpu.CompilerParams(collective_id=0, has_side_effects=True,
                                             vmem_limit_bytes=14 << 20),
    )(*[pltpu.with_memory_space_constraint(x, pltpu.HBM) for x in (
        adjacency, adjoint_height, adjoint_momenta, depth, wet_mask, nest_gain, nest_index)])
    state = [pltpu.with_memory_space_constraint(x, pltpu.VMEM) for x in state]
    return pl.pallas_call(
        functools.partial(settle, rows),
        out_shape=(jax.ShapeDtypeStruct(adjoint_height.shape, f32),
                   jax.ShapeDtypeStruct(adjoint_momenta.shape, f32)),
        in_specs=[here] * 9,
        out_specs=(anywhere, anywhere),
        scratch_shapes=[*whole, dma((9,))],
        compiler_params=pltpu.CompilerParams(vmem_limit_bytes=12 << 20),
    )(*state)


def solution(mesh):
    in_specs = (
        P(("parts", "level"), ("patch", "sub"), None),
        P(None, ("parts", "level"), ("patch", "sub"), None),
        P("level", ("patch", "sub"), None),
        P("level", ("patch", "sub"), None),
        P("level", None, None),
        P(None, ("patch", "sub")),
        P(None, ("patch", "sub")),
    )
    out_specs = (
        P(("parts", "level"), ("patch", "sub"), None),
        P(None, ("parts", "level"), ("patch", "sub"), None),
    )
    run = two_level if mesh.shape["level"] == 2 else body
    return jax.shard_map(functools.partial(run, mesh), mesh=mesh, in_specs=in_specs,
                         out_specs=out_specs, check_vma=False)
```

```python
import functools

import jax
import jax.numpy as jnp
from jax import lax
from jax.experimental import pallas as pl
from jax.experimental.pallas import tpu as pltpu
from jax.sharding import PartitionSpec as P

STEPS = 2
COURANT = 0.45
LANES = 128
BLOCK = 8


def advance(r, E, Pm, Q, H, W, halo, E_to, P_to, Q_to):
    cols = Pm.shape[1]
    lane_ids = lax.broadcasted_iota(jnp.int32, (BLOCK, cols), 1)
    span = slice(r, r + BLOCK)
    e = E[span, :]
    wet = W[span, :].astype(jnp.float32)
    e_south = E[r + 1:r + 1 + BLOCK, :]
    e_east = pltpu.roll(e, cols - 1, 1)
    if halo is not None:
        e_east = jnp.where(lane_ids == cols - 1, halo[span, 0:1], e_east)
    p = wet * (Pm[span, :] - COURANT * (e_east - e))
    q = wet * (Q[8 + r:16 + r, :] - COURANT * (e_south - e))
    p_west = pltpu.roll(p, 1, 1)
    if halo is not None:
        p_edge = halo[span, 1:2] - COURANT * halo[span, 2:3] * e[:, 0:1]
        p_west = jnp.where(lane_ids == 0, p_edge, p_west)
    P_to[span, :] = p
    Q_to[8 + r:16 + r, :] = q
    q_north = Q_to[7 + r:15 + r, :]
    E_to[span, :] = wet * (e - COURANT * H[span, :] * ((p - p_west) + (q - q_north)))


def finish(rows, E, Pm, Q, H, W, halo, E2, P2, Q2, eta_out, mom_out, Ef, Pf, Qf, sems):
    cols = Pm.shape[1]
    end = rows - BLOCK
    mid = slice(BLOCK, end)
    head, tail = slice(0, LANES), slice(cols - LANES, cols)
    before, inner = slice(0, cols - LANES), slice(LANES, cols - LANES)
    stores = []

    def store(src, dst):
        copy = pltpu.make_async_copy(src, dst, sems.at[len(stores)])
        copy.start()
        stores.append(copy)

    eta_to, row_to, col_to = eta_out.at[0], mom_out.at[0, 0], mom_out.at[1, 0]
    store(Q2.at[BLOCK + 8:end + 8], col_to.at[mid])
    store(P2.at[mid, before], row_to.at[mid, before])
    store(E2.at[mid, inner], eta_to.at[mid, inner])
    edges = halo[...]
    lane_ids = lax.broadcasted_iota(jnp.int32, (end - BLOCK, LANES), 1)

    across = Q2[BLOCK + 8:end + 8, head] - Q2[BLOCK + 7:end + 7, head]
    e = E[mid, head]
    wet = W[mid, head].astype(jnp.float32)
    p_edge = edges[mid, 1:2] - COURANT * edges[mid, 2:3] * e[:, 0:1]
    fixed = wet * (e - COURANT * H[mid, head] * ((P2[mid, head] - p_edge) + across))
    Ef[mid, head] = jnp.where(lane_ids == 0, fixed, E2[mid, head])
    store(Ef.at[mid, head], eta_to.at[mid, head])

    across = Q2[BLOCK + 8:end + 8, tail] - Q2[BLOCK + 7:end + 7, tail]
    e = E[mid, tail]
    wet = W[mid, tail].astype(jnp.float32)
    p = wet * (Pm[mid, tail] - COURANT * (edges[mid, 0:1] - e))
    p = jnp.where(lane_ids == LANES - 1, p, P2[mid, tail])
    Pf[mid, tail] = p
    store(Pf.at[mid, tail], row_to.at[mid, tail])
    fixed = wet * (e - COURANT * H[mid, tail] * ((p - pltpu.roll(p, 1, 1)) + across))
    Ef[mid, tail] = jnp.where(lane_ids == LANES - 1, fixed, E2[mid, tail])
    store(Ef.at[mid, tail], eta_to.at[mid, tail])

    for r in (0, end):
        Qf[7 + r:8 + r, :] = (Q if r == 0 else Q2)[7 + r:8 + r, :]
        advance(r, E, Pm, Q, H, W, edges, Ef, Pf, Qf)
        at = slice(r, r + BLOCK)
        store(Pf.at[at], row_to.at[at])
        store(Qf.at[8 + r:16 + r], col_to.at[at])
        store(Ef.at[at], eta_to.at[at])
    for copy in stores:
        copy.wait()


def exchange(patches, levels, rows, cols,
             adj_hbm, eta_hbm, mom_hbm, depth_hbm, wet_hbm, gain_hbm, table_hbm,
             E1, P1, Q1, H, W, halo_out, E2, P2, Q2,
             adj, E0, P0, Q0, gain_v, table_v, f8, idx8, gain8, tmp,
             sfirst, slast, scol, sinf, sew,
             rown, in_sems, send_sems, recv_sems, own_sems, *landing):
    rfirst, rlast, rcol, rnbr, rew = (landing[n * STEPS:(n + 1) * STEPS] for n in range(5))
    fields = ((E0, P0, Q0), (E1, P1, Q1))
    patch = lax.axis_index("patch")
    level = lax.axis_index("level")
    half = lax.axis_index("sub")
    chunks = cols // LANES
    other = 1 - half

    loads = [
        pltpu.make_async_copy(eta_hbm.at[0], E0.at[0:rows], in_sems.at[0]),
        pltpu.make_async_copy(mom_hbm.at[0, 0], P0, in_sems.at[1]),
        pltpu.make_async_copy(mom_hbm.at[1, 0], Q0.at[8:8 + rows], in_sems.at[2]),
        pltpu.make_async_copy(wet_hbm.at[0], W, in_sems.at[3]),
        pltpu.make_async_copy(table_hbm, table_v, in_sems.at[4]),
        pltpu.make_async_copy(gain_hbm, gain_v, in_sems.at[5]),
        pltpu.make_async_copy(adj_hbm, adj, in_sems.at[6]),
        pltpu.make_async_copy(depth_hbm.at[0], H, in_sems.at[7]),
    ]
    barrier = pltpu.get_barrier_semaphore()

    peers = [patch] + [lax.rem(patch + d, patches) for d in range(1, patches)]

    def greet(d, h, lev):
        pl.semaphore_signal(barrier, inc=1, device_id={
            "patch": peers[d], "sub": h, "level": lev},
            device_id_type=pl.DeviceIdType.MESH)

    for d in range(patches - 1, -1, -1):
        greet(d, other, level)
        if d:
            greet(d, half, level)

    @pl.when(level > 0)
    def _():
        for d in range(patches):
            greet(d, half, level - 1)
            greet(d, other, level - 1)

    @pl.when(level < levels - 1)
    def _():
        for d in range(patches):
            greet(d, half, level + 1)
            greet(d, other, level + 1)

    for load in loads:
        load.start()

    for load in loads[:7]:
        load.wait()

    lower = jnp.maximum(level - 1, 0)
    for c in range(chunks):
        lane = slice(c * LANES, (c + 1) * LANES)
        index, gain = table_v[0:1, lane], gain_v[0:1, lane]
        for lev in range(1, levels - 1):
            index = jnp.where(lower == lev, table_v[lev:lev + 1, lane], index)
            gain = jnp.where(lower == lev, gain_v[lev:lev + 1, lane], gain)
        idx8[c:c + 1, :] = index
        gain8[c:c + 1, :] = gain

    def remote(t, kind, src, buf, slot, d, h, lev):
        return pltpu.make_async_remote_copy(
            src_ref=src, dst_ref=buf, send_sem=send_sems.at[t, kind, d],
            recv_sem=recv_sems.at[t, kind, slot],
            device_id={"patch": peers[d], "sub": h, "level": lev},
            device_id_type=pl.DeviceIdType.MESH)

    def last_part(t):
        return slice(0, 2) if t == 0 else slice(t + 1, t + 2)

    def column_copy(t, slot, d):
        return remote(t, 0, scol.at[t, 0:3], rcol[t].at[slot, 0:3], slot, d, half, level)

    def first_copy(t, slot, d):
        return remote(t, 1, sfirst.at[t], rfirst[t].at[slot], slot, d, other, level)

    def last_copy(t, slot, d):
        part = last_part(t)
        return remote(t, 2, slast.at[part], rlast[t].at[slot], slot, d, other, level)

    def beside_copy(t, slot, d):
        return remote(t, 3, sinf.at[t], rnbr[t].at[slot], slot, d, other, lower)

    def ends_copy(t, slot, d):
        return remote(t, 4, sew.at[t], rew[t].at[slot], slot, d, half, lower)

    def per_half(across, inside, act):
        @pl.when(half == across)
        def _():
            for d in range(1, patches):
                act(d)

        @pl.when(half == inside)
        def _():
            act(0)

    def own_copy(t):
        return pltpu.make_async_remote_copy(
            src_ref=sinf.at[t], dst_ref=rown.at[t], send_sem=own_sems.at[t, 0],
            recv_sem=own_sems.at[t, 1], device_id={"level": lower},
            device_id_type=pl.DeviceIdType.MESH)

    def make_inflow(t):
        E = fields[t][0]
        for c in range(chunks):
            f8[c:c + 1, :] = E[0:1, c * LANES:(c + 1) * LANES]
        index = idx8[...]
        inside = jnp.bitwise_and(index, LANES - 1)
        which = lax.shift_right_logical(index, 7)
        picked = jnp.zeros((chunks, LANES), jnp.float32)
        for c in range(chunks):
            source = jnp.broadcast_to(f8[c:c + 1, :], (chunks, LANES))
            got = jnp.take_along_axis(source, inside, axis=1, mode="promise_in_bounds")
            picked = jnp.where(which == c, got, picked)
        inflow = gain8[...] * picked
        sinf[t] = inflow
        sew[t, 0:1, :] = inflow[0:1, :]
        sew[t, 1:2, :] = pltpu.roll(inflow[chunks - 1:chunks, :], 1, 1)

    def send_inflow(t):
        own_copy(t).start()
        per_half(0, 1, lambda d: beside_copy(t, patch, d).start())
        for d in range(1, patches):
            ends_copy(t, patch, d).start()

    def inflow_waits(t):
        per_half(1, 0, lambda d: beside_copy(t, peers[d], d).wait_recv())
        for d in range(1, patches):
            ends_copy(t, peers[d], d).wait_recv()

    def inflow_send_waits(t):
        own_copy(t).wait_send()
        per_half(0, 1, lambda d: beside_copy(t, patch, d).wait_send())
        for d in range(1, patches):
            ends_copy(t, patch, d).wait_send()

    def send_halos(t, act):
        send_rows(t, act)
        send_columns(t, act)

    def send_columns(t, act):
        for d in range(1, patches):
            act(column_copy(t, patch, d))

    def send_rows(t, act):
        @pl.when(half == 0)
        def _():
            for d in range(1, patches):
                act(first_copy(t, patch, d))
            act(last_copy(t, patch, 0))

        @pl.when(half == 1)
        def _():
            for d in range(1, patches):
                act(last_copy(t, patch, d))
            act(first_copy(t, patch, 0))

    def receive_halos(t):
        @pl.when(half == 0)
        def _():
            first_copy(t, peers[0], 0).wait_recv()
            for d in range(1, patches):
                last_copy(t, peers[d], d).wait_recv()

        @pl.when(half == 1)
        def _():
            last_copy(t, peers[0], 0).wait_recv()
            for d in range(1, patches):
                first_copy(t, peers[d], d).wait_recv()

        for d in range(1, patches):
            column_copy(t, peers[d], d).wait_recv()

    north = adj[0, patch, 0]
    south = adj[0, patch, 1]
    west = adj[0, patch, 2]
    east = adj[0, patch, 3]
    south_ok = jnp.logical_or(half == 0, south >= 0)
    north_ok = jnp.logical_or(half == 1, north >= 0)
    south_at = jnp.where(half == 0, patch, jnp.maximum(south, 0))
    north_at = jnp.where(half == 1, patch, jnp.maximum(north, 0))
    west_at = jnp.maximum(west, 0)
    east_at = jnp.maximum(east, 0)
    finer = level < levels - 1
    lane_ids = lax.broadcasted_iota(jnp.int32, (rows, LANES), 1)
    first_lane = lax.broadcasted_iota(jnp.int32, (1, LANES), 1) == 0
    tail = slice(cols - LANES, cols)
    end = rows - 1

    def make_messages(t):
        @pl.when(level == levels - 1)
        def _():
            make_inflow(t)

        make_rows(t)
        make_columns(t)

    def make_rows(t):
        E, Pm, Q = fields[t]
        sfirst[t] = E[0:1, :]
        wet_row = W[end:rows, :].astype(jnp.float32)
        slast[t + 1] = wet_row * (Q[8 + end:8 + rows, :] + COURANT * E[end:rows, :])
        if t == 0:
            slast[0] = wet_row

    def make_columns(t):
        E, Pm, Q = fields[t]
        wet_tail = W[:, tail].astype(jnp.float32)
        share = wet_tail * (Pm[:, tail] + COURANT * E[0:rows, tail])
        mixed = jnp.where(lane_ids == 0, E[0:rows, 0:LANES],
                          jnp.where(lane_ids == 1, pltpu.roll(share, 2, 1),
                                    pltpu.roll(wet_tail, 3, 1)))
        scol[t] = jnp.transpose(mixed[:, 0:8])

    def send_messages(t):
        @pl.when(level == levels - 1)
        def _():
            send_inflow(t)

        send_halos(t, lambda copy: copy.start())

    def receive(t):
        E, Pm, Q = fields[t]

        @pl.when(finer)
        def _():
            own_copy(t).wait_recv()
            for c in range(chunks):
                lane = slice(c * LANES, (c + 1) * LANES)
                E[0:1, lane] += rown[t, c:c + 1, :]

        if levels > 2:
            @pl.when(jnp.logical_and(level > 0, level < levels - 1))
            def _():
                make_inflow(t)
                send_inflow(t)

        receive_halos(t)

        @pl.when(finer)
        def _():
            inflow_waits(t)

        east_row = rcol[t][east_at][0:1, :]
        east_row += jnp.where(jnp.logical_and(first_lane, finer), rew[t][east_at][0:1, :], 0.0)
        west_cols = rcol[t][west_at]
        share = west_cols[1:2, :]
        wet_w = west_cols[2:3, :]
        share += jnp.where(jnp.logical_and(first_lane, finer),
                           COURANT * wet_w * rew[t][west_at][1:2, :], 0.0)
        tmp[0:1, :] = jnp.where(east >= 0, east_row, 0.0)
        tmp[1:2, :] = jnp.where(west >= 0, share, 0.0)
        tmp[2:3, :] = jnp.where(west >= 0, wet_w, 0.0)
        beside = rnbr[t][south_at]
        below = rfirst[t][south_at]
        for c in range(chunks):
            lane = slice(c * LANES, (c + 1) * LANES)
            value = below[:, lane] + jnp.where(finer, beside[c:c + 1, :], 0.0)
            E[rows:rows + 1, lane] = jnp.where(south_ok, value, 0.0)
        share_n = rlast[t][north_at, 1 if t == 0 else 0]
        wet_n = rlast[0][north_at, 0]
        Q_to = Q1
        Q_to[7:8, :] = jnp.where(north_ok, share_n - COURANT * wet_n * E[0:1, :], 0.0)
        return jnp.transpose(tmp[...])

    make_messages(0)
    sides = (level > 0).astype(jnp.int32) + (level < levels - 1).astype(jnp.int32)
    pl.semaphore_wait(barrier, 2 * patches - 1 + 2 * patches * sides)
    send_messages(0)
    loads[7].wait()
    for r in range(0, rows - BLOCK, BLOCK):
        advance(r, E0, P0, Q0, H, W, None, E1, P1, Q1)
    halo = receive(0)
    for r in (0, rows - BLOCK):
        advance(r, E0, P0, Q0, H, W, None, E1, P1, Q1)
    head = slice(0, LANES)
    e = E0[0:rows, head]
    wet = W[:, head].astype(jnp.float32)
    p_edge = halo[:, 1:2] - COURANT * halo[:, 2:3] * e[:, 0:1]
    across = Q1[8:8 + rows, head] - Q1[7:7 + rows, head]
    fixed = wet * (e - COURANT * H[:, head] * ((P1[:, head] - p_edge) + across))
    E1[0:rows, head] = jnp.where(lane_ids == 0, fixed, E1[0:rows, head])
    e = E0[0:rows, tail]
    wet = W[:, tail].astype(jnp.float32)
    p = wet * (P0[:, tail] - COURANT * (halo[:, 0:1] - e))
    p = jnp.where(lane_ids == LANES - 1, p, P1[:, tail])
    P1[:, tail] = p
    across = Q1[8:8 + rows, tail] - Q1[7:7 + rows, tail]
    fixed = wet * (e - COURANT * H[:, tail] * ((p - pltpu.roll(p, 1, 1)) + across))
    E1[0:rows, tail] = jnp.where(lane_ids == LANES - 1, fixed, E1[0:rows, tail])

    @pl.when(level == levels - 1)
    def _():
        make_inflow(1)
        send_inflow(1)

    make_rows(1)
    send_rows(1, lambda copy: copy.start())
    make_columns(1)
    send_columns(1, lambda copy: copy.start())
    for r in range(0, rows - BLOCK, BLOCK):
        advance(r, E1, P1, Q1, H, W, None, E2, P2, Q2)
    halo_out[...] = receive(1)
    for t in range(STEPS):
        send_halos(t, lambda copy: copy.wait_send())

        @pl.when(level > 0)
        def _():
            inflow_send_waits(t)


def body(mesh, adjoint_height, adjoint_momenta, depth, wet_mask, adjacency, nest_gain, nest_index):
    patches, levels = mesh.shape["patch"], mesh.shape["level"]
    rows, cols = adjoint_height.shape[1:]
    chunks = cols // LANES
    f32 = jnp.float32
    anywhere = pl.BlockSpec(memory_space=pl.ANY)
    v = pltpu.VMEM
    dma = pltpu.SemaphoreType.DMA
    whole = (v((rows + 8, cols), f32), v((rows, cols), f32), v((rows + 8, cols), f32))
    scratch = [
        pltpu.SMEM(adjacency.shape, jnp.int32),
        *whole,
        v(nest_gain.shape, f32), v(nest_index.shape, jnp.int32),
        v((chunks, LANES), f32), v((chunks, LANES), jnp.int32), v((chunks, LANES), f32),
        v((8, LANES), f32),
        v((STEPS, 1, cols), f32), v((STEPS + 1, 1, cols), f32), v((STEPS, 8, LANES), f32),
        v((STEPS, chunks, LANES), f32), v((STEPS, 2, LANES), f32),
        v((STEPS, chunks, LANES), f32),
        dma((8,)), dma((STEPS, 5, patches)), dma((STEPS, 5, patches)), dma((STEPS, 2)),
    ]
    scratch += [v((patches, 1, cols), f32)] * STEPS
    scratch += [v((patches, 2 if t == 0 else 1, 1, cols), f32) for t in range(STEPS)]
    scratch += [v((patches, 8, LANES), f32)] * STEPS
    scratch += [v((patches, chunks, LANES), f32)] * STEPS
    scratch += [v((patches, 2, LANES), f32)] * STEPS
    here = pl.BlockSpec(memory_space=pltpu.VMEM)
    state = pl.pallas_call(
        functools.partial(exchange, patches, levels, rows, cols),
        out_shape=(*whole, v((rows, cols), f32), v((rows, cols), jnp.int32), v((rows, 8), f32), *whole),
        in_specs=[anywhere] * 7,
        out_specs=(here,) * 9,
        scratch_shapes=scratch,
        compiler_params=pltpu.CompilerParams(collective_id=0, has_side_effects=True,
                                             vmem_limit_bytes=12 << 20),
    )(*[pltpu.with_memory_space_constraint(x, pltpu.HBM) for x in (
        adjacency, adjoint_height, adjoint_momenta, depth, wet_mask, nest_gain, nest_index)])
    state = [pltpu.with_memory_space_constraint(x, pltpu.VMEM) for x in state]
    return pl.pallas_call(
        functools.partial(finish, rows),
        out_shape=(jax.ShapeDtypeStruct(adjoint_height.shape, f32),
                   jax.ShapeDtypeStruct(adjoint_momenta.shape, f32)),
        in_specs=[here] * 9,
        out_specs=(anywhere, anywhere),
        scratch_shapes=[*whole, dma((12,))],
        compiler_params=pltpu.CompilerParams(vmem_limit_bytes=12 << 20),
    )(*state)


FULL, TAIL, ENDS = (0, 42), (24, 42), (40, 42)
DRY = 1e30


def step_rows(r, E, Pm, Q, H, W, edge, E_to, P_to, Q_to):
    cols = Pm.shape[1]
    lane_ids = lax.broadcasted_iota(jnp.int32, (BLOCK, cols), 1)
    span = slice(r, r + BLOCK)
    e = E[span, :]
    wet = W[span, :].astype(jnp.float32)
    e_south = E[r + 1:r + 1 + BLOCK, :]
    e_east = pltpu.roll(e, cols - 1, 1)
    if edge is not None:
        e_east = jnp.where(lane_ids == cols - 1, edge[:, 0:1], e_east)
    p = wet * (Pm[span, :] - COURANT * (e_east - e))
    q = wet * (Q[8 + r:16 + r, :] - COURANT * (e_south - e))
    p_west = pltpu.roll(p, 1, 1)
    if edge is not None:
        p_west = jnp.where(lane_ids == 0, edge[:, 1:2] - edge[:, 2:3] * e[:, 0:1], p_west)
    P_to[span, :] = p
    Q_to[8 + r:16 + r, :] = q
    q_north = Q_to[7 + r:15 + r, :]
    E_to[span, :] = wet * (e - COURANT * H[span, :] * ((p - p_west) + (q - q_north)))


def settle(rows, E, Pm, Q, H, W, halo, E2, P2, Q2, eta_out, mom_out, Ef, Pf, Qf, sems):
    end = rows - BLOCK
    mid = slice(BLOCK, end)
    stores = []

    def store(src, dst):
        copy = pltpu.make_async_copy(src, dst, sems.at[len(stores)])
        copy.start()
        stores.append(copy)

    eta_to, row_to, col_to = eta_out.at[0], mom_out.at[0, 0], mom_out.at[1, 0]
    store(Q2.at[BLOCK + 8:end + 8], col_to.at[mid])
    store(P2.at[mid], row_to.at[mid])
    store(E2.at[mid], eta_to.at[mid])
    def ends(r):
        at = slice(r, r + BLOCK)
        step_rows(r, E, Pm, Q, H, W, halo[at, :], Ef, Pf, Qf)
        store(Pf.at[at], row_to.at[at])
        store(Qf.at[8 + r:16 + r], col_to.at[at])
        store(Ef.at[at], eta_to.at[at])

    for r in (0, end):
        Qf[7 + r:8 + r, :] = Q2[7 + r:8 + r, :]
        ends(r)
    for copy in stores:
        copy.wait()


def swap(patches, rows, cols,
         adj_hbm, eta_hbm, mom_hbm, depth_hbm, wet_hbm, gain_hbm, table_hbm,
         E1, P1, Q1, H, W, halo_out, E2, P2, Q2,
         adj, fine, E0, P0, Q0, gain_v, table_v, line, stack, qb, sfirst, slast, sdown, scol,
         tmp, in_sems, send_sems, recv_sems, down_sems, fine_sems,
         rfirst, rlast, rcol, rdown):
    f32 = jnp.float32
    patch = lax.axis_index("patch")
    level = lax.axis_index("level")
    half = lax.axis_index("sub")
    other = 1 - half
    chunks = cols // LANES
    last = cols - 1
    end = rows - BLOCK
    head, tail = slice(0, LANES), slice(cols - LANES, cols)
    inner = slice(LANES, cols - LANES)
    mid = slice(BLOCK, end)
    loads = []

    def load(src, dst):
        copy = pltpu.make_async_copy(src, dst, in_sems.at[len(loads)])
        copy.start()
        loads.append(copy)

    fields = ((eta_hbm.at[0], E0, 0), (mom_hbm.at[0, 0], P0, 0), (mom_hbm.at[1, 0], Q0, 8),
              (wet_hbm.at[0], W, 0), (depth_hbm.at[0], H, 0))

    def load_part(at, lane):
        for src, dst, shift in fields:
            load(src.at[at, lane], dst.at[at.start + shift:at.stop + shift, lane])

    barrier = pltpu.get_barrier_semaphore()
    peers = [patch] + [jnp.where(patch < d, d, d - 1) for d in range(1, patches)]

    def greet(d, h, lev):
        pl.semaphore_signal(barrier, inc=1, device_id={
            "patch": peers[d], "sub": h, "level": lev},
            device_id_type=pl.DeviceIdType.MESH)

    for d in range(1, patches):
        greet(d, other, level)
        greet(d, half, level)
    greet(0, other, level)

    @pl.when(level == 0)
    def _():
        for d in list(range(1, patches)) + [0]:
            greet(d, half, 1)
            greet(d, other, 1)

    for at in (slice(0, BLOCK), slice(end, rows)):
        load_part(at, slice(0, cols))
    load(adj_hbm, adj)
    load(table_hbm, table_v)
    load(gain_hbm, gain_v)
    n_rows = len(loads)

    for lane in (head, tail):
        load_part(mid, lane)
    n_tiles = len(loads)
    load_part(mid, inner)

    E0[rows:rows + 8, :] = jnp.zeros((8, cols), f32)
    qb[0:8, :] = jnp.zeros((8, LANES), f32)
    lane_ids = lax.broadcasted_iota(jnp.int32, (chunks, LANES), 1)
    cell_ids = lax.broadcasted_iota(jnp.int32, (chunks, LANES), 0) * LANES + lane_ids
    row_lane = lax.broadcasted_iota(jnp.int32, (1, LANES), 1)

    def east_of(x, beyond):
        y = pltpu.roll(x, LANES - 1, 1)
        y = jnp.where(lane_ids == LANES - 1, pltpu.roll(y, chunks - 1, 0), y)
        return jnp.where(cell_ids == last, beyond, y)

    def west_of(x, beyond):
        y = pltpu.roll(x, 1, 1)
        y = jnp.where(lane_ids == 0, pltpu.roll(y, 1, 0), y)
        return jnp.where(cell_ids == 0, beyond, y)

    def gather(x, index):
        inside = jnp.bitwise_and(index, LANES - 1)
        which = lax.shift_right_logical(index, 7)
        picked = jnp.zeros((chunks, LANES), f32)
        for c in range(chunks):
            source = jnp.broadcast_to(x[c:c + 1, :], (chunks, LANES))
            got = jnp.take_along_axis(source, inside, axis=1, mode="promise_in_bounds")
            picked = jnp.where(which == c, got, picked)
        return picked

    def row_messages():
        for n, (ref, r) in enumerate(((E0, rows - 2), (Q0, rows + 6), (W, rows - 2))):
            lines(11 + n, ref, r)
        sfirst[0:8, :] = e
        sfirst[8:16, :] = mp - west_of(mp, 0.0) + (m * q - km * line[1])
        sfirst[16:24, :] = khm
        sfirst[32:40, :] = gain
        sfirst[40:48, :] = line[15]
        p_new = ml * line[7] - kml * (east_of(el, 0.0) - el)
        q_above = line[13] * (line[12] - COURANT * (el - line[11]))
        slast[0:8, :] = ml * el - khml * (p_new - west_of(p_new, 0.0) - q_above)
        slast[8:16, :] = aq
        slast[16:24, :] = khml

    tile_lanes = lax.broadcasted_iota(jnp.int32, (rows, LANES), 1)

    def column_message():
        for copy in loads[n_rows:n_tiles]:
            copy.wait()
        mixed = None
        for lane in (head, tail):
            e = E0[0:rows, lane]
            m = W[:, lane].astype(f32)
            km = COURANT * m
            khm = km * H[:, lane]
            p_new = m * P0[:, lane] - km * (pltpu.roll(e, LANES - 1, 1) - e)
            q_new = m * Q0[8:8 + rows, lane] - km * (E0[1:rows + 1, lane] - e)
            qb[8:8 + rows, :] = q_new
            across = q_new - qb[7:7 + rows, :]
            if lane == head:
                parts = ((e, 0), (m * e - khm * (p_new + across), 0), (khm, 0))
            else:
                parts = ((m * P0[:, lane] + km * e, LANES - 1),
                         (m * e - khm * (across - pltpu.roll(p_new, 1, 1)), LANES - 1),
                         (khm, LANES - 1), (e, LANES - 1), (km, LANES - 2))
            for n, (x, at) in enumerate(parts):
                to = n + (0 if lane == head else 3)
                moved = pltpu.roll(x, (to - at) % LANES, 1) if (to - at) % LANES else x
                mixed = moved if mixed is None else jnp.where(tile_lanes == to, moved, mixed)
        scol[...] = jnp.transpose(mixed[:, 0:8])

    def remote(kind, src, dst, recv_sem, d, h, lev):
        return pltpu.make_async_remote_copy(
            src_ref=src, dst_ref=dst, send_sem=send_sems.at[kind, d], recv_sem=recv_sem,
            device_id={"patch": peers[d], "sub": h, "level": lev},
            device_id_type=pl.DeviceIdType.MESH)

    def column_copy(slot, d):
        return remote(0, scol, rcol.at[slot], recv_sems.at[0, slot], d, half, level)

    def first_copy(slot, d, size):
        return remote(1, sfirst.at[0:size], rfirst.at[slot, 0:size], recv_sems.at[1, slot], d, other, level)

    def by_level(act):
        for lev, size in enumerate((48, 26)):
            @pl.when(level == lev)
            def _():
                act(size)

    def last_copy(slot, d):
        return remote(2, slast.at[0:26], rlast.at[slot, 0:26], recv_sems.at[2, slot], d, other, level)

    def down_copy(part, from_half, slot, d, h):
        at = slice(*part)
        return remote(3 + h, sdown.at[at], rdown.at[from_half, slot, at],
                      down_sems.at[from_half, slot], d, h, 1 - level)

    def fine_copy():
        return pltpu.make_async_remote_copy(
            src_ref=adj, dst_ref=fine, send_sem=fine_sems.at[0], recv_sem=fine_sems.at[1],
            device_id={"level": 1 - level}, device_id_type=pl.DeviceIdType.MESH)

    far = list(range(1, patches)) + [0]

    def send_rows(act):
        @pl.when(half == 0)
        def _():
            def firsts(size):
                for d in range(1, patches):
                    act(first_copy(patch, d, size))

            by_level(firsts)
            act(last_copy(patch, 0))

        @pl.when(half == 1)
        def _():
            for d in range(1, patches):
                act(last_copy(patch, d))
            by_level(lambda size: act(first_copy(patch, 0, size)))

    def send_down(act):
        @pl.when(jnp.logical_and(level == 1, half == 0))
        def _():
            for d in far:
                act(down_copy(ENDS if d else FULL, 0, patch, d, 0))
                act(down_copy(FULL if d else TAIL, 0, patch, d, 1))

        @pl.when(jnp.logical_and(level == 1, half == 1))
        def _():
            for d in far:
                act(down_copy(TAIL if d else FULL, 1, patch, d, 0))
                act(down_copy(TAIL if d else FULL, 1, patch, d, 1))

    def send_columns(act):
        for d in range(1, patches):
            act(column_copy(patch, d))

    def receive_columns():
        for d in range(1, patches):
            column_copy(peers[d], d).wait_recv()

    def receive_rows():
        @pl.when(half == 0)
        def _():
            by_level(lambda size: first_copy(patch, 0, size).wait_recv())
            for d in range(1, patches):
                last_copy(peers[d], d).wait_recv()

        @pl.when(half == 1)
        def _():
            def firsts(size):
                for d in range(1, patches):
                    first_copy(peers[d], d, size).wait_recv()

            last_copy(patch, 0).wait_recv()
            by_level(firsts)

    def receive_down():
        @pl.when(jnp.logical_and(level == 0, half == 0))
        def _():
            for d in far:
                down_copy(TAIL if d else FULL, 1, peers[d], d, 0).wait_recv()
                down_copy(ENDS if d else FULL, 0, peers[d], d, 0).wait_recv()

        @pl.when(jnp.logical_and(level == 0, half == 1))
        def _():
            for d in far:
                down_copy(TAIL if d else FULL, 1, peers[d], d, 1).wait_recv()
                down_copy(FULL if d else TAIL, 0, peers[d], d, 1).wait_recv()

    for copy in loads[:n_rows]:
        copy.wait()

    @pl.when(level == 0)
    def _():
        column_message()
        pl.semaphore_wait(barrier, 2 * patches - 1)
        send_columns(lambda copy: copy.start())


    def lines(n, ref, r):
        for c in range(chunks):
            line[n, c:c + 1, :] = ref[r:r + 1, c * LANES:(c + 1) * LANES].astype(f32)

    for n, (ref, r) in enumerate((
            (E0, 0), (E0, 1), (P0, 0), (Q0, 8), (W, 0), (H, 0),
            (E0, rows - 1), (P0, rows - 1), (Q0, rows + 7), (W, rows - 1), (H, rows - 1))):
        lines(n, ref, r)

    e, p, q, m = line[0], line[2], line[3], line[4]
    e_first = e
    km = COURANT * m
    khm = km * line[5]
    mp = m * p
    stack[4:5, :] = jnp.where(row_lane < 64, e[0:1, :], e[chunks - 1:chunks, :])
    stack[5:6, :] = jnp.where(row_lane < 64, mp[0:1, :], mp[chunks - 1:chunks, :])
    stack[6:7, :] = jnp.where(row_lane < 64, km[0:1, :], km[chunks - 1:chunks, :])
    el, ml = line[6], line[9]
    kml = COURANT * ml
    khml = kml * line[10]
    aq = ml * line[8] + kml * el
    ap = ml * line[7] + kml * el
    sdown[24:32, :] = aq
    sdown[32:40, :] = khml
    for n, x in enumerate((el, aq, kml, ap)):
        stack[n:n + 1, :] = jnp.where(row_lane < 64, x[0:1, :], x[chunks - 1:chunks, :])
    stack[13:16, :] = jnp.zeros((3, LANES), f32)

    @pl.when(level == 0)
    def _():
        stack[7:13, :] = jnp.zeros((6, LANES), f32)

    for c in range(chunks):
        lane = slice(c * LANES, (c + 1) * LANES)
        line[14, c:c + 1, :] = gain_v[0:1, lane]
        line[15, c:c + 1, :] = table_v[0:1, lane].astype(f32)
    gain, index = line[14], line[15].astype(jnp.int32)

    @pl.when(level == 1)
    def _():
        p_new = mp - km * (east_of(e, 0.0) - e)
        q_new = m * q - km * (line[1] - e)
        there = m * e - khm * (p_new - west_of(p_new, 0.0) + q_new)
        parts = [gather(x, index) for x in (e, there, khm)]
        for n, x in enumerate(parts):
            sdown[8 * n:8 * n + 8, :] = x
        inflow = gain * parts[0]
        rows_of = (inflow, None, gain * parts[1], gain * parts[2],
                   COURANT * parts[2] * inflow, line[15])
        for n, x in enumerate(rows_of):
            if x is None:
                low = pltpu.roll(inflow, LANES - 1, 1)[0:1, :]
                high = pltpu.roll(inflow, 1, 1)[chunks - 1:chunks, :]
            else:
                low, high = x[0:1, :], x[chunks - 1:chunks, :]
            stack[7 + n:8 + n, :] = jnp.where(row_lane < 64, low, high)

    turned = jnp.transpose(stack[...])
    for ref, at in ((sfirst, 24), (slast, 24), (sdown, 40)):
        ref[at:at + 1, 0:16] = turned[0:1, :]
        ref[at + 1:at + 2, 0:16] = turned[LANES - 1:LANES, :]

    @pl.when(level == 0)
    def _():
        row_messages()

    @pl.when(level == 1)
    def _():
        column_message()
        pl.semaphore_wait(barrier, 4 * patches - 1)
        fine_copy().start()

    send_down(lambda copy: copy.start())

    @pl.when(level == 1)
    def _():
        row_messages()
        send_columns(lambda copy: copy.start())

    send_rows(lambda copy: copy.start())

    for copy in loads[n_tiles:]:
        copy.wait()
    for r in range(0, rows, BLOCK):
        step_rows(r, E0, P0, Q0, H, W, None, E1, P1, Q1)
    for r in range(0, end, BLOCK):
        step_rows(r, E1, P1, Q1, H, W, None, E2, P2, Q2)

    north, south = adj[0, patch, 0], adj[0, patch, 1]
    west, east = adj[0, patch, 2], adj[0, patch, 3]
    south_ok = jnp.logical_or(half == 0, south >= 0)
    north_ok = jnp.logical_or(half == 1, north >= 0)
    south_at = jnp.where(half == 0, patch, jnp.maximum(south, 0))
    north_at = jnp.where(half == 1, patch, jnp.maximum(north, 0))
    west_ok, east_ok = west >= 0, east >= 0
    west_at, east_at = jnp.maximum(west, 0), jnp.maximum(east, 0)

    def beyond(at, ok, side):
        to = adj[0, at, side]
        return jnp.maximum(to, 0), jnp.logical_and(ok, to >= 0)

    nw_at, nw_ok = beyond(north_at, north_ok, 2)
    ne_at, ne_ok = beyond(north_at, north_ok, 3)
    sw_at, sw_ok = beyond(south_at, south_ok, 2)
    se_at, se_ok = beyond(south_at, south_ok, 3)

    def kept(ok, x):
        return jnp.where(ok, x, 0.0)

    receive_columns()
    col_w, col_e = kept(west_ok, rcol[west_at]), kept(east_ok, rcol[east_at])
    khm_w, khm_e = col_w[5:6, :], col_e[2:3, :]
    m_w, m_e = (khm_w > 0.0).astype(f32), (khm_e > 0.0).astype(f32)
    km_w, km_e = COURANT * m_w, COURANT * m_e
    for n, v in enumerate((col_e[0:1, :], col_w[3:4, :], km_w, col_w[4:5, :], khm_w, col_e[1:2, :], khm_e)):
        tmp[n:n + 1, :] = v
    tmp[7:8, :] = jnp.zeros((1, LANES), f32)
    halo = jnp.transpose(tmp[...])

    def next_halo(at, halo, e, p):
        p_edge = halo[:, 1:2] - halo[:, 2:3] * e[:, 0:1]
        halo_out[at, 0:1] = halo[:, 5:6] + halo[:, 6:7] * p[:, LANES - 1:LANES]
        halo_out[at, 1:2] = p_edge + halo[:, 2:3] * (halo[:, 3:4] - halo[:, 4:5] * p_edge)
        halo_out[at, 2:3] = halo[:, 2:3]

    e_head = E0[0:rows, head]
    wet_head = W[:, head].astype(f32)
    p_edge = halo[:, 1:2] - halo[:, 2:3] * e_head[:, 0:1]
    across = Q1[8:8 + rows, head] - Q1[7:7 + rows, head]
    fixed = wet_head * (e_head - COURANT * H[:, head] * ((P1[:, head] - p_edge) + across))
    E1[0:rows, head] = jnp.where(tile_lanes == 0, fixed, E1[0:rows, head])
    e = E0[0:rows, tail]
    wet_tail = W[:, tail].astype(f32)
    p = wet_tail * (P0[:, tail] - COURANT * (halo[:, 0:1] - e))
    p = jnp.where(tile_lanes == LANES - 1, p, P1[:, tail])
    P1[:, tail] = p
    across = Q1[8:8 + rows, tail] - Q1[7:7 + rows, tail]
    fixed = wet_tail * (e - COURANT * H[:, tail] * ((p - pltpu.roll(p, 1, 1)) + across))
    E1[0:rows, tail] = jnp.where(tile_lanes == LANES - 1, fixed, E1[0:rows, tail])
    next_halo(slice(0, rows), halo, e_head, p)
    edge = halo_out[...]
    for lane in (head, tail):
        e = E1[0:rows, lane]
        wet = wet_head if lane == head else wet_tail
        q = wet * (Q1[8:8 + rows, lane] - COURANT * (E1[1:rows + 1, lane] - e))
        Q2[8:8 + rows, lane] = q
        across = q - Q2[7:7 + rows, lane]
        e_east = pltpu.roll(e, LANES - 1, 1)
        if lane == tail:
            e_east = jnp.where(tile_lanes == LANES - 1, edge[:, 0:1], e_east)
        p = wet * (P1[:, lane] - COURANT * (e_east - e))
        p_west = pltpu.roll(p, 1, 1)
        if lane == head:
            p = jnp.where(tile_lanes == LANES - 1, P2[:, lane], p)
            p_west = jnp.where(tile_lanes == 0, edge[:, 1:2] - edge[:, 2:3] * e[:, 0:1], p_west)
        eta = wet * (e - COURANT * H[:, lane] * ((p - p_west) + across))
        E2[0:rows, lane] = jnp.where(tile_lanes == (LANES - 1 if lane == head else 0),
                                     E2[0:rows, lane], eta)
        P2[:, lane] = p

    receive_rows()

    def complete(coarse):
        flow = [jnp.zeros((chunks, LANES), f32)] * 4
        corner = [jnp.zeros((1, 1), f32)] * 8
        if coarse:
            ends = slice(*ENDS)

            def above(at, own):
                to = fine[0, at, 0]
                return jnp.where(own, at, jnp.maximum(to, 0)), jnp.logical_or(own, to >= 0)

            def marked(h, at, ok):
                wet = jnp.logical_and(rdown[h, at, 32:40, :] > 0.0, ok)
                return jnp.where(wet, rdown[h, at, 24:32, :], DRY)

            def terms(h, at, x):
                to_w, to_e = fine[0, at, 2], fine[0, at, 3]
                w = kept(to_w >= 0, rdown[h, jnp.maximum(to_w, 0), ends, :])
                e = kept(to_e >= 0, rdown[h, jnp.maximum(to_e, 0), ends, :])
                p_edge = w[1:2, 5:6] + w[1:2, 6:7] * (w[1:2, 4:5] - x[0:1, 4:5])
                return p_edge, COURANT * e[0:1, 4:5]

            strips = ((half, patch, other, above(patch, half == 1), line[14], line[15]),
                      (other, south_at, half, above(south_at, half == 0),
                       rfirst[south_at, 32:40, :], rfirst[south_at, 40:48, :]))
            for n, (h, at, up, (up_at, up_ok), gain, index) in enumerate(strips):
                first_term, last_term = terms(h, at, rdown[h, at, ends, :])
                index = index.astype(jnp.int32)
                got = gather(marked(up, up_at, up_ok), index)
                eta_at = rdown[h, at, 0:8, :]
                change = jnp.where(got < 0.5 * DRY, got - COURANT * eta_at, 0.0)
                change += jnp.where(index == 0, first_term, 0.0)
                change += jnp.where(index == last, last_term, 0.0)
                flow[2 * n] = gain * eta_at
                flow[2 * n + 1] = gain * (rdown[h, at, 8:16, :] + rdown[h, at, 16:24, :] * change)

            def spread(v):
                return jnp.broadcast_to(v, (1, LANES))

            row_ids = lax.broadcasted_iota(jnp.int32, (chunks, LANES), 0)
            for n, at, r in ((0, west_at, 1), (1, east_at, 0)):
                x = rdown[half, at, ends, :]
                first_term, last_term = terms(half, at, x)
                up_at, up_ok = above(at, half == 1)
                one = slice(r, r + 1)
                index = spread(x[one, 12:13]).astype(jnp.int32)
                inside = jnp.broadcast_to(jnp.bitwise_and(index, LANES - 1), (chunks, LANES))
                which = lax.shift_right_logical(index, 7)
                got = jnp.take_along_axis(marked(other, up_at, up_ok), inside, axis=1,
                                          mode="promise_in_bounds")
                got = jnp.sum(jnp.where(row_ids == which, got, 0.0), axis=0, keepdims=True)
                wet = got < 0.5 * DRY
                value = jnp.where(wet, got, 0.0)
                value += jnp.where(index == 0, first_term, 0.0)
                value += jnp.where(index == last, last_term, 0.0)
                second = x[one, 9:10] + x[one, 10:11] * value - jnp.where(wet, x[one, 11:12], 0.0)
                ok = (west_ok, east_ok)[n]
                corner[3 * n:3 * n + 3] = [kept(ok, v) for v in (x[one, 7:8], x[one, 8:9], second[:, 0:1])]
            corner[6] = kept(sw_ok, rdown[other, sw_at, 41:42, 7:8])
            corner[7] = kept(se_ok, rdown[other, se_at, 40:41, 7:8])

        def beside(at, row):
            return jnp.where(half == 0, rlast[at, row, :], rfirst[at, row, :])

        low_end, high_end = slice(24, 25), slice(25, 26)
        n_ends = kept(north_ok, rlast[north_at, 24:25, :])
        nw_ends, ne_ends = kept(nw_ok, beside(nw_at, high_end)), kept(ne_ok, beside(ne_at, low_end))
        sw_ends, se_ends = kept(sw_ok, beside(sw_at, high_end)), kept(se_ok, beside(se_at, low_end))
        sw_eta = sw_ends[:, 4:5] + corner[6]
        se_eta = se_ends[:, 4:5] + corner[7]

        e_below = kept(south_ok, rfirst[south_at, 0:8, :] + flow[2])
        khm = kept(south_ok, rfirst[south_at, 16:24, :])
        m = (khm > 0.0).astype(f32)
        km = COURANT * m
        push = km * (e_below - east_of(e_below, se_eta))
        p_out = sw_ends[:, 5:6] + sw_ends[:, 6:7] * (sw_eta - e_below[0:1, 0:1])
        flat = rfirst[south_at, 8:16, :] + push - west_of(push, p_out) + km * e_below
        below = kept(south_ok, m * e_below - khm * kept(south_ok, flat) + flow[3])
        e_here = e_first + flow[0]
        khm_n = kept(north_ok, rlast[north_at, 16:24, :])
        km_n = COURANT * (khm_n > 0.0).astype(f32)
        q_n = kept(north_ok, rlast[north_at, 8:16, :]) - km_n * e_here
        p_out = nw_ends[:, 3:4] - nw_ends[:, 2:3] * n_ends[:, 0:1]
        side = jnp.where(cell_ids == 0, p_out, 0.0)
        side += jnp.where(cell_ids == last, COURANT * ne_ends[:, 0:1], 0.0)
        e_n = kept(north_ok, rlast[north_at, 0:8, :]) - khm_n * (q_n - side)
        for n, x in enumerate((q_n + km_n * e_n, km_n, below, khm, flow[1], e_below, q_n, e_here)):
            line[n] = x
        for c in range(chunks):
            lane = slice(c * LANES, (c + 1) * LANES)
            if coarse:
                E0[0:1, lane] = line[7, c:c + 1, :]
            E0[rows:rows + 1, lane] = line[5, c:c + 1, :]
            Q1[7:8, lane] = line[6, c:c + 1, :]

        side_lane = lax.broadcasted_iota(jnp.int32, (BLOCK, 8), 1)
        side_row = lax.broadcasted_iota(jnp.int32, (BLOCK, 8), 0)

        def put(block, terms):
            for r, n, v in terms:
                here = jnp.logical_and(side_row == r, side_lane == n)
                block += jnp.where(here, v, 0.0)
            return block

        one = slice(0, 1)
        in1 = corner[0]
        in2 = corner[1]
        km0 = km_w[:, one]
        q_nw = nw_ends[:, 1:2] - nw_ends[:, 2:3] * (col_w[6:7, one] + in1)
        tip = m_w[:, one] * in1 - khm_w[:, one] * (col_w[7:8, one] * (in1 - in2) + km0 * in1 - q_nw)
        terms_up = [(0, 1, km0 * in1), (0, 3, tip + corner[2]),
                    (1, 3, khm_w[:, 1:2] * km0 * in1)]
        in1 = corner[3]
        in2 = corner[4]
        km0 = km_e[:, one]
        q_ne = ne_ends[:, 1:2] - ne_ends[:, 2:3] * (col_e[0:1, one] + in1)
        tip = m_e[:, one] * in1 + khm_e[:, one] * (km0 * (in2 - in1) - km0 * in1 + q_ne)
        terms_up += [(0, 0, in1), (0, 5, tip + corner[5]),
                     (1, 5, khm_e[:, 1:2] * km0 * in1)]
        low = slice(rows - 1, rows)
        terms_low = [(BLOCK - 1, 3, khm_w[:, low] * km_w[:, low] * sw_eta),
                     (BLOCK - 1, 5, khm_e[:, low] * km_e[:, low] * se_eta)]
        for r, terms_at in ((0, terms_up), (end, terms_low)):
            at = slice(r, r + BLOCK)
            block = put(halo[at, :], terms_at)
            step_rows(r, E0, P0, Q0, H, W, block, E1, P1, Q1)
            next_halo(at, block, E0[at, head], P1[at, tail])
        for c in range(chunks):
            lane = slice(c * LANES, (c + 1) * LANES)
            e1 = E1[0:1, lane]
            if coarse:
                e1 += line[4, c:c + 1, :]
                E1[0:1, lane] = e1
            E1[rows:rows + 1, lane] = line[2, c:c + 1, :] + line[3, c:c + 1, :] * Q1[rows + 7:rows + 8, lane]
            Q2[7:8, lane] = line[0, c:c + 1, :] - line[1, c:c + 1, :] * e1

    @pl.when(level == 1)
    def _():
        complete(False)

    @pl.when(level == 0)
    def _():
        fine_copy().wait_recv()
        receive_down()
        complete(True)

    send_columns(lambda copy: copy.wait_send())
    send_rows(lambda copy: copy.wait_send())
    send_down(lambda copy: copy.wait_send())

    @pl.when(level == 1)
    def _():
        fine_copy().wait_send()


def two_level(mesh, adjoint_height, adjoint_momenta, depth, wet_mask, adjacency, nest_gain, nest_index):
    patches = mesh.shape["patch"]
    rows, cols = adjoint_height.shape[1:]
    chunks = cols // LANES
    f32 = jnp.float32
    anywhere = pl.BlockSpec(memory_space=pl.ANY)
    v = pltpu.VMEM
    dma = pltpu.SemaphoreType.DMA
    whole = (v((rows + 8, cols), f32), v((rows, cols), f32), v((rows + 8, cols), f32))
    scratch = [
        pltpu.SMEM(adjacency.shape, jnp.int32), pltpu.SMEM(adjacency.shape, jnp.int32),
        *whole,
        v(nest_gain.shape, f32), v(nest_index.shape, jnp.int32),
        v((16, chunks, LANES), f32), v((16, LANES), f32), v((rows + 8, LANES), f32),
        v((48, LANES), f32), v((32, LANES), f32), v((48, LANES), f32), v((8, LANES), f32),
        v((8, LANES), f32),
        dma((28,)), dma((5, patches)), dma((3, patches)), dma((2, patches)), dma((2,)),
        v((patches, 48, LANES), f32), v((patches, 32, LANES), f32), v((patches, 8, LANES), f32),
        v((2, patches, 48, LANES), f32),
    ]
    here = pl.BlockSpec(memory_space=pltpu.VMEM)
    state = pl.pallas_call(
        functools.partial(swap, patches, rows, cols),
        out_shape=(*whole, v((rows, cols), f32), v((rows, cols), jnp.int32), v((rows, 8), f32), *whole),
        in_specs=[anywhere] * 7,
        out_specs=(here,) * 9,
        scratch_shapes=scratch,
        compiler_params=pltpu.CompilerParams(collective_id=0, has_side_effects=True,
                                             vmem_limit_bytes=14 << 20),
    )(*[pltpu.with_memory_space_constraint(x, pltpu.HBM) for x in (
        adjacency, adjoint_height, adjoint_momenta, depth, wet_mask, nest_gain, nest_index)])
    state = [pltpu.with_memory_space_constraint(x, pltpu.VMEM) for x in state]
    return pl.pallas_call(
        functools.partial(settle, rows),
        out_shape=(jax.ShapeDtypeStruct(adjoint_height.shape, f32),
                   jax.ShapeDtypeStruct(adjoint_momenta.shape, f32)),
        in_specs=[here] * 9,
        out_specs=(anywhere, anywhere),
        scratch_shapes=[*whole, dma((9,))],
        compiler_params=pltpu.CompilerParams(vmem_limit_bytes=12 << 20),
    )(*state)


def solution(mesh):
    in_specs = (
        P(("parts", "level"), ("patch", "sub"), None),
        P(None, ("parts", "level"), ("patch", "sub"), None),
        P("level", ("patch", "sub"), None),
        P("level", ("patch", "sub"), None),
        P("level", None, None),
        P(None, ("patch", "sub")),
        P(None, ("patch", "sub")),
    )
    out_specs = (
        P(("parts", "level"), ("patch", "sub"), None),
        P(None, ("parts", "level"), ("patch", "sub"), None),
    )
    run = two_level if mesh.shape["level"] == 2 else body
    return jax.shard_map(functools.partial(run, mesh), mesh=mesh, in_specs=in_specs,
                         out_specs=out_specs, check_vma=False)
```
